32 devices in a mesh: row: 4 (over y, core), col: 8 (over z, x).
Axes of the slice: x: 2, y: 2, z: 4, core: 2. Of those that a mesh axis runs over, the one named last changes fastest.
Arguments:
- object_field: float32 [2, 1024, 2048], P(None, 'row', 'col'), may hold values from -4 to 4
- modes: bfloat16 [4, 12, 2, 256, 256], P('row', None, None, 'col'), may hold values from -5 to 5
- coeffs: float32 [4, 8, 4, 12], P('row', 'col'), may hold values from -1.5 to 1.5
- offsets: int32 [4, 8, 4, 2], P('row', 'col'), may hold values from -128 to 128, as said below
- region: int32 [4, 8, 4], P('row', 'col'), may hold values from 0 to 3, as said below
- counts: int32 [4, 8], P('row', 'col'), may hold values from 1 to 4, as said below
- intensity: bfloat16 [4, 8, 4, 256, 256], P('row', 'col'), may hold values from 0.049804688 to 4
Outputs:
- object_grad: float32 [2, 1024, 2048], P(None, 'row', 'col')
- mode_grad: float32 [4, 12, 2, 256, 256], P('row', None, None, 'col')
The draws below stay inside these ranges and needn't reach their ends.
Inputs may be any that keep to these rules, and one draw needn't show every extreme that they name: `offsets`: every window reaches at most 128 cells beyond its tile on each side; every tile has a live slot whose window starts at row offset -128 and column offset 256 - 256 / 2. A position's region is its tile's row index or the next one; slot 0 of every tile has its own row's region. Slots 0 to counts - 1 of a tile are live, the rest are ignored; some tile is full and some tile has one live slot.
All inputs are finite; a program needn't handle non-finite values.
Results may differ from the reference program's by a relative error of at most 0.014.
Values may be sent and summed in bfloat16 or wider, within the bound.
No kernel may reach another device: no remote copies, remote signals or barrier semaphores. Data moves between devices by JAX's collectives and lax.ppermute only.
A program may use at most 64 MiB of HBM per device.

```python
import math
import jax
import jax.numpy as jnp
from jax import lax

W = 256
K = 12
TILE = 256
P_DEV = 4
REGIONS = 4
TILE_COLS = 8
NY = 1024
NX = 2048


def common_counts(key):
    base_key = jax.random.fold_in(key, 101)
    tile_total = REGIONS * TILE_COLS
    counts = jax.random.randint(base_key, (tile_total,), 1, P_DEV + 1)
    full_tile = jax.random.randint(jax.random.fold_in(base_key, 1), (), 0, tile_total)
    tile_gap = jax.random.randint(jax.random.fold_in(base_key, 2), (), 1, tile_total)
    single_tile = (full_tile + tile_gap) % tile_total
    counts = counts.at[full_tile].set(P_DEV).at[single_tile].set(1)
    return counts.reshape(REGIONS, TILE_COLS).astype(jnp.int32)


def draw_counts(key, part):
    return common_counts(key)


def draw_offsets(key, part):
    counts = common_counts(key)
    half_size = W // 2
    corners = jax.random.randint(jax.random.fold_in(key, 202), (REGIONS, TILE_COLS, P_DEV, 2), -half_size, TILE - half_size + 1)
    picks = jax.random.randint(jax.random.fold_in(key, 203), (REGIONS, TILE_COLS), 0, 1 << 20) % counts
    chosen = jnp.arange(P_DEV, dtype=jnp.int32)[None, None, :] == picks[:, :, None]
    top_side = jnp.where(chosen, -half_size, corners[..., 0])
    left_side = jnp.where(chosen, TILE - half_size, corners[..., 1])
    return jnp.stack([top_side, left_side], axis=-1).astype(jnp.int32)


def draw_region(key, part):
    steps_up = jax.random.randint(jax.random.fold_in(key, 303), (REGIONS, TILE_COLS, P_DEV), 0, 2)
    steps_up = steps_up.at[:, :, 0].set(0)
    row_ids = jnp.arange(REGIONS, dtype=jnp.int32)[:, None, None]
    return jnp.minimum(row_ids + steps_up, REGIONS - 1).astype(jnp.int32)


def levels(rng, dims, pieces, smallest, largest):
    factor_of = 1.0
    for axis_at, parts in pieces:
        draws = jax.random.uniform(jax.random.fold_in(jax.random.fold_in(rng, 6), axis_at), (parts,), jnp.float32, smallest / len(pieces), largest / len(pieces))
        factor_of = factor_of * jnp.repeat(jnp.exp(draws), dims[axis_at] // parts).reshape((-1,) + (1,) * (len(dims) - 1 - axis_at))
    return factor_of


def bell_draw(stream_key, dims, scale, bound, cuts=(), kind=jnp.bfloat16):
    gain = levels(stream_key, dims, cuts, -0.22, 0.18) if cuts else 1.0
    result = jax.random.normal(stream_key, dims, jnp.float32) * scale * gain
    return jnp.minimum(jnp.maximum(result, -bound), bound).astype(kind)


def setup_inputs(seed: int = 0) -> dict:
    keys = jax.random.split(jax.random.key(seed), 8)
    return {
        "object_field": bell_draw(keys[0], (2, NY, NX), 0.7, 4.0, ((1, 4), (2, 8)), jnp.float32),
        "modes": bell_draw(keys[1], (REGIONS, K, 2, W, W), 1.0, 5.0, ((0, 4), (3, 8))),
        "coeffs": bell_draw(keys[2], (REGIONS, TILE_COLS, P_DEV, K), 0.3, 1.5, ((0, 4), (1, 8)), jnp.float32),
        "offsets": draw_offsets(jax.random.fold_in(keys[7], 71), 0),
        "region": draw_region(jax.random.fold_in(keys[7], 71), 0),
        "counts": draw_counts(jax.random.fold_in(keys[7], 71), 0),
        "intensity": jnp.clip(jnp.exp(math.log(4.0) - 4.3859405 * jax.random.uniform(keys[6], (REGIONS, TILE_COLS, P_DEV, W, W), jnp.float32) ** levels(keys[6], (REGIONS, TILE_COLS, P_DEV, W, W), ((0, 4), (1, 8)), -0.2, 0.2)), 0.049804688, 4.0).astype(jnp.bfloat16),
    }


FLOOR = 0.25

def dft_tables(length):
    indices = jnp.arange(length, dtype=jnp.int32)
    phases = indices[:, None] * indices[None, :] % length
    angles = phases.astype(jnp.float32) * (2.0 * math.pi / length)
    scaling = 1.0 / math.sqrt(length)
    return ((jnp.cos(angles) * scaling).astype(jnp.bfloat16), (-jnp.sin(angles) * scaling).astype(jnp.bfloat16))

def left_apply(table_re, table_im, real_part, imag_part, orient):

    def multiply(table, operand):
        return jnp.einsum('mr,prn->pmn', table.astype(jnp.float32), operand.astype(jnp.float32), precision=lax.Precision.HIGHEST)
    out_re = multiply(table_re, real_part) - orient * multiply(table_im, imag_part)
    out_im = multiply(table_re, imag_part) + orient * multiply(table_im, real_part)
    return (out_re, out_im)

def right_apply(table_re, table_im, real_part, imag_part, orient):

    def multiply(operand, table):
        return jnp.einsum('pmc,cn->pmn', operand.astype(jnp.float32), table.astype(jnp.float32), precision=lax.Precision.HIGHEST)
    out_re = multiply(real_part, table_re) - orient * multiply(imag_part, table_im)
    out_im = multiply(imag_part, table_re) + orient * multiply(real_part, table_im)
    return (out_re, out_im)

def reference(object_field, modes, coeffs, offsets, region, counts, intensity):
    half_size = W // 2
    table_re, table_im = dft_tables(W)
    padded = jnp.pad(object_field.astype(jnp.bfloat16), ((0, 0), (half_size, half_size), (half_size, half_size)))
    grad_init = jnp.zeros(padded.shape, jnp.float32)
    modes_init = jnp.zeros(modes.shape, jnp.float32)

    def tile_step(carry, tile_id):
        grad_acc, mode_acc = carry
        row_id = tile_id // TILE_COLS
        col_id = tile_id % TILE_COLS
        next_row = jnp.minimum(row_id + 1, REGIONS - 1)
        weights = coeffs[row_id, col_id]
        regions = region[row_id, col_id]
        corners = offsets[row_id, col_id]
        own_mask = (regions == row_id).astype(jnp.float32)
        next_mask = (regions == row_id + 1).astype(jnp.float32)
        mixing = jnp.concatenate([weights * own_mask[:, None], weights * next_mask[:, None]], axis=1)
        stacked = jnp.concatenate([modes[row_id], modes[next_row]], axis=0).astype(jnp.float32).reshape(2 * K, -1)
        probes = jnp.dot(mixing, stacked, precision=lax.Precision.HIGHEST).reshape(P_DEV, 2, W, W).astype(jnp.bfloat16)
        base_row = row_id * TILE
        base_col = col_id * TILE

        def cut_window(corner):
            return lax.dynamic_slice(padded, (jnp.int32(0), base_row + corner[0] + half_size, base_col + corner[1] + half_size), (2, W, W))
        windows = jax.vmap(cut_window)(corners)
        probe_re = probes[:, 0].astype(jnp.float32)
        probe_im = probes[:, 1].astype(jnp.float32)
        window_re = windows[:, 0].astype(jnp.float32)
        window_im = windows[:, 1].astype(jnp.float32)
        exit_re = (probe_re * window_re - probe_im * window_im).astype(jnp.bfloat16)
        exit_im = (probe_re * window_im + probe_im * window_re).astype(jnp.bfloat16)
        half_re, half_im = left_apply(table_re, table_im, exit_re, exit_im, 1.0)
        far_re, far_im = right_apply(table_re, table_im, half_re.astype(jnp.bfloat16), half_im.astype(jnp.bfloat16), 1.0)
        magnitude = jnp.sqrt(far_re * far_re + far_im * far_im)
        measured = jnp.sqrt(intensity[row_id, col_id].astype(jnp.float32))
        live = (jnp.arange(P_DEV, dtype=jnp.int32) < counts[row_id, col_id]).astype(jnp.float32)
        factor = (measured / jnp.maximum(magnitude, FLOOR) - 1.0) * live[:, None, None]
        change_re = (far_re * factor).astype(jnp.bfloat16)
        change_im = (far_im * factor).astype(jnp.bfloat16)
        back_re, back_im = left_apply(table_re, table_im, change_re, change_im, -1.0)
        update_re, update_im = right_apply(table_re, table_im, back_re.astype(jnp.bfloat16), back_im.astype(jnp.bfloat16), -1.0)
        object_terms = jnp.stack([probe_re * update_re + probe_im * update_im, probe_re * update_im - probe_im * update_re], axis=1)

        def place(position, accum):
            start_row = base_row + corners[position, 0] + half_size
            start_col = base_col + corners[position, 1] + half_size
            current = lax.dynamic_slice(accum, (jnp.int32(0), start_row, start_col), (2, W, W))
            return lax.dynamic_update_slice(accum, current + object_terms[position], (jnp.int32(0), start_row, start_col))
        grad_acc = lax.fori_loop(0, P_DEV, place, grad_acc)
        terms = jnp.stack([window_re * update_re + window_im * update_im, window_re * update_im - window_im * update_re], axis=1).astype(jnp.bfloat16)
        partial_sum = jnp.dot(mixing.T, terms.reshape(P_DEV, -1).astype(jnp.float32), precision=lax.Precision.HIGHEST)
        partial_sum = lax.optimization_barrier(partial_sum.astype(jnp.bfloat16)).astype(jnp.float32).reshape(2 * K, 2, W, W)
        mode_acc = mode_acc.at[row_id].add(partial_sum[:K])
        mode_acc = mode_acc.at[next_row].add(partial_sum[K:])
        return ((grad_acc, mode_acc), None)
    (grad_acc, mode_acc), _ = lax.scan(tile_step, (grad_init, modes_init), jnp.arange(REGIONS * TILE_COLS, dtype=jnp.int32))
    return (grad_acc[:, half_size:-half_size, half_size:-half_size], mode_acc)
```

```python
import functools
import math

import jax
import jax.numpy as jnp
import numpy as np
from jax import lax
from jax.experimental import pallas as pl
from jax.experimental.pallas import tpu as pltpu
from jax.sharding import PartitionSpec as P

FLOOR = 0.25
LANES = 128
SUBLANES = 8

VMEM = pl.BlockSpec(memory_space=pltpu.VMEM)
SMEM = pl.BlockSpec(memory_space=pltpu.SMEM)


def shift(value, axis, steps):
    count = lax.axis_size(axis)
    leading, last = (max(0, -steps), min(count, count - steps))
    return lax.ppermute(value, axis, [(source, source + steps) for source in range(leading, last)])


def dft_tables(length):
    indices = np.arange(length)
    phases = indices[:, None] * indices[None, :] % length
    angles = phases * (2.0 * math.pi / length)
    scaling = 1.0 / math.sqrt(length)
    re = (np.cos(angles) * scaling).astype(np.float32)
    im = (-np.sin(angles) * scaling).astype(np.float32)
    forward = np.block([[re, -im], [im, re]])
    inverse = np.block([[re, im], [-im, re]])
    return jnp.asarray(forward, jnp.bfloat16), jnp.asarray(inverse, jnp.bfloat16)


def gather_weights(payload, axis):
    count = lax.axis_size(axis)
    if count & (count - 1):
        return lax.all_gather(payload, axis, axis=0, tiled=True)
    mine = lax.broadcasted_iota(jnp.int32, (count, 1), 0) == lax.axis_index(axis)
    state = jnp.where(mine, payload, 0.0)
    step = 1
    while step < count:
        state = state + lax.ppermute(state, axis, [(i, i ^ step) for i in range(count)])
        step *= 2
    return state


def slab_kernel(slots, slot_count, weights, own, follower, out, table):
    num_modes = own.shape[1]
    devices = out.shape[0]
    table[0] = own[0].astype(jnp.float32)
    if follower is not None:
        table[1] = follower[0].astype(jnp.float32)

    def device_step(device, carry):
        for at, slot in enumerate(slots):
            if follower is None:
                which = 0
            else:
                which = jnp.where(weights[device, slot_count * num_modes + slot] > 0.5, 1, 0)
            for part in range(2):
                total = weights[device, slot * num_modes] * table[which, 0, part]
                for k in range(1, num_modes):
                    total += weights[device, slot * num_modes + k] * table[which, k, part]
                out[device, at, part] = total.astype(jnp.bfloat16)
        return carry

    lax.fori_loop(0, devices, device_step, 0)


def slabs(slots, slot_count, weights, own, follower):
    devices = weights.shape[0]
    shape = (devices, len(slots)) + own.shape[2:]
    if follower is None:

        def body(weights, own, out, table):
            slab_kernel(slots, slot_count, weights, own, None, out, table)

        operands, regions = ((weights, own), 1)
    else:
        body = functools.partial(slab_kernel, slots, slot_count)
        operands, regions = ((weights, own, follower), 2)
    return pl.pallas_call(
        body,
        out_shape=jax.ShapeDtypeStruct(shape, jnp.bfloat16),
        in_specs=[SMEM] + [VMEM] * (len(operands) - 1),
        out_specs=VMEM,
        scratch_shapes=[pltpu.VMEM((regions,) + own.shape[1:], jnp.float32)],
        name="slabs",
    )(*operands)


def corner_of(corners, slot, half, limit):
    row = jnp.clip(corners[slot, 0] + half, 0, limit)
    col = jnp.clip(corners[slot, 1] + half, 0, limit)
    rest_row, rest_col = (row & (SUBLANES - 1), col & (LANES - 1))
    base_row = pl.multiple_of(row - rest_row, SUBLANES)
    base_col = pl.multiple_of(col - rest_col, LANES)
    return base_row, rest_row, base_col, rest_col


def window_kernel(corners, tile, left, right, top, bottom, intensity, out, measured, ext):
    size = out.shape[-1]
    half = left.shape[-1]
    rows, cols = tile.shape[1:]
    for part in range(2):
        ext[part, :half, : cols + 2 * half] = top[part].astype(jnp.float32)
        ext[part, half : half + rows, :half] = left[part].astype(jnp.float32)
        ext[part, half : half + rows, half : half + cols] = tile[part].astype(jnp.float32)
        ext[part, half : half + rows, half + cols : cols + 2 * half] = right[part].astype(jnp.float32)
        ext[part, half + rows : 2 * half + rows, : cols + 2 * half] = bottom[part].astype(jnp.float32)
    tall = size + SUBLANES
    wide = size + LANES

    def slot_step(slot, carry):
        base_row, rest_row, base_col, rest_col = corner_of(
            corners, slot, half, rows + 2 * half - size
        )
        for part in range(2):
            block = ext[part, pl.ds(base_row, tall), pl.ds(base_col, wide)]
            block = pltpu.roll(block, lax.rem(tall - rest_row, tall), 0)[:size]
            block = pltpu.roll(block, lax.rem(wide - rest_col, wide), 1)[:, :size]
            out[slot, part] = block.astype(jnp.bfloat16)
        measured[slot] = jnp.sqrt(intensity[0, 0, slot].astype(jnp.float32))
        return carry

    lax.fori_loop(0, out.shape[0], slot_step, 0)


def windows_of(corners, tile, left, right, top, bottom, intensity):
    slot_count = corners.shape[0]
    size = intensity.shape[-1]
    half = left.shape[-1]
    extent = (2, tile.shape[1] + 2 * half + SUBLANES, tile.shape[2] + 2 * half + LANES)
    return pl.pallas_call(
        window_kernel,
        out_shape=(
            jax.ShapeDtypeStruct((slot_count, 2, size, size), jnp.bfloat16),
            jax.ShapeDtypeStruct((slot_count, size, size), jnp.float32),
        ),
        in_specs=[SMEM] + [VMEM] * 6,
        out_specs=(VMEM, VMEM),
        scratch_shapes=[pltpu.VMEM(extent, jnp.float32)],
        name="windows",
    )(corners, tile, left, right, top, bottom, intensity)


def dft_kernel(slots, counts, probes, windows, measured, forward, inverse, terms, placed):
    size = windows.shape[-1]
    devices = probes.shape[0]

    def joined(ref, at, part):
        return ref[:, at, part].reshape(size, size).astype(jnp.float32)

    def dot(left, right):
        return jnp.dot(left, right, preferred_element_type=jnp.float32)

    for at, slot in enumerate(slots):
        probe_re, probe_im = (joined(probes, at, 0), joined(probes, at, 1))
        window_re = windows[slot, 0].astype(jnp.float32)
        window_im = windows[slot, 1].astype(jnp.float32)
        leaving = jnp.concatenate(
            [
                (probe_re * window_re - probe_im * window_im).astype(jnp.bfloat16),
                (probe_re * window_im + probe_im * window_re).astype(jnp.bfloat16),
            ],
            axis=0,
        )
        half = dot(forward[...], leaving).astype(jnp.bfloat16)
        far = dot(jnp.concatenate([half[:size], half[size:]], axis=1), inverse[...])
        far_re, far_im = (far[:, :size], far[:, size:])
        power = jnp.maximum(far_re * far_re + far_im * far_im, FLOOR * FLOOR)
        live = jnp.where(slot < counts[0, 0], 1.0, 0.0).astype(jnp.float32)
        factor = (measured[slot] * lax.rsqrt(power) - 1.0) * live
        change = jnp.concatenate(
            [(far_re * factor).astype(jnp.bfloat16), (far_im * factor).astype(jnp.bfloat16)], axis=0
        )
        back = dot(inverse[...], change).astype(jnp.bfloat16)
        update = dot(jnp.concatenate([back[:size], back[size:]], axis=1), forward[...])
        update_re, update_im = (update[:, :size], update[:, size:])
        blocks = (devices, size // devices, size)
        terms[:, at, 0] = (
            (window_re * update_re + window_im * update_im).astype(jnp.bfloat16).reshape(blocks)
        )
        terms[:, at, 1] = (
            (window_re * update_im - window_im * update_re).astype(jnp.bfloat16).reshape(blocks)
        )
        placed[at, 0] = probe_re * update_re + probe_im * update_im
        placed[at, 1] = probe_re * update_im - probe_im * update_re


def dft_step(slots, counts, probes, windows, measured, tables):
    size = windows.shape[-1]
    return pl.pallas_call(
        functools.partial(dft_kernel, slots),
        out_shape=(
            jax.ShapeDtypeStruct(probes.shape, jnp.bfloat16),
            jax.ShapeDtypeStruct((len(slots), 2, size, size), jnp.float32),
        ),
        in_specs=[SMEM] + [VMEM] * 5,
        out_specs=(VMEM, VMEM),
        name="dft_chain",
    )(counts, probes, windows, measured, *tables)


def place_kernel(groups, half, corners, *refs):
    pieces = refs[: len(groups)]
    top, middle, bottom, accum = refs[len(groups) :]
    size = pieces[0].shape[-1]
    rows = middle.shape[1]
    width = middle.shape[2]
    accum[...] = jnp.zeros_like(accum)
    for slots, piece in zip(groups, pieces):
        for at, slot in enumerate(slots):
            base_row, rest_row, base_col, rest_col = corner_of(
                corners, slot, half, rows + 2 * half - size
            )
            for part in range(2):
                block = jnp.concatenate(
                    [piece[at, part], jnp.zeros((size, LANES), jnp.float32)], axis=1
                )
                block = pltpu.roll(block, rest_col, 1)
                block = jnp.concatenate(
                    [block, jnp.zeros((SUBLANES, size + LANES), jnp.float32)], axis=0
                )
                block = pltpu.roll(block, rest_row, 0)
                where = (part, pl.ds(base_row, size + SUBLANES), pl.ds(base_col, size + LANES))
                accum[where] += block
    top[...] = accum[:, :half, :width].astype(jnp.bfloat16)
    middle[...] = accum[:, half : half + rows, :width]
    bottom[...] = accum[:, half + rows : 2 * half + rows, :width].astype(jnp.bfloat16)


def place(groups, corners, pieces, rows, cols):
    half = pieces[0].shape[-1] // 2
    width = cols + 2 * half
    return pl.pallas_call(
        functools.partial(place_kernel, groups, half),
        out_shape=(
            jax.ShapeDtypeStruct((2, half, width), jnp.bfloat16),
            jax.ShapeDtypeStruct((2, rows, width), jnp.float32),
            jax.ShapeDtypeStruct((2, half, width), jnp.bfloat16),
        ),
        in_specs=[SMEM] + [VMEM] * len(pieces),
        out_specs=(VMEM, VMEM, VMEM),
        scratch_shapes=[
            pltpu.VMEM((2, rows + 2 * half + SUBLANES, width + LANES), jnp.float32)
        ],
        name="place",
    )(corners, *pieces)


def sums_kernel(slots, slot_count, weights, received, own, following, terms):
    num_modes = own.shape[0]
    devices = received.shape[0]
    flags = slot_count * num_modes
    for at in range(len(slots)):
        terms[:, at] = received[:, at].astype(jnp.float32)

    def mode_step(k, carry):
        for part in range(2):
            totals = [jnp.zeros(own.shape[2:], jnp.float32) for _ in range(2)]
            for device in range(devices):
                for at, slot in enumerate(slots):
                    weight = weights[device, slot * num_modes + k]
                    is_next = weights[device, flags + slot]
                    term = terms[device, at, part]
                    totals[0] += (weight * (1.0 - is_next)) * term
                    totals[1] += (weight * is_next) * term
            own[k, part] = totals[0]
            following[k, part] = totals[1].astype(jnp.bfloat16)
        return carry

    lax.fori_loop(0, num_modes, mode_step, 0)


def sums(slots, slot_count, num_modes, weights, received):
    shape = (num_modes,) + received.shape[2:]
    return pl.pallas_call(
        functools.partial(sums_kernel, slots, slot_count),
        out_shape=(
            jax.ShapeDtypeStruct(shape, jnp.float32),
            jax.ShapeDtypeStruct(shape, jnp.bfloat16),
        ),
        in_specs=[SMEM, VMEM],
        out_specs=(VMEM, VMEM),
        scratch_shapes=[pltpu.VMEM(received.shape, jnp.float32)],
        name="mode_sums",
    )(weights, received)


def last_kernel(slots, weights, received, own, passed, out):
    num_modes = own.shape[0]
    devices = received.shape[0]

    def mode_step(k, carry):
        for part in range(2):
            total = own[k, part] + passed[k, part].astype(jnp.float32)
            for device in range(devices):
                for at, slot in enumerate(slots):
                    weight = weights[device, slot * num_modes + k]
                    total += weight * received[device, at, part].astype(jnp.float32)
            out[0, k, part] = total
        return carry

    lax.fori_loop(0, num_modes, mode_step, 0)


def last_sums(slots, weights, received, own, passed):
    return pl.pallas_call(
        functools.partial(last_kernel, slots),
        out_shape=jax.ShapeDtypeStruct((1,) + own.shape, jnp.float32),
        in_specs=[SMEM] + [VMEM] * 3,
        out_specs=VMEM,
        name="last_sums",
    )(weights, received, own, passed)


def local(object_field, modes, coeffs, offsets, region, counts, intensity):
    size = modes.shape[-1]
    half = size // 2
    num_modes = modes.shape[1]
    slot_count = coeffs.shape[2]
    rows, cols = object_field.shape[1:]
    row_index = lax.axis_index("row")

    follower = shift(modes, "row", -1)
    is_own = region[0, 0] == row_index
    is_next = region[0, 0] == row_index + 1
    scaled = coeffs[0, 0] * (is_own | is_next).astype(jnp.float32)[:, None]
    payload = jnp.concatenate([scaled.reshape(-1), is_next.astype(jnp.float32)])
    padding = -payload.shape[0] % LANES
    payload = jnp.pad(payload, (0, padding))[None]
    weights = gather_weights(payload, "col")

    low = object_field.astype(jnp.bfloat16)
    left = shift(low[:, :, cols - half :], "col", 1)
    right = shift(low[:, :, :half], "col", -1)
    wide_top = jnp.concatenate([left[:, :half], low[:, :half], right[:, :half]], axis=2)
    wide_bottom = jnp.concatenate(
        [left[:, rows - half :], low[:, rows - half :], right[:, rows - half :]], axis=2
    )
    top = shift(wide_bottom, "row", 1)
    bottom = shift(wide_top, "row", -1)

    def exchange(value):
        return lax.all_to_all(value, "col", split_axis=0, concat_axis=0, tiled=True)

    first = tuple(range(1, slot_count))
    second = (0,)
    corners = offsets[0, 0]
    tables = dft_tables(size)
    probes_first = exchange(slabs(first, slot_count, weights, modes, follower))
    probes_second = exchange(slabs(second, slot_count, weights, modes, None))
    windows, measured = windows_of(corners, low, left, right, top, bottom, intensity)
    terms_first, placed_first = dft_step(first, counts, probes_first, windows, measured, tables)
    terms_first = exchange(terms_first)
    terms_second, placed_second = dft_step(second, counts, probes_second, windows, measured, tables)
    terms_second = exchange(terms_second)

    over_top, middle, over_bottom = place(
        (first, second), corners, (placed_first, placed_second), rows, cols
    )
    got_top = shift(over_bottom, "row", 1)
    got_bottom = shift(over_top, "row", -1)
    middle = middle.at[:, :half].add(got_top.astype(jnp.float32))
    middle = middle.at[:, rows - half :].add(got_bottom.astype(jnp.float32))
    got_left = shift(middle[:, :, half + cols :].astype(jnp.bfloat16), "col", 1)
    got_right = shift(middle[:, :, :half].astype(jnp.bfloat16), "col", -1)
    object_grad = middle[:, :, half : half + cols]
    object_grad = object_grad.at[:, :, :half].add(got_left.astype(jnp.float32))
    object_grad = object_grad.at[:, :, cols - half :].add(got_right.astype(jnp.float32))

    own, following = sums(first, slot_count, num_modes, weights, terms_first)
    passed = shift(following, "row", 1)
    mode_grad = last_sums(second, weights, terms_second, own, passed)
    return (object_grad, mode_grad)


def solution(mesh):
    in_specs = (
        P(None, "row", "col"),
        P("row", None, None, "col", None),
        P("row", "col", None, None),
        P("row", "col", None, None),
        P("row", "col", None),
        P("row", "col"),
        P("row", "col", None, None, None),
    )
    out_specs = (P(None, "row", "col"), P("row", None, None, "col", None))
    return jax.shard_map(local, mesh=mesh, in_specs=in_specs, out_specs=out_specs, check_vma=False)
```

```python
import functools
import math

import jax
import jax.numpy as jnp
import numpy as np
from jax import lax
from jax.experimental import pallas as pl
from jax.experimental.pallas import tpu as pltpu
from jax.sharding import PartitionSpec as P

FLOOR = 0.25
LANES = 128
SUBLANES = 8

VMEM = pl.BlockSpec(memory_space=pltpu.VMEM)
SMEM = pl.BlockSpec(memory_space=pltpu.SMEM)


def shift(value, axis, steps):
    count = lax.axis_size(axis)
    leading, last = (max(0, -steps), min(count, count - steps))
    return lax.ppermute(value, axis, [(source, source + steps) for source in range(leading, last)])


def dft_tables(length):
    indices = np.arange(length)
    phases = indices[:, None] * indices[None, :] % length
    angles = phases * (2.0 * math.pi / length)
    scaling = 1.0 / math.sqrt(length)
    re = (np.cos(angles) * scaling).astype(np.float32)
    im = (-np.sin(angles) * scaling).astype(np.float32)
    forward = np.block([[re, -im], [im, re]])
    inverse = np.block([[re, im], [-im, re]])
    return jnp.asarray(forward, jnp.bfloat16), jnp.asarray(inverse, jnp.bfloat16)


def partners(axis):
    count = lax.axis_size(axis)
    steps = list(range(count // 2, count)) + list(range(1, count // 2))
    paired = count & (count - 1) == 0

    def goes_to(index, step):
        return index ^ step if paired else (index + step) % count

    def comes_from(index, step):
        return index ^ step if paired else (index - step + count) % count

    return steps, goes_to, comes_from


def call(body, name, outs, *operands, scratch=(), limit=20):
    arrays = [o[0] if isinstance(o, tuple) else o for o in operands]
    specs = [o[1] if isinstance(o, tuple) else VMEM for o in operands]
    outs = [jax.ShapeDtypeStruct(shape, dtype) for shape, dtype in outs]
    return pl.pallas_call(
        body,
        out_shape=tuple(outs),
        in_specs=specs,
        out_specs=tuple(VMEM for _ in outs),
        scratch_shapes=list(scratch),
        compiler_params=pltpu.CompilerParams(vmem_limit_bytes=limit * 1024 * 1024),
        name=name,
    )(*arrays)


def slab_kernel(count, row, *refs):
    weights = refs[:count]
    own, follower = refs[count : count + 2]
    outs = refs[count + 2 : -1]
    table = refs[-1]
    num_modes = own.shape[1]
    table[0] = own[0].astype(jnp.float32)
    table[1] = follower[0].astype(jnp.float32)
    next_row = (row[0] + 1).astype(jnp.float32)
    for weight, out in zip(weights, outs):

        def slot_step(slot, carry, weight=weight, out=out):
            which = jnp.where(weight[slot, num_modes] == next_row, 1, 0)
            known = jnp.where(jnp.abs(weight[slot, num_modes] - next_row + 0.5) < 1.0, 1.0, 0.0)
            scales = [weight[slot, k] * known for k in range(num_modes)]
            for part in range(2):
                total = scales[0] * table[which, 0, part]
                for k in range(1, num_modes):
                    total += scales[k] * table[which, k, part]
                out[slot, part] = total.astype(jnp.bfloat16)
            return carry

        lax.fori_loop(0, out.shape[0], slot_step, 0)


def slabs(row, weights, own, follower):
    shape = (weights[0].shape[0],) + own.shape[2:]
    return call(
        functools.partial(slab_kernel, len(weights)),
        "slabs",
        [(shape, jnp.bfloat16)] * len(weights),
        (row, SMEM),
        *[(w, SMEM) for w in weights],
        own,
        follower,
        scratch=[pltpu.VMEM((2,) + own.shape[1:], jnp.float32)],
    )


def widen_kernel(tile, left, right, top, bottom):
    half = left.shape[-1]
    rows, cols = tile.shape[1:]
    for out, start in ((top, 0), (bottom, rows - half)):
        out[:, :, :half] = left[:, start : start + half]
        out[:, :, half : half + cols] = tile[:, start : start + half].astype(jnp.bfloat16)
        out[:, :, half + cols :] = right[:, start : start + half]


def corner_of(corners, slot, half, limit):
    row = jnp.clip(corners[slot, 0] + half, 0, limit)
    col = jnp.clip(corners[slot, 1] + half, 0, limit)
    rest_row, rest_col = (row & (SUBLANES - 1), col & (LANES - 1))
    base_row = pl.multiple_of(row - rest_row, SUBLANES)
    base_col = pl.multiple_of(col - rest_col, LANES)
    return base_row, rest_row, base_col, rest_col


def window_kernel(corners, tile, left, right, top, bottom, intensity, out, measured, ext):
    size = out.shape[-1]
    half = left.shape[-1]
    rows, cols = tile.shape[1:]
    for part in range(2):
        ext[part, :half, : cols + 2 * half] = top[part].astype(jnp.float32)
        ext[part, half : half + rows, :half] = left[part].astype(jnp.float32)
        low = tile[part].astype(jnp.bfloat16)
        ext[part, half : half + rows, half : half + cols] = low.astype(jnp.float32)
        ext[part, half : half + rows, half + cols : cols + 2 * half] = right[part].astype(jnp.float32)
        ext[part, half + rows : 2 * half + rows, : cols + 2 * half] = bottom[part].astype(jnp.float32)
    tall = size + SUBLANES
    wide = size + LANES

    def slot_step(slot, carry):
        base_row, rest_row, base_col, rest_col = corner_of(
            corners, slot, half, rows + 2 * half - size
        )
        for part in range(2):
            block = ext[part, pl.ds(base_row, tall), pl.ds(base_col, wide)]
            block = pltpu.roll(block, lax.rem(tall - rest_row, tall), 0)[:size]
            block = pltpu.roll(block, lax.rem(wide - rest_col, wide), 1)[:, :size]
            out[slot, part] = block.astype(jnp.bfloat16)
        measured[slot] = jnp.sqrt(intensity[0, 0, slot].astype(jnp.float32))
        return carry

    lax.fori_loop(0, out.shape[0], slot_step, 0)


def windows_of(corners, tile, left, right, top, bottom, intensity):
    slot_count = corners.shape[0]
    size = intensity.shape[-1]
    half = left.shape[-1]
    extent = (2, tile.shape[1] + 2 * half + SUBLANES, tile.shape[2] + 2 * half + LANES)
    return call(
        window_kernel,
        "windows",
        [((slot_count, 2, size, size), jnp.bfloat16), ((slot_count, size, size), jnp.float32)],
        (corners, SMEM),
        tile,
        left,
        right,
        top,
        bottom,
        intensity,
        scratch=[pltpu.VMEM(extent, jnp.float32)],
    )


def dft_kernel(goes_to, comes_from, steps, counts, me, *refs):
    blocks = refs[: len(steps)]
    windows, measured, forward, inverse = refs[len(steps) : len(steps) + 4]
    outs = refs[len(steps) + 4 : 2 * len(steps) + 4]
    placed, probes, terms = refs[2 * len(steps) + 4 :]
    size = windows.shape[-1]
    rows = blocks[0].shape[2]
    starts = [pl.multiple_of(comes_from(me[0], step) * rows, rows) for step in steps]
    targets = [pl.multiple_of(goes_to(me[0], step) * rows, rows) for step in steps]

    def dot(left, right):
        return jnp.dot(left, right, preferred_element_type=jnp.float32)

    for block, start in zip(blocks, starts):
        probes[:, :, pl.ds(start, rows)] = block[...]
    for slot in range(windows.shape[0]):
        probe_re = probes[slot, 0].astype(jnp.float32)
        probe_im = probes[slot, 1].astype(jnp.float32)
        window_re = windows[slot, 0].astype(jnp.float32)
        window_im = windows[slot, 1].astype(jnp.float32)
        leaving = jnp.concatenate(
            [
                (probe_re * window_re - probe_im * window_im).astype(jnp.bfloat16),
                (probe_re * window_im + probe_im * window_re).astype(jnp.bfloat16),
            ],
            axis=0,
        )
        half = dot(forward[...], leaving).astype(jnp.bfloat16)
        far = dot(jnp.concatenate([half[:size], half[size:]], axis=1), inverse[...])
        far_re, far_im = (far[:, :size], far[:, size:])
        power = jnp.maximum(far_re * far_re + far_im * far_im, FLOOR * FLOOR)
        live = jnp.where(slot < counts[0, 0], 1.0, 0.0).astype(jnp.float32)
        factor = (measured[slot] * lax.rsqrt(power) - 1.0) * live
        change = jnp.concatenate(
            [(far_re * factor).astype(jnp.bfloat16), (far_im * factor).astype(jnp.bfloat16)], axis=0
        )
        back = dot(inverse[...], change).astype(jnp.bfloat16)
        update = dot(jnp.concatenate([back[:size], back[size:]], axis=1), forward[...])
        update_re, update_im = (update[:, :size], update[:, size:])
        terms[slot, 0] = (window_re * update_re + window_im * update_im).astype(jnp.bfloat16)
        terms[slot, 1] = (window_re * update_im - window_im * update_re).astype(jnp.bfloat16)
        placed[slot, 0] = probe_re * update_re + probe_im * update_im
        placed[slot, 1] = probe_re * update_im - probe_im * update_re
    for out, start in zip(outs, targets):
        out[...] = terms[:, :, pl.ds(start, rows)]


def place_kernel(half, corners, pieces, top, middle, bottom, accum):
    size = pieces.shape[-1]
    rows = middle.shape[1]
    width = middle.shape[2]
    accum[...] = jnp.zeros_like(accum)
    for slot in range(pieces.shape[0]):
        base_row, rest_row, base_col, rest_col = corner_of(
            corners, slot, half, rows + 2 * half - size
        )
        for part in range(2):
            block = jnp.concatenate(
                [pieces[slot, part], jnp.zeros((size, LANES), jnp.float32)], axis=1
            )
            block = pltpu.roll(block, rest_col, 1)
            block = jnp.concatenate(
                [block, jnp.zeros((SUBLANES, size + LANES), jnp.float32)], axis=0
            )
            block = pltpu.roll(block, rest_row, 0)
            where = (part, pl.ds(base_row, size + SUBLANES), pl.ds(base_col, size + LANES))
            accum[where] += block
    top[...] = accum[:, :half, :width].astype(jnp.bfloat16)
    middle[...] = accum[:, half : half + rows, :width]
    bottom[...] = accum[:, half + rows : 2 * half + rows, :width].astype(jnp.bfloat16)


def rows_kernel(middle, got_top, got_bottom, left, center, right, total):
    half = got_top.shape[1]
    rows = middle.shape[1]
    cols = center.shape[2]
    total[...] = middle[...]
    total[:, :half] += got_top[...].astype(jnp.float32)
    total[:, rows - half :] += got_bottom[...].astype(jnp.float32)
    left[...] = total[:, :, :half].astype(jnp.bfloat16)
    center[...] = total[:, :, half : half + cols]
    right[...] = total[:, :, half + cols :].astype(jnp.bfloat16)


def cols_kernel(center, got_left, got_right, out):
    half = got_left.shape[2]
    cols = out.shape[2]
    out[...] = center[...]
    out[:, :, :half] += got_left[...].astype(jnp.float32)
    out[:, :, cols - half :] += got_right[...].astype(jnp.float32)


def sums_kernel(count, goals, row, *refs):
    weights = refs[:count]
    received = refs[count : 2 * count]
    added = refs[2 * count : 2 * count + sum(goal[2] for goal in goals)]
    outs = refs[2 * count + len(added) : -1]
    terms = refs[-1]
    num_modes = outs[0].shape[-4]
    slot_count = received[0].shape[0]
    first = min(goal[1] for goal in goals)
    for at in range(count):
        terms[at, first:] = received[at][first:].astype(jnp.float32)

    def mode_step(k, carry):
        rest = list(added)
        for (step, first, adds), out in zip(goals, outs):
            region = (row[0] + step).astype(jnp.float32)
            addend = rest.pop(0) if adds else None
            scales = [
                jnp.where(weight[slot, num_modes] == region, weight[slot, k], 0.0)
                for weight in weights
                for slot in range(first, slot_count)
            ]
            for part in range(2):
                pieces = [
                    terms[at, slot, part] for at in range(count) for slot in range(first, slot_count)
                ]
                total = scales[0] * pieces[0]
                for scale, piece in zip(scales[1:], pieces[1:]):
                    total += scale * piece
                if adds:
                    total += addend[k, part].astype(jnp.float32)
                out[k, part] = total.astype(out.dtype)
        return carry

    lax.fori_loop(0, num_modes, mode_step, 0)


def sums(row, goals, weights, received, added, num_modes, dtypes):
    shape = (num_modes,) + received[0].shape[1:]
    return call(
        functools.partial(sums_kernel, len(received), goals),
        "mode_sums",
        [(shape, dtype) for dtype in dtypes],
        (row, SMEM),
        *[(w, SMEM) for w in weights],
        *received,
        *added,
        scratch=[pltpu.VMEM((len(received),) + received[0].shape, jnp.float32)],
    )


def local(object_field, modes, coeffs, offsets, region, counts, intensity):
    size = modes.shape[-1]
    half = size // 2
    num_modes = modes.shape[1]
    slot_count = coeffs.shape[2]
    rows, cols = object_field.shape[1:]
    block = (slot_count,) + modes.shape[2:]
    row = lax.axis_index("row").reshape(1)
    me = lax.axis_index("col").reshape(1)
    steps, goes_to, comes_from = partners("col")
    count = lax.axis_size("col")
    crossing = steps[: count - count // 2]
    staying = steps[count - count // 2 :]

    def move(value, step):
        return lax.ppermute(value, "col", [(i, goes_to(i, step)) for i in range(count)])

    follower = shift(modes, "row", -1)
    lanes = lax.broadcasted_iota(jnp.int32, (slot_count, LANES), 1)
    payload = jnp.where(
        lanes < num_modes,
        jnp.pad(coeffs[0, 0], ((0, 0), (0, LANES - num_modes))),
        region[0, 0].astype(jnp.float32)[:, None],
    )
    weights = {0: payload}
    for step in steps:
        weights[step] = move(payload, step)

    def made_for(step):
        return weights[step] if goes_to(1, step) == comes_from(1, step) else weights[count - step]

    low = object_field.astype(jnp.bfloat16)
    left = shift(low[:, :, cols - half :], "col", 1)
    right = shift(low[:, :, :half], "col", -1)
    wide = (2, half, cols + 2 * half)
    wide_top, wide_bottom = call(
        widen_kernel, "widen", [(wide, jnp.bfloat16)] * 2, object_field, left, right
    )
    top = shift(wide_bottom, "row", 1)
    bottom = shift(wide_top, "row", -1)

    blocks = {}
    for group in (crossing, [0] + staying):
        made = slabs(row, [made_for(step) for step in group], modes, follower)
        for step, slab in zip(group, made):
            blocks[step] = move(slab, step) if step else slab

    corners = offsets[0, 0]
    windows, measured = windows_of(corners, object_field, left, right, top, bottom, intensity)
    every = [0] + steps
    whole = (slot_count, 2, size, size)
    *terms, placed = call(
        functools.partial(dft_kernel, goes_to, comes_from, every),
        "dft_chain",
        [(block, jnp.bfloat16)] * count + [(whole, jnp.float32)],
        (counts, SMEM),
        (me, SMEM),
        *[blocks[step] for step in every],
        windows,
        measured,
        *dft_tables(size),
        scratch=[pltpu.VMEM(whole, jnp.bfloat16)] * 2,
        limit=32,
    )
    terms = dict(zip(every, terms))
    received = {step: move(terms[step], step) if step else terms[step] for step in every}

    extent = (2, rows + 2 * half + SUBLANES, cols + 2 * half + LANES)
    over_top, middle, over_bottom = call(
        functools.partial(place_kernel, half),
        "place",
        [(wide, jnp.bfloat16), ((2, rows, cols + 2 * half), jnp.float32), (wide, jnp.bfloat16)],
        (corners, SMEM),
        placed,
        scratch=[pltpu.VMEM(extent, jnp.float32)],
    )
    got_top = shift(over_bottom, "row", 1)
    got_bottom = shift(over_top, "row", -1)
    side = ((2, rows, half), jnp.bfloat16)
    over_left, center, over_right = call(
        rows_kernel,
        "rows",
        [side, ((2, rows, cols), jnp.float32), side],
        middle,
        got_top,
        got_bottom,
        scratch=[pltpu.VMEM((2, rows, cols + 2 * half), jnp.float32)],
    )
    got_left = shift(over_right, "col", 1)
    got_right = shift(over_left, "col", -1)
    (object_grad,) = call(
        cols_kernel, "cols", [(object_field.shape, jnp.float32)], center, got_left, got_right
    )

    def add_up(group, goals, added, dtypes):
        return sums(
            row,
            goals,
            [came_from(step) for step in group],
            [received[step] for step in group],
            added,
            num_modes,
            dtypes,
        )

    def came_from(step):
        return weights[step]

    own, following = add_up(
        [0] + staying, ((0, 0, False), (1, 1, False)), [], [jnp.float32, jnp.float32]
    )
    (following,) = add_up(crossing, ((1, 1, True),), [following], [jnp.bfloat16])
    passed = shift(following, "row", 1)
    (own,) = add_up(crossing, ((0, 0, True),), [own], [jnp.float32])
    mode_grad = (own + passed.astype(jnp.float32))[None]
    return (object_grad, mode_grad)


def solution(mesh):
    in_specs = (
        P(None, "row", "col"),
        P("row", None, None, "col", None),
        P("row", "col", None, None),
        P("row", "col", None, None),
        P("row", "col", None),
        P("row", "col"),
        P("row", "col", None, None, None),
    )
    out_specs = (P(None, "row", "col"), P("row", None, None, "col", None))
    return jax.shard_map(local, mesh=mesh, in_specs=in_specs, out_specs=out_specs, check_vma=False)
```

```python
import functools
import math

import jax
import jax.numpy as jnp
import numpy as np
from jax import lax
from jax.experimental import pallas as pl
from jax.experimental.pallas import tpu as pltpu
from jax.sharding import PartitionSpec as P


FLOOR = 0.25
LANES = 128
SUBLANES = 8

VMEM = pl.BlockSpec(memory_space=pltpu.VMEM)
SMEM = pl.BlockSpec(memory_space=pltpu.SMEM)


def shift(value, axis, steps):
    count = lax.axis_size(axis)
    leading, last = (max(0, -steps), min(count, count - steps))
    pairs = [(source, source + steps) for source in range(leading, last)]
    return lax.ppermute(value, axis, pairs)


def dft_tables(length):
    indices = np.arange(length)
    phases = indices[:, None] * indices[None, :] % length
    angles = phases * (2.0 * math.pi / length)
    scaling = 1.0 / math.sqrt(length)
    re = (np.cos(angles) * scaling).astype(np.float32)
    im = (-np.sin(angles) * scaling).astype(np.float32)
    forward = np.block([[re, -im], [im, re]])
    inverse = np.block([[re, im], [-im, re]])
    return jnp.asarray(forward, jnp.bfloat16), jnp.asarray(inverse, jnp.bfloat16)


def partners(axis):
    count = lax.axis_size(axis)
    steps = list(range(count // 2, count)) + list(range(1, count // 2))
    paired = count & (count - 1) == 0

    def goes_to(index, step):
        return index ^ step if paired else (index + step) % count

    def comes_from(index, step):
        return index ^ step if paired else (index - step + count) % count

    return steps, goes_to, comes_from


def call(body, outs, *operands, scratch=(), limit=20):
    arrays = [o[0] if isinstance(o, tuple) else o for o in operands]
    specs = [o[1] if isinstance(o, tuple) else VMEM for o in operands]
    outs = [jax.ShapeDtypeStruct(shape, dtype) for shape, dtype in outs]
    return pl.pallas_call(
        body,
        out_shape=tuple(outs),
        in_specs=specs,
        out_specs=tuple(VMEM for _ in outs),
        scratch_shapes=list(scratch),
        compiler_params=pltpu.CompilerParams(vmem_limit_bytes=limit * 1024 * 1024),
    )(*arrays)


def fetch(arrays, held, sem):
    copies = [pltpu.make_async_copy(a, held.at[at], sem.at[at]) for at, a in enumerate(arrays)]
    for copy in copies:
        copy.start()
    return copies


def held_weights(count, weights):
    return [pltpu.SMEM((count,) + weights.shape, jnp.float32), pltpu.SemaphoreType.DMA((count,))]


def slab_kernel(count, row, *refs):
    own, follower = refs[count : count + 2]
    outs = refs[count + 2 : -3]
    table, held, sem = refs[-3:]
    copies = fetch(refs[:count], held, sem)
    num_modes = own.shape[1]
    table[0] = own[0].astype(jnp.float32)
    table[1] = follower[0].astype(jnp.float32)
    next_row = (row[0] + 1).astype(jnp.float32)
    for copy in copies:
        copy.wait()
    for at, out in enumerate(outs):

        def slot_step(slot, carry, at=at, out=out):
            region = held[at, slot, num_modes]
            which = jnp.where(region == next_row, 1, 0)
            known = jnp.where(jnp.abs(region - next_row + 0.5) < 1.0, 1.0, 0.0)
            scales = [held[at, slot, k] * known for k in range(num_modes)]
            for part in range(2):
                total = scales[0] * table[which, 0, part]
                for k in range(1, num_modes):
                    total += scales[k] * table[which, k, part]
                out[slot, part] = total.astype(jnp.bfloat16)
            return carry

        lax.fori_loop(0, out.shape[0], slot_step, 0)


def slabs(row, weights, own, follower):
    shape = (weights[0].shape[0],) + own.shape[2:]
    return call(
        functools.partial(slab_kernel, len(weights)),
        [(shape, jnp.bfloat16)] * len(weights),
        (row, SMEM),
        *weights,
        own,
        follower,
        scratch=[pltpu.VMEM((2,) + own.shape[1:], jnp.float32)]
        + held_weights(len(weights), weights[0]),
    )


def widen_kernel(tile, left, right, top, bottom):
    half = left.shape[-1]
    rows, cols = tile.shape[1:]
    for out, start in ((top, 0), (bottom, rows - half)):
        out[:, :, :half] = left[:, start : start + half]
        out[:, :, half : half + cols] = tile[:, start : start + half].astype(jnp.bfloat16)
        out[:, :, half + cols :] = right[:, start : start + half]


def corner_of(corners, slot, half, limit):
    row = jnp.clip(corners[slot, 0] + half, 0, limit)
    col = jnp.clip(corners[slot, 1] + half, 0, limit)
    rest_row, rest_col = (row & (SUBLANES - 1), col & (LANES - 1))
    base_row = pl.multiple_of(row - rest_row, SUBLANES)
    base_col = pl.multiple_of(col - rest_col, LANES)
    return base_row, rest_row, base_col, rest_col


def window_kernel(corners, tile, left, right, top, bottom, intensity, out, measured, ext):
    size = out.shape[-1]
    half = left.shape[-1]
    rows, cols = tile.shape[1:]
    for part in range(2):
        ext[part, :half, : cols + 2 * half] = top[part].astype(jnp.float32)
        ext[part, half : half + rows, :half] = left[part].astype(jnp.float32)
        low = tile[part].astype(jnp.bfloat16)
        ext[part, half : half + rows, half : half + cols] = low.astype(jnp.float32)
        ext[part, half : half + rows, half + cols : cols + 2 * half] = right[part].astype(jnp.float32)
        ext[part, half + rows : 2 * half + rows, : cols + 2 * half] = bottom[part].astype(jnp.float32)
    tall = size + SUBLANES
    wide = size + LANES

    def slot_step(slot, carry):
        base_row, rest_row, base_col, rest_col = corner_of(
            corners, slot, half, rows + 2 * half - size
        )
        for part in range(2):
            block = ext[part, pl.ds(base_row, tall), pl.ds(base_col, wide)]
            block = pltpu.roll(block, lax.rem(tall - rest_row, tall), 0)[:size]
            block = pltpu.roll(block, lax.rem(wide - rest_col, wide), 1)[:, :size]
            out[slot, part] = block.astype(jnp.bfloat16)
        measured[slot] = jnp.sqrt(intensity[0, 0, slot].astype(jnp.float32))
        return carry

    lax.fori_loop(0, out.shape[0], slot_step, 0)


def windows_of(corners, tile, left, right, top, bottom, intensity):
    slot_count = corners.shape[0]
    size = intensity.shape[-1]
    half = left.shape[-1]
    extent = (2, tile.shape[1] + 2 * half + SUBLANES, tile.shape[2] + 2 * half + LANES)
    return call(
        window_kernel,
        [((slot_count, 2, size, size), jnp.bfloat16), ((slot_count, size, size), jnp.float32)],
        (corners, SMEM),
        tile,
        left,
        right,
        top,
        bottom,
        intensity,
        scratch=[pltpu.VMEM(extent, jnp.float32)],
    )


def dft_kernel(goes_to, comes_from, steps, counts, me, *refs):
    blocks = refs[: len(steps)]
    windows, measured, forward, inverse = refs[len(steps) : len(steps) + 4]
    outs = refs[len(steps) + 4 : 2 * len(steps) + 4]
    placed, probes, terms = refs[2 * len(steps) + 4 :]
    size = windows.shape[-1]
    rows = blocks[0].shape[2]
    starts = [pl.multiple_of(comes_from(me[0], step) * rows, rows) for step in steps]
    targets = [pl.multiple_of(goes_to(me[0], step) * rows, rows) for step in steps]

    def dot(left, right):
        return jnp.dot(left, right, preferred_element_type=jnp.float32)

    for block, start in zip(blocks, starts):
        probes[:, :, pl.ds(start, rows)] = block[...]
    for slot in range(windows.shape[0]):
        probe_re = probes[slot, 0].astype(jnp.float32)
        probe_im = probes[slot, 1].astype(jnp.float32)
        window_re = windows[slot, 0].astype(jnp.float32)
        window_im = windows[slot, 1].astype(jnp.float32)
        leaving = jnp.concatenate(
            [
                (probe_re * window_re - probe_im * window_im).astype(jnp.bfloat16),
                (probe_re * window_im + probe_im * window_re).astype(jnp.bfloat16),
            ],
            axis=0,
        )
        half = dot(forward[...], leaving).astype(jnp.bfloat16)
        far = dot(jnp.concatenate([half[:size], half[size:]], axis=1), inverse[...])
        far_re, far_im = (far[:, :size], far[:, size:])
        power = jnp.maximum(far_re * far_re + far_im * far_im, FLOOR * FLOOR)
        live = jnp.where(slot < counts[0, 0], 1.0, 0.0).astype(jnp.float32)
        factor = (measured[slot] * lax.rsqrt(power) - 1.0) * live
        change = jnp.concatenate(
            [(far_re * factor).astype(jnp.bfloat16), (far_im * factor).astype(jnp.bfloat16)], axis=0
        )
        back = dot(inverse[...], change).astype(jnp.bfloat16)
        update = dot(jnp.concatenate([back[:size], back[size:]], axis=1), forward[...])
        update_re, update_im = (update[:, :size], update[:, size:])
        terms[slot, 0] = (window_re * update_re + window_im * update_im).astype(jnp.bfloat16)
        terms[slot, 1] = (window_re * update_im - window_im * update_re).astype(jnp.bfloat16)
        placed[slot, 0] = probe_re * update_re + probe_im * update_im
        placed[slot, 1] = probe_re * update_im - probe_im * update_re
    for out, start in zip(outs, targets):
        out[...] = terms[:, :, pl.ds(start, rows)]


def place_kernel(half, corners, pieces, top, middle, bottom, accum):
    size = pieces.shape[-1]
    rows = middle.shape[1]
    width = middle.shape[2]
    accum[...] = jnp.zeros_like(accum)
    for slot in range(pieces.shape[0]):
        base_row, rest_row, base_col, rest_col = corner_of(
            corners, slot, half, rows + 2 * half - size
        )
        for part in range(2):
            block = jnp.concatenate(
                [pieces[slot, part], jnp.zeros((size, LANES), jnp.float32)], axis=1
            )
            block = pltpu.roll(block, rest_col, 1)
            block = jnp.concatenate(
                [block, jnp.zeros((SUBLANES, size + LANES), jnp.float32)], axis=0
            )
            block = pltpu.roll(block, rest_row, 0)
            where = (part, pl.ds(base_row, size + SUBLANES), pl.ds(base_col, size + LANES))
            accum[where] += block
    top[...] = accum[:, :half, :width].astype(jnp.bfloat16)
    middle[...] = accum[:, half : half + rows, :width]
    bottom[...] = accum[:, half + rows : 2 * half + rows, :width].astype(jnp.bfloat16)


def rows_kernel(middle, got_top, got_bottom, left, center, right, total):
    half = got_top.shape[1]
    rows = middle.shape[1]
    cols = center.shape[2]
    total[...] = middle[...]
    total[:, :half] += got_top[...].astype(jnp.float32)
    total[:, rows - half :] += got_bottom[...].astype(jnp.float32)
    left[...] = total[:, :, :half].astype(jnp.bfloat16)
    center[...] = total[:, :, half : half + cols]
    right[...] = total[:, :, half + cols :].astype(jnp.bfloat16)


def cols_kernel(center, got_left, got_right, out):
    half = got_left.shape[2]
    cols = out.shape[2]
    out[...] = center[...]
    out[:, :, :half] += got_left[...].astype(jnp.float32)
    out[:, :, cols - half :] += got_right[...].astype(jnp.float32)


def sums_kernel(count, goals, row, *refs):
    received = refs[count : 2 * count]
    added = refs[2 * count : 2 * count + sum(goal[2] for goal in goals)]
    outs = refs[2 * count + len(added) : -3]
    terms, held, sem = refs[-3:]
    copies = fetch(refs[:count], held, sem)
    num_modes = outs[0].shape[-4]
    slot_count = received[0].shape[0]
    first = min(goal[1] for goal in goals)
    for at in range(count):
        terms[at, first:] = received[at][first:].astype(jnp.float32)
    for copy in copies:
        copy.wait()

    def mode_step(k, carry):
        rest = list(added)
        for (step, first, adds), out in zip(goals, outs):
            region = (row[0] + step).astype(jnp.float32)
            addend = rest.pop(0) if adds else None
            scales = [
                jnp.where(held[at, slot, num_modes] == region, held[at, slot, k], 0.0)
                for at in range(count)
                for slot in range(first, slot_count)
            ]
            for part in range(2):
                pieces = [
                    terms[at, slot, part] for at in range(count) for slot in range(first, slot_count)
                ]
                total = scales[0] * pieces[0]
                for scale, piece in zip(scales[1:], pieces[1:]):
                    total += scale * piece
                if adds:
                    total += addend[k, part].astype(jnp.float32)
                out[k, part] = total.astype(out.dtype)
        return carry

    lax.fori_loop(0, num_modes, mode_step, 0)


def sums(row, goals, weights, received, added, num_modes, dtypes):
    shape = (num_modes,) + received[0].shape[1:]
    return call(
        functools.partial(sums_kernel, len(received), goals),
        [(shape, dtype) for dtype in dtypes],
        (row, SMEM),
        *weights,
        *received,
        *added,
        scratch=[pltpu.VMEM((len(received),) + received[0].shape, jnp.float32)]
        + held_weights(len(weights), weights[0]),
    )


def gradients(object_field, modes, coeffs, offsets, region, counts, intensity):
    size = modes.shape[-1]
    half = size // 2
    num_modes = modes.shape[1]
    slot_count = coeffs.shape[2]
    rows, cols = object_field.shape[1:]
    block = (slot_count,) + modes.shape[2:]
    row = lax.axis_index("row").reshape(1)
    me = lax.axis_index("col").reshape(1)
    steps, goes_to, comes_from = partners("col")
    count = lax.axis_size("col")
    crossing = steps[: count - count // 2]
    staying = steps[count - count // 2 :]

    def move(value, step):
        return lax.ppermute(value, "col", [(i, goes_to(i, step)) for i in range(count)])

    follower = shift(modes, "row", -1)
    lanes = lax.broadcasted_iota(jnp.int32, (slot_count, LANES), 1)
    payload = jnp.where(
        lanes < num_modes,
        jnp.pad(coeffs[0, 0], ((0, 0), (0, LANES - num_modes))),
        region[0, 0].astype(jnp.float32)[:, None],
    )
    weights = {0: payload}
    for step in steps:
        weights[step] = move(payload, step)

    def made_for(step):
        return weights[step] if goes_to(1, step) == comes_from(1, step) else weights[count - step]

    low = object_field.astype(jnp.bfloat16)
    left = shift(low[:, :, cols - half :], "col", 1)
    right = shift(low[:, :, :half], "col", -1)
    wide = (2, half, cols + 2 * half)
    wide_top, wide_bottom = call(
        widen_kernel, [(wide, jnp.bfloat16)] * 2, object_field, left, right
    )
    top = shift(wide_bottom, "row", 1)
    bottom = shift(wide_top, "row", -1)

    blocks = {}
    for group in (crossing, [0] + staying):
        made = slabs(row, [made_for(step) for step in group], modes, follower)
        for step, slab in zip(group, made):
            blocks[step] = move(slab, step) if step else slab

    corners = offsets[0, 0]
    windows, measured = windows_of(corners, object_field, left, right, top, bottom, intensity)
    every = [0] + steps
    whole = (slot_count, 2, size, size)
    *terms, placed = call(
        functools.partial(dft_kernel, goes_to, comes_from, every),
        [(block, jnp.bfloat16)] * count + [(whole, jnp.float32)],
        (counts, SMEM),
        (me, SMEM),
        *[blocks[step] for step in every],
        windows,
        measured,
        *dft_tables(size),
        scratch=[pltpu.VMEM(whole, jnp.bfloat16)] * 2,
        limit=32,
    )
    terms = dict(zip(every, terms))
    received = {step: move(terms[step], step) if step else terms[step] for step in every}

    extent = (2, rows + 2 * half + SUBLANES, cols + 2 * half + LANES)
    over_top, middle, over_bottom = call(
        functools.partial(place_kernel, half),
        [(wide, jnp.bfloat16), ((2, rows, cols + 2 * half), jnp.float32), (wide, jnp.bfloat16)],
        (corners, SMEM),
        placed,
        scratch=[pltpu.VMEM(extent, jnp.float32)],
    )
    got_top = shift(over_bottom, "row", 1)
    got_bottom = shift(over_top, "row", -1)
    side = ((2, rows, half), jnp.bfloat16)
    over_left, center, over_right = call(
        rows_kernel,
        [side, ((2, rows, cols), jnp.float32), side],
        middle,
        got_top,
        got_bottom,
        scratch=[pltpu.VMEM((2, rows, cols + 2 * half), jnp.float32)],
    )
    got_left = shift(over_right, "col", 1)
    got_right = shift(over_left, "col", -1)
    (object_grad,) = call(
        cols_kernel, [(object_field.shape, jnp.float32)], center, got_left, got_right
    )

    def add_up(group, goals, added, dtypes):
        return sums(
            row,
            goals,
            [came_from(step) for step in group],
            [received[step] for step in group],
            added,
            num_modes,
            dtypes,
        )

    def came_from(step):
        return weights[step]

    own, following = add_up(
        [0] + staying, ((0, 0, False), (1, 1, False)), [], [jnp.float32, jnp.float32]
    )
    (following,) = add_up(crossing, ((1, 1, True),), [following], [jnp.bfloat16])
    passed = shift(following, "row", 1)
    (own,) = add_up(crossing, ((0, 0, True),), [own], [jnp.float32])
    mode_grad = (own + passed.astype(jnp.float32))[None]
    return (object_grad, mode_grad)


def solution(mesh):
    in_specs = (
        P(None, "row", "col"),
        P("row", None, None, "col", None),
        P("row", "col", None, None),
        P("row", "col", None, None),
        P("row", "col", None),
        P("row", "col"),
        P("row", "col", None, None, None),
    )
    out_specs = (P(None, "row", "col"), P("row", None, None, "col", None))
    return jax.shard_map(gradients, mesh=mesh, in_specs=in_specs, out_specs=out_specs, check_vma=False)
```

```python
import functools
import math

import jax
import jax.numpy as jnp
import numpy as np
from jax import lax
from jax.experimental import pallas as pl
from jax.experimental.pallas import tpu as pltpu
from jax.sharding import PartitionSpec as P


FLOOR = 0.25
LANES = 128
SUBLANES = 8

VMEM = pl.BlockSpec(memory_space=pltpu.VMEM)
SMEM = pl.BlockSpec(memory_space=pltpu.SMEM)


def shift(value, axis, steps):
    count = lax.axis_size(axis)
    leading, last = (max(0, -steps), min(count, count - steps))
    pairs = [(source, source + steps) for source in range(leading, last)]
    return lax.ppermute(value, axis, pairs)


def dft_tables(length):
    indices = np.arange(length)
    phases = indices[:, None] * indices[None, :] % length
    angles = phases * (2.0 * math.pi / length)
    scaling = 1.0 / math.sqrt(length)
    re = (np.cos(angles) * scaling).astype(np.float32)
    im = (-np.sin(angles) * scaling).astype(np.float32)
    forward = np.block([[re, -im], [im, re]])
    inverse = np.block([[re, im], [-im, re]])
    return jnp.asarray(forward, jnp.bfloat16), jnp.asarray(inverse, jnp.bfloat16)


def partners(axis):
    count = lax.axis_size(axis)
    steps = list(range(count // 2, count)) + list(range(1, count // 2))
    paired = count & (count - 1) == 0

    def goes_to(index, step):
        return index ^ step if paired else (index + step) % count

    def comes_from(index, step):
        return index ^ step if paired else (index - step + count) % count

    return steps, goes_to, comes_from


def call(body, outs, *operands, scratch=(), limit=20):
    arrays = [o[0] if isinstance(o, tuple) else o for o in operands]
    specs = [o[1] if isinstance(o, tuple) else VMEM for o in operands]
    outs = [jax.ShapeDtypeStruct(shape, dtype) for shape, dtype in outs]
    return pl.pallas_call(
        body,
        out_shape=tuple(outs),
        in_specs=specs,
        out_specs=tuple(VMEM for _ in outs),
        scratch_shapes=list(scratch),
        compiler_params=pltpu.CompilerParams(vmem_limit_bytes=limit * 1024 * 1024),
    )(*arrays)


def fetch(arrays, held, sem):
    copies = [pltpu.make_async_copy(a, held.at[at], sem.at[at]) for at, a in enumerate(arrays)]
    for copy in copies:
        copy.start()
    return copies


def held_weights(count, weights):
    return [pltpu.SMEM((count,) + weights.shape, jnp.float32), pltpu.SemaphoreType.DMA((count,))]


def slab_kernel(count, row, *refs):
    own, follower = refs[count : count + 2]
    outs = refs[count + 2 : -3]
    table, held, sem = refs[-3:]
    copies = fetch(refs[:count], held, sem)
    num_modes = own.shape[1]
    table[0] = own[0].astype(jnp.float32)
    table[1] = follower[0].astype(jnp.float32)
    next_row = (row[0] + 1).astype(jnp.float32)
    slots = outs[0].shape[0]
    for copy in copies:
        copy.wait()
    for at, out in enumerate(outs):

        def slot_step(slot, carry, at=at, out=out):
            region = held[at, slots, slot]
            which = jnp.where(region == next_row, 1, 0)
            known = jnp.where(jnp.abs(region - next_row + 0.5) < 1.0, 1.0, 0.0)
            scales = [held[at, slot, k] * known for k in range(num_modes)]
            for part in range(2):
                total = scales[0] * table[which, 0, part]
                for k in range(1, num_modes):
                    total += scales[k] * table[which, k, part]
                out[slot, part] = total.astype(jnp.bfloat16)
            return carry

        lax.fori_loop(0, out.shape[0], slot_step, 0)


def slabs(row, weights, own, follower):
    shape = (weights[0].shape[0] - 1,) + own.shape[2:]
    return call(
        functools.partial(slab_kernel, len(weights)),
        [(shape, jnp.bfloat16)] * len(weights),
        (row, SMEM),
        *weights,
        own,
        follower,
        scratch=[pltpu.VMEM((2,) + own.shape[1:], jnp.float32)]
        + held_weights(len(weights), weights[0]),
    )


def widen_kernel(tile, left, right, top, bottom):
    half = left.shape[-1]
    rows, cols = tile.shape[1:]
    for out, start in ((top, 0), (bottom, rows - half)):
        out[:, :, :half] = left[:, start : start + half]
        out[:, :, half : half + cols] = tile[:, start : start + half].astype(jnp.bfloat16)
        out[:, :, half + cols :] = right[:, start : start + half]


def corner_of(corners, slot, half, limit):
    row = jnp.clip(corners[0, slot] + half, 0, limit)
    col = jnp.clip(corners[1, slot] + half, 0, limit)
    rest_row, rest_col = (row & (SUBLANES - 1), col & (LANES - 1))
    base_row = pl.multiple_of(row - rest_row, SUBLANES)
    base_col = pl.multiple_of(col - rest_col, LANES)
    return base_row, rest_row, base_col, rest_col


def window_kernel(corners, tile, left, right, top, bottom, intensity, out, measured, ext):
    size = out.shape[-1]
    half = left.shape[-1]
    rows, cols = tile.shape[1:]
    for part in range(2):
        ext[part, :half, : cols + 2 * half] = top[part].astype(jnp.float32)
        ext[part, half : half + rows, :half] = left[part].astype(jnp.float32)
        low = tile[part].astype(jnp.bfloat16)
        ext[part, half : half + rows, half : half + cols] = low.astype(jnp.float32)
        ext[part, half : half + rows, half + cols : cols + 2 * half] = right[part].astype(jnp.float32)
        ext[part, half + rows : 2 * half + rows, : cols + 2 * half] = bottom[part].astype(jnp.float32)
    tall = size + SUBLANES
    wide = size + LANES

    def slot_step(slot, carry):
        base_row, rest_row, base_col, rest_col = corner_of(
            corners, slot, half, rows + 2 * half - size
        )
        for part in range(2):
            block = ext[part, pl.ds(base_row, tall), pl.ds(base_col, wide)]
            block = pltpu.roll(block, lax.rem(tall - rest_row, tall), 0)[:size]
            block = pltpu.roll(block, lax.rem(wide - rest_col, wide), 1)[:, :size]
            out[slot, part] = block.astype(jnp.bfloat16)
        measured[slot] = jnp.sqrt(intensity[0, 0, slot].astype(jnp.float32))
        return carry

    lax.fori_loop(0, out.shape[0], slot_step, 0)


def windows_of(corners, tile, left, right, top, bottom, intensity):
    slot_count = intensity.shape[2]
    size = intensity.shape[-1]
    half = left.shape[-1]
    extent = (2, tile.shape[1] + 2 * half + SUBLANES, tile.shape[2] + 2 * half + LANES)
    return call(
        window_kernel,
        [((slot_count, 2, size, size), jnp.bfloat16), ((slot_count, size, size), jnp.float32)],
        (corners, SMEM),
        tile,
        left,
        right,
        top,
        bottom,
        intensity,
        scratch=[pltpu.VMEM(extent, jnp.float32)],
    )


def dft_kernel(goes_to, comes_from, steps, counts, me, *refs):
    blocks = refs[: len(steps)]
    windows, measured, forward, inverse = refs[len(steps) : len(steps) + 4]
    outs = refs[len(steps) + 4 : 2 * len(steps) + 4]
    placed, probes, terms = refs[2 * len(steps) + 4 :]
    size = windows.shape[-1]
    rows = blocks[0].shape[2]
    starts = [pl.multiple_of(comes_from(me[0], step) * rows, rows) for step in steps]
    targets = [pl.multiple_of(goes_to(me[0], step) * rows, rows) for step in steps]

    def dot(left, right):
        return jnp.dot(left, right, preferred_element_type=jnp.float32)

    for block, start in zip(blocks, starts):
        probes[:, :, pl.ds(start, rows)] = block[...]
    for slot in range(windows.shape[0]):
        probe_re = probes[slot, 0].astype(jnp.float32)
        probe_im = probes[slot, 1].astype(jnp.float32)
        window_re = windows[slot, 0].astype(jnp.float32)
        window_im = windows[slot, 1].astype(jnp.float32)
        leaving = jnp.concatenate(
            [
                (probe_re * window_re - probe_im * window_im).astype(jnp.bfloat16),
                (probe_re * window_im + probe_im * window_re).astype(jnp.bfloat16),
            ],
            axis=0,
        )
        half = dot(forward[...], leaving).astype(jnp.bfloat16)
        far = dot(jnp.concatenate([half[:size], half[size:]], axis=1), inverse[...])
        far_re, far_im = (far[:, :size], far[:, size:])
        power = jnp.maximum(far_re * far_re + far_im * far_im, FLOOR * FLOOR)
        live = jnp.where(slot < counts[0, 0], 1.0, 0.0).astype(jnp.float32)
        factor = (measured[slot] * lax.rsqrt(power) - 1.0) * live
        change = jnp.concatenate(
            [(far_re * factor).astype(jnp.bfloat16), (far_im * factor).astype(jnp.bfloat16)], axis=0
        )
        back = dot(inverse[...], change).astype(jnp.bfloat16)
        update = dot(jnp.concatenate([back[:size], back[size:]], axis=1), forward[...])
        update_re, update_im = (update[:, :size], update[:, size:])
        terms[slot, 0] = (window_re * update_re + window_im * update_im).astype(jnp.bfloat16)
        terms[slot, 1] = (window_re * update_im - window_im * update_re).astype(jnp.bfloat16)
        placed[slot, 0] = probe_re * update_re + probe_im * update_im
        placed[slot, 1] = probe_re * update_im - probe_im * update_re
    for out, start in zip(outs, targets):
        out[...] = terms[:, :, pl.ds(start, rows)]


def place_kernel(half, corners, pieces, top, middle, bottom, accum):
    size = pieces.shape[-1]
    rows = middle.shape[1]
    width = middle.shape[2]
    accum[...] = jnp.zeros_like(accum)
    for slot in range(pieces.shape[0]):
        base_row, rest_row, base_col, rest_col = corner_of(
            corners, slot, half, rows + 2 * half - size
        )
        for part in range(2):
            block = jnp.concatenate(
                [pieces[slot, part], jnp.zeros((size, LANES), jnp.float32)], axis=1
            )
            block = pltpu.roll(block, rest_col, 1)
            block = jnp.concatenate(
                [block, jnp.zeros((SUBLANES, size + LANES), jnp.float32)], axis=0
            )
            block = pltpu.roll(block, rest_row, 0)
            where = (part, pl.ds(base_row, size + SUBLANES), pl.ds(base_col, size + LANES))
            accum[where] += block
    top[...] = accum[:, :half, :width].astype(jnp.bfloat16)
    middle[...] = accum[:, half : half + rows, :width]
    bottom[...] = accum[:, half + rows : 2 * half + rows, :width].astype(jnp.bfloat16)


def rows_kernel(middle, got_top, got_bottom, left, center, right, total):
    half = got_top.shape[1]
    rows = middle.shape[1]
    cols = center.shape[2]
    total[...] = middle[...]
    total[:, :half] += got_top[...].astype(jnp.float32)
    total[:, rows - half :] += got_bottom[...].astype(jnp.float32)
    left[...] = total[:, :, :half].astype(jnp.bfloat16)
    center[...] = total[:, :, half : half + cols]
    right[...] = total[:, :, half + cols :].astype(jnp.bfloat16)


def cols_kernel(center, got_left, got_right, out):
    half = got_left.shape[2]
    cols = out.shape[2]
    out[...] = center[...]
    out[:, :, :half] += got_left[...].astype(jnp.float32)
    out[:, :, cols - half :] += got_right[...].astype(jnp.float32)


def sums_kernel(count, goals, row, *refs):
    received = refs[count : 2 * count]
    added = refs[2 * count : 2 * count + sum(goal[2] for goal in goals)]
    outs = refs[2 * count + len(added) : -3]
    terms, held, sem = refs[-3:]
    copies = fetch(refs[:count], held, sem)
    num_modes = outs[0].shape[-4]
    slot_count = received[0].shape[0]
    slots = slot_count
    first = min(goal[1] for goal in goals)
    for at in range(count):
        terms[at, first:] = received[at][first:].astype(jnp.float32)
    for copy in copies:
        copy.wait()

    def mode_step(k, carry):
        rest = list(added)
        for (step, first, adds), out in zip(goals, outs):
            region = (row[0] + step).astype(jnp.float32)
            addend = rest.pop(0) if adds else None
            scales = [
                jnp.where(held[at, slots, slot] == region, held[at, slot, k], 0.0)
                for at in range(count)
                for slot in range(first, slot_count)
            ]
            for part in range(2):
                pieces = [
                    terms[at, slot, part] for at in range(count) for slot in range(first, slot_count)
                ]
                total = scales[0] * pieces[0]
                for scale, piece in zip(scales[1:], pieces[1:]):
                    total += scale * piece
                if adds:
                    total += addend[k, part].astype(jnp.float32)
                out[k, part] = total.astype(out.dtype)
        return carry

    lax.fori_loop(0, num_modes, mode_step, 0)


def sums(row, goals, weights, received, added, num_modes, dtypes):
    shape = (num_modes,) + received[0].shape[1:]
    return call(
        functools.partial(sums_kernel, len(received), goals),
        [(shape, dtype) for dtype in dtypes],
        (row, SMEM),
        *weights,
        *received,
        *added,
        scratch=[pltpu.VMEM((len(received),) + received[0].shape, jnp.float32)]
        + held_weights(len(weights), weights[0]),
    )


def gradients(object_field, modes, coeffs, offsets, region, counts, intensity):
    size = modes.shape[-1]
    half = size // 2
    num_modes = modes.shape[1]
    slot_count = coeffs.shape[2]
    rows, cols = object_field.shape[1:]
    block = (slot_count,) + modes.shape[2:]
    row = lax.axis_index("row").reshape(1)
    me = lax.axis_index("col").reshape(1)
    steps, goes_to, comes_from = partners("col")
    every = [0] + steps
    count = lax.axis_size("col")
    crossing = steps[: count - count // 2]
    staying = steps[count - count // 2 :]

    def move(value, step):
        return lax.ppermute(value, "col", [(i, goes_to(i, step)) for i in range(count)])

    follower = shift(modes, "row", -1)
    payload = jnp.pad(coeffs[0, 0], ((0, 1), (0, LANES - num_modes))) + jnp.pad(
        region[0].astype(jnp.float32), ((slot_count, 0), (0, LANES - slot_count))
    )
    weights = {0: payload}
    for step in steps:
        weights[step] = move(payload, step)

    def made_for(step):
        return weights[step] if goes_to(1, step) == comes_from(1, step) else weights[count - step]

    low = object_field.astype(jnp.bfloat16)
    left = shift(low[:, :, cols - half :], "col", 1)
    right = shift(low[:, :, :half], "col", -1)
    wide = (2, half, cols + 2 * half)
    wide_top, wide_bottom = call(
        widen_kernel, [(wide, jnp.bfloat16)] * 2, object_field, left, right
    )
    top = shift(wide_bottom, "row", 1)
    bottom = shift(wide_top, "row", -1)

    blocks = {}
    made = slabs(row, [made_for(step) for step in every], modes, follower)
    for step, slab in zip(every, made):
        blocks[step] = move(slab, step) if step else slab

    corners = offsets[0, 0].T
    windows, measured = windows_of(corners, object_field, left, right, top, bottom, intensity)
    whole = (slot_count, 2, size, size)
    *terms, placed = call(
        functools.partial(dft_kernel, goes_to, comes_from, every),
        [(block, jnp.bfloat16)] * count + [(whole, jnp.float32)],
        (counts, SMEM),
        (me, SMEM),
        *[blocks[step] for step in every],
        windows,
        measured,
        *dft_tables(size),
        scratch=[pltpu.VMEM(whole, jnp.bfloat16)] * 2,
        limit=32,
    )
    terms = dict(zip(every, terms))
    received = {step: move(terms[step], step) if step else terms[step] for step in every}

    extent = (2, rows + 2 * half + SUBLANES, cols + 2 * half + LANES)
    over_top, middle, over_bottom = call(
        functools.partial(place_kernel, half),
        [(wide, jnp.bfloat16), ((2, rows, cols + 2 * half), jnp.float32), (wide, jnp.bfloat16)],
        (corners, SMEM),
        placed,
        scratch=[pltpu.VMEM(extent, jnp.float32)],
    )
    got_top = shift(over_bottom, "row", 1)
    got_bottom = shift(over_top, "row", -1)
    side = ((2, rows, half), jnp.bfloat16)
    over_left, center, over_right = call(
        rows_kernel,
        [side, ((2, rows, cols), jnp.float32), side],
        middle,
        got_top,
        got_bottom,
        scratch=[pltpu.VMEM((2, rows, cols + 2 * half), jnp.float32)],
    )
    got_left = shift(over_right, "col", 1)
    got_right = shift(over_left, "col", -1)
    (object_grad,) = call(
        cols_kernel, [(object_field.shape, jnp.float32)], center, got_left, got_right
    )

    def add_up(group, goals, added, dtypes):
        return sums(
            row,
            goals,
            [came_from(step) for step in group],
            [received[step] for step in group],
            added,
            num_modes,
            dtypes,
        )

    def came_from(step):
        return weights[step]

    own, following = add_up(
        [0] + staying, ((0, 0, False), (1, 1, False)), [], [jnp.float32, jnp.float32]
    )
    (following,) = add_up(crossing, ((1, 1, True),), [following], [jnp.bfloat16])
    passed = shift(following, "row", 1)
    (own,) = add_up(crossing, ((0, 0, True),), [own], [jnp.float32])
    mode_grad = (own + passed.astype(jnp.float32))[None]
    return (object_grad, mode_grad)


def solution(mesh):
    in_specs = (
        P(None, "row", "col"),
        P("row", None, None, "col", None),
        P("row", "col", None, None),
        P("row", "col", None, None),
        P("row", "col", None),
        P("row", "col"),
        P("row", "col", None, None, None),
    )
    out_specs = (P(None, "row", "col"), P("row", None, None, "col", None))
    return jax.shard_map(gradients, mesh=mesh, in_specs=in_specs, out_specs=out_specs, check_vma=False)
```

```python
import functools
import math

import jax
import jax.numpy as jnp
import numpy as np
from jax import lax
from jax.experimental import pallas as pl
from jax.experimental.pallas import tpu as pltpu
from jax.sharding import PartitionSpec as P


FLOOR = 0.25
LANES = 128
SUBLANES = 8

VMEM = pl.BlockSpec(memory_space=pltpu.VMEM)
SMEM = pl.BlockSpec(memory_space=pltpu.SMEM)
HBM = pl.BlockSpec(memory_space=pltpu.HBM)


def shift(value, axis, steps):
    count = lax.axis_size(axis)
    leading, last = (max(0, -steps), min(count, count - steps))
    pairs = [(source, source + steps) for source in range(leading, last)]
    return lax.ppermute(value, axis, pairs)


def swap(values, axis):
    count = lax.axis_size(axis)
    got = []
    for odd, value in enumerate(values):
        pairs = []
        for i in range(odd, count - 1, 2):
            pairs += [(i, i + 1), (i + 1, i)]
        got.append(lax.ppermute(value, axis, pairs) if pairs else jnp.zeros_like(value))
    return got


def by_side(index, low, high):
    even = index % 2 == 0
    return jnp.where(even, high, low), jnp.where(even, low, high)


def from_sides(index, first, second):
    high, low = by_side(index, second, first)
    return low, high


def dft_tables(length):
    indices = np.arange(length)
    phases = indices[:, None] * indices[None, :] % length
    angles = phases * (2.0 * math.pi / length)
    scaling = 1.0 / math.sqrt(length)
    re = (np.cos(angles) * scaling).astype(np.float32)
    im = (-np.sin(angles) * scaling).astype(np.float32)
    forward = np.block([[re, -im], [im, re]])
    inverse = np.block([[re, im], [-im, re]])
    return jnp.asarray(forward, jnp.bfloat16), jnp.asarray(inverse, jnp.bfloat16)


def partners(axis):
    count = lax.axis_size(axis)
    steps = list(range(1, count))
    paired = count & (count - 1) == 0

    def goes_to(index, step):
        return index ^ step if paired else (index + step) % count

    def comes_from(index, step):
        return index ^ step if paired else (index - step + count) % count

    return steps, goes_to, comes_from


def call(body, outs, *operands, scratch=(), limit=20):
    arrays = [o[0] if isinstance(o, tuple) else o for o in operands]
    arrays = [
        pltpu.with_memory_space_constraint(a, pltpu.HBM)
        if isinstance(o, tuple) and o[1] is HBM
        else a
        for a, o in zip(arrays, operands)
    ]
    specs = [o[1] if isinstance(o, tuple) else VMEM for o in operands]
    outs = [jax.ShapeDtypeStruct(shape, dtype) for shape, dtype in outs]
    return pl.pallas_call(
        body,
        out_shape=tuple(outs),
        in_specs=specs,
        out_specs=tuple(VMEM for _ in outs),
        scratch_shapes=list(scratch),
        compiler_params=pltpu.CompilerParams(vmem_limit_bytes=limit * 1024 * 1024),
    )(*arrays)


def fetch(arrays, held, sem):
    copies = [pltpu.make_async_copy(a, held.at[at], sem.at[at]) for at, a in enumerate(arrays)]
    for copy in copies:
        copy.start()
    return copies


def held_weights(count, weights):
    return [pltpu.SMEM((count,) + weights.shape, jnp.float32), pltpu.SemaphoreType.DMA((count,))]


def slab_kernel(count, row, *refs):
    own, follower = refs[count : count + 2]
    outs = refs[count + 2 : -5]
    table, near, held, sem, near_sem = refs[-5:]
    copy_own = pltpu.make_async_copy(own, near, near_sem)
    copy_own.start()
    copies = fetch(refs[:count], held, sem)
    num_modes = own.shape[1]
    table[1] = follower[0].astype(jnp.float32)
    copy_own.wait()
    table[0] = near[0].astype(jnp.float32)
    next_row = (row[0] + 1).astype(jnp.float32)
    slots = outs[0].shape[0]
    for copy in copies:
        copy.wait()
    for at, out in enumerate(outs):

        def slot_step(slot, carry, at=at, out=out):
            region = held[at, slots, slot]
            which = jnp.where(region == next_row, 1, 0)
            known = jnp.where(jnp.abs(region - next_row + 0.5) < 1.0, 1.0, 0.0)
            scales = [held[at, slot, k] * known for k in range(num_modes)]
            for part in range(2):
                total = scales[0] * table[which, 0, part]
                for k in range(1, num_modes):
                    total += scales[k] * table[which, k, part]
                out[slot, part] = total.astype(jnp.bfloat16)
            return carry

        lax.fori_loop(0, out.shape[0], slot_step, 0)


def slabs(row, weights, own, follower):
    shape = (weights[0].shape[0] - 1,) + own.shape[2:]
    return call(
        functools.partial(slab_kernel, len(weights)),
        [(shape, jnp.bfloat16)] * len(weights),
        (row, SMEM),
        *weights,
        (own, HBM),
        follower,
        scratch=[pltpu.VMEM((2,) + own.shape[1:], jnp.float32), pltpu.VMEM(own.shape, own.dtype)]
        + held_weights(len(weights), weights[0])
        + [pltpu.SemaphoreType.DMA],
    )


def prepare_kernel(
    me, coeffs, region, tile, payload, low, even, odd, coeffs_held, region_held, tile_held, sem
):
    slots, num_modes = coeffs.shape[2:]
    half = even.shape[2]
    copies = [
        pltpu.make_async_copy(source, held, sem.at[at])
        for at, (source, held) in enumerate(
            ((coeffs, coeffs_held), (region, region_held), (tile, tile_held))
        )
    ]
    for copy in copies:
        copy.start()
    payload[...] = jnp.zeros_like(payload)
    for copy in copies:
        copy.wait()
    payload[:slots, :num_modes] = coeffs_held[0, 0]
    payload[slots:, :slots] = region_held[0].astype(jnp.float32)
    low[...] = tile_held[...].astype(jnp.bfloat16)
    first, second = by_side(me[0], low[:, :, :half], low[:, :, low.shape[2] - half :])
    even[...] = first
    odd[...] = second


def widen_kernel(row, me, tile, even, odd, first, second):
    half = even.shape[2]
    rows, _ = tile.shape[1:]

    def extended(start):
        left, right = from_sides(
            me[0], even[:, start : start + half], odd[:, start : start + half]
        )
        return jnp.concatenate([left, tile[:, start : start + half], right], axis=2)

    first[...], second[...] = by_side(row[0], extended(0), extended(rows - half))


def corner_of(corners, slot, half, limit):
    row = jnp.clip(corners[0, slot] + half, 0, limit)
    col = jnp.clip(corners[1, slot] + half, 0, limit)
    rest_row, rest_col = (row & (SUBLANES - 1), col & (LANES - 1))
    base_row = pl.multiple_of(row - rest_row, SUBLANES)
    base_col = pl.multiple_of(col - rest_col, LANES)
    return base_row, rest_row, base_col, rest_col


def window_kernel(
    row, me, corners, tile, side_even, side_odd, end_even, end_odd, intensity, out, measured, ext,
    held, sem,
):
    copy = pltpu.make_async_copy(intensity, held, sem)
    copy.start()
    size = out.shape[-1]
    half = side_even.shape[-1]
    rows, cols = tile.shape[1:]
    left, right = from_sides(me[0], side_even[...], side_odd[...])
    top, bottom = from_sides(row[0], end_even[...], end_odd[...])
    for part in range(2):
        ext[part, :half, : cols + 2 * half] = top[part].astype(jnp.float32)
        ext[part, half : half + rows, :half] = left[part].astype(jnp.float32)
        ext[part, half : half + rows, half : half + cols] = tile[part].astype(jnp.float32)
        ext[part, half : half + rows, half + cols : cols + 2 * half] = right[part].astype(jnp.float32)
        ext[part, half + rows : 2 * half + rows, : cols + 2 * half] = bottom[part].astype(jnp.float32)
    tall = size + SUBLANES
    wide = size + LANES

    def slot_step(slot, carry):
        base_row, rest_row, base_col, rest_col = corner_of(
            corners, slot, half, rows + 2 * half - size
        )
        for part in range(2):
            block = ext[part, pl.ds(base_row, tall), pl.ds(base_col, wide)]
            block = pltpu.roll(block, lax.rem(tall - rest_row, tall), 0)[:size]
            block = pltpu.roll(block, lax.rem(wide - rest_col, wide), 1)[:, :size]
            out[slot, part] = block.astype(jnp.bfloat16)
        return carry

    lax.fori_loop(0, out.shape[0], slot_step, 0)
    copy.wait()
    for slot in range(out.shape[0]):
        measured[slot] = jnp.sqrt(held[0, 0, slot].astype(jnp.float32))


def windows_of(row, me, corners, tile, sides, ends, intensity):
    slot_count = intensity.shape[2]
    size = intensity.shape[-1]
    half = sides[0].shape[-1]
    extent = (2, tile.shape[1] + 2 * half + SUBLANES, tile.shape[2] + 2 * half + LANES)
    return call(
        window_kernel,
        [((slot_count, 2, size, size), jnp.bfloat16), ((slot_count, size, size), jnp.float32)],
        (row, SMEM),
        (me, SMEM),
        (corners, SMEM),
        tile,
        *sides,
        *ends,
        (intensity, HBM),
        scratch=[
            pltpu.VMEM(extent, jnp.float32),
            pltpu.VMEM(intensity.shape, intensity.dtype),
            pltpu.SemaphoreType.DMA,
        ],
    )


def dft_kernel(goes_to, comes_from, steps, counts, me, *refs):
    blocks = refs[: len(steps)]
    windows, measured, forward, inverse = refs[len(steps) : len(steps) + 4]
    outs = refs[len(steps) + 4 : 2 * len(steps) + 4]
    placed, probes, terms = refs[2 * len(steps) + 4 :]
    size = windows.shape[-1]
    rows = blocks[0].shape[2]
    starts = [pl.multiple_of(comes_from(me[0], step) * rows, rows) for step in steps]
    targets = [pl.multiple_of(goes_to(me[0], step) * rows, rows) for step in steps]

    def dot(left, right):
        return jnp.dot(left, right, preferred_element_type=jnp.float32)

    for block, start in zip(blocks, starts):
        probes[:, :, pl.ds(start, rows)] = block[...]
    for slot in range(windows.shape[0]):
        probe_re = probes[slot, 0].astype(jnp.float32)
        probe_im = probes[slot, 1].astype(jnp.float32)
        window_re = windows[slot, 0].astype(jnp.float32)
        window_im = windows[slot, 1].astype(jnp.float32)
        leaving = jnp.concatenate(
            [
                (probe_re * window_re - probe_im * window_im).astype(jnp.bfloat16),
                (probe_re * window_im + probe_im * window_re).astype(jnp.bfloat16),
            ],
            axis=0,
        )
        half = dot(forward[...], leaving).astype(jnp.bfloat16)
        far = dot(jnp.concatenate([half[:size], half[size:]], axis=1), inverse[...])
        far_re, far_im = (far[:, :size], far[:, size:])
        power = jnp.maximum(far_re * far_re + far_im * far_im, FLOOR * FLOOR)
        live = jnp.where(slot < counts[0, 0], 1.0, 0.0).astype(jnp.float32)
        factor = (measured[slot] * lax.rsqrt(power) - 1.0) * live
        change = jnp.concatenate(
            [(far_re * factor).astype(jnp.bfloat16), (far_im * factor).astype(jnp.bfloat16)], axis=0
        )
        back = dot(inverse[...], change).astype(jnp.bfloat16)
        update = dot(jnp.concatenate([back[:size], back[size:]], axis=1), forward[...])
        update_re, update_im = (update[:, :size], update[:, size:])
        terms[slot, 0] = (window_re * update_re + window_im * update_im).astype(jnp.bfloat16)
        terms[slot, 1] = (window_re * update_im - window_im * update_re).astype(jnp.bfloat16)
        placed[slot, 0] = probe_re * update_re + probe_im * update_im
        placed[slot, 1] = probe_re * update_im - probe_im * update_re
    for out, start in zip(outs, targets):
        out[...] = terms[:, :, pl.ds(start, rows)]


def place_kernel(half, row, corners, pieces, first, middle, second, accum):
    size = pieces.shape[-1]
    rows = middle.shape[1]
    width = middle.shape[2]
    accum[...] = jnp.zeros_like(accum)
    for slot in range(pieces.shape[0]):
        base_row, rest_row, base_col, rest_col = corner_of(
            corners, slot, half, rows + 2 * half - size
        )
        for part in range(2):
            block = jnp.concatenate(
                [pieces[slot, part], jnp.zeros((size, LANES), jnp.float32)], axis=1
            )
            block = pltpu.roll(block, rest_col, 1)
            block = jnp.concatenate(
                [block, jnp.zeros((SUBLANES, size + LANES), jnp.float32)], axis=0
            )
            block = pltpu.roll(block, rest_row, 0)
            where = (part, pl.ds(base_row, size + SUBLANES), pl.ds(base_col, size + LANES))
            accum[where] += block
    middle[...] = accum[:, half : half + rows, :width]
    top = accum[:, :half, :width].astype(jnp.bfloat16)
    bottom = accum[:, half + rows : 2 * half + rows, :width].astype(jnp.bfloat16)
    first[...], second[...] = by_side(row[0], top, bottom)


def rows_kernel(row, me, middle, even, odd, first, center, second, total):
    half = even.shape[1]
    rows = middle.shape[1]
    cols = center.shape[2]
    got_top, got_bottom = from_sides(row[0], even[...], odd[...])
    total[...] = middle[...]
    total[:, :half] += got_top.astype(jnp.float32)
    total[:, rows - half :] += got_bottom.astype(jnp.float32)
    center[...] = total[:, :, half : half + cols]
    left = total[:, :, :half].astype(jnp.bfloat16)
    right = total[:, :, half + cols :].astype(jnp.bfloat16)
    first[...], second[...] = by_side(me[0], left, right)


def cols_kernel(me, center, even, odd, out):
    half = even.shape[2]
    cols = out.shape[2]
    got_left, got_right = from_sides(me[0], even[...], odd[...])
    out[...] = center[...]
    out[:, :, :half] += got_left.astype(jnp.float32)
    out[:, :, cols - half :] += got_right.astype(jnp.float32)


def sums_kernel(count, goals, row, *refs):
    received = refs[count : 2 * count]
    added = refs[2 * count : 2 * count + sum(goal[2] for goal in goals)]
    outs = refs[2 * count + len(added) : -3]
    terms, held, sem = refs[-3:]
    copies = fetch(refs[:count], held, sem)
    num_modes = outs[0].shape[-4]
    slot_count = received[0].shape[0]
    slots = slot_count
    first = min(goal[1] for goal in goals)
    for at in range(count):
        terms[at, first:] = received[at][first:].astype(jnp.float32)
    for copy in copies:
        copy.wait()

    def mode_step(k, carry):
        rest = list(added)
        for (step, first, adds), out in zip(goals, outs):
            region = (row[0] + step).astype(jnp.float32)
            addend = rest.pop(0) if adds else None
            scales = [
                jnp.where(held[at, slots, slot] == region, held[at, slot, k], 0.0)
                for at in range(count)
                for slot in range(first, slot_count)
            ]
            for part in range(2):
                pieces = [
                    terms[at, slot, part] for at in range(count) for slot in range(first, slot_count)
                ]
                total = scales[0] * pieces[0]
                for scale, piece in zip(scales[1:], pieces[1:]):
                    total += scale * piece
                if adds:
                    total += addend[k, part].astype(jnp.float32)
                out[k, part] = total.astype(out.dtype)
        return carry

    lax.fori_loop(0, num_modes, mode_step, 0)


def sums(row, goals, weights, received, added, num_modes, dtypes):
    shape = (num_modes,) + received[0].shape[1:]
    return call(
        functools.partial(sums_kernel, len(received), goals),
        [(shape, dtype) for dtype in dtypes],
        (row, SMEM),
        *weights,
        *received,
        *added,
        scratch=[pltpu.VMEM((len(received),) + received[0].shape, jnp.float32)]
        + held_weights(len(weights), weights[0]),
    )


def gradients(object_field, modes, coeffs, offsets, region, counts, intensity):
    size = modes.shape[-1]
    half = size // 2
    num_modes = modes.shape[1]
    slot_count = coeffs.shape[2]
    rows, cols = object_field.shape[1:]
    block = (slot_count,) + modes.shape[2:]
    row = lax.axis_index("row").reshape(1)
    me = lax.axis_index("col").reshape(1)
    steps, goes_to, comes_from = partners("col")
    every = [0] + steps
    count = lax.axis_size("col")
    staying = steps[: count // 2 - 1]
    crossing = steps[count // 2 - 1 :]

    def move(value, step):
        return lax.ppermute(value, "col", [(i, goes_to(i, step)) for i in range(count)])

    follower = shift(modes, "row", -1)
    side = (2, rows, half)
    payload, low, *edges = call(
        prepare_kernel,
        [((slot_count + 1, LANES), jnp.float32), (object_field.shape, jnp.bfloat16)]
        + [(side, jnp.bfloat16)] * 2,
        (me, SMEM),
        (coeffs, HBM),
        (region, HBM),
        (object_field, HBM),
        scratch=[pltpu.VMEM(x.shape, x.dtype) for x in (coeffs, region, object_field)]
        + [pltpu.SemaphoreType.DMA((3,))],
    )
    weights = {0: payload}
    for step in steps:
        weights[step] = move(payload, step)

    def made_for(step):
        return weights[step] if goes_to(1, step) == comes_from(1, step) else weights[count - step]

    sides = swap(edges, "col")
    wide = (2, half, cols + 2 * half)
    ends = call(widen_kernel, [(wide, jnp.bfloat16)] * 2, (row, SMEM), (me, SMEM), low, *sides)
    ends = swap(ends, "row")

    blocks = {}
    made = slabs(row, [made_for(step) for step in every], modes, follower)
    for step, slab in zip(every, made):
        blocks[step] = move(slab, step) if step else slab

    corners = pltpu.with_memory_space_constraint(offsets[0, 0].T, pltpu.HBM)
    windows, measured = windows_of(row, me, corners, low, sides, ends, intensity)
    whole = (slot_count, 2, size, size)
    *terms, placed = call(
        functools.partial(dft_kernel, goes_to, comes_from, every),
        [(block, jnp.bfloat16)] * count + [(whole, jnp.float32)],
        (counts, SMEM),
        (me, SMEM),
        *[blocks[step] for step in every],
        windows,
        measured,
        *dft_tables(size),
        scratch=[pltpu.VMEM(whole, jnp.bfloat16)] * 2,
        limit=32,
    )
    terms = dict(zip(every, terms))
    received = {step: move(terms[step], step) if step else terms[step] for step in every}

    extent = (2, rows + 2 * half + SUBLANES, cols + 2 * half + LANES)
    even, middle, odd = call(
        functools.partial(place_kernel, half),
        [(wide, jnp.bfloat16), ((2, rows, cols + 2 * half), jnp.float32), (wide, jnp.bfloat16)],
        (row, SMEM),
        (corners, SMEM),
        placed,
        scratch=[pltpu.VMEM(extent, jnp.float32)],
    )
    over_ends = swap([even, odd], "row")
    even, center, odd = call(
        rows_kernel,
        [(side, jnp.bfloat16), ((2, rows, cols), jnp.float32), (side, jnp.bfloat16)],
        (row, SMEM),
        (me, SMEM),
        middle,
        *over_ends,
        scratch=[pltpu.VMEM((2, rows, cols + 2 * half), jnp.float32)],
    )
    over_sides = swap([even, odd], "col")
    (object_grad,) = call(
        cols_kernel, [(object_field.shape, jnp.float32)], (me, SMEM), center, *over_sides
    )

    def add_up(group, goals, added, dtypes):
        return sums(
            row,
            goals,
            [came_from(step) for step in group],
            [received[step] for step in group],
            added,
            num_modes,
            dtypes,
        )

    def came_from(step):
        return weights[step]

    own, following = add_up(
        [0] + staying, ((0, 0, False), (1, 1, False)), [], [jnp.float32, jnp.float32]
    )
    (following,) = add_up(crossing, ((1, 1, True),), [following], [jnp.bfloat16])
    passed = shift(following, "row", 1)
    (own,) = add_up(crossing, ((0, 0, True),), [own], [jnp.float32])
    mode_grad = (own + passed.astype(jnp.float32))[None]
    return (object_grad, mode_grad)


def solution(mesh):
    in_specs = (
        P(None, "row", "col"),
        P("row", None, None, "col", None),
        P("row", "col", None, None),
        P("row", "col", None, None),
        P("row", "col", None),
        P("row", "col"),
        P("row", "col", None, None, None),
    )
    out_specs = (P(None, "row", "col"), P("row", None, None, "col", None))
    return jax.shard_map(gradients, mesh=mesh, in_specs=in_specs, out_specs=out_specs, check_vma=False)
```

```python
import functools
import math

import jax
import jax.numpy as jnp
import numpy as np
from jax import lax
from jax.experimental import pallas as pl
from jax.experimental.pallas import tpu as pltpu
from jax.sharding import PartitionSpec as P


FLOOR = 0.25
LANES = 128
SUBLANES = 8

VMEM = pl.BlockSpec(memory_space=pltpu.VMEM)
SMEM = pl.BlockSpec(memory_space=pltpu.SMEM)
HBM = pl.BlockSpec(memory_space=pltpu.HBM)


def shift(value, axis, steps):
    count = lax.axis_size(axis)
    leading, last = (max(0, -steps), min(count, count - steps))
    pairs = [(source, source + steps) for source in range(leading, last)]
    return lax.ppermute(value, axis, pairs)


def swap(values, axis):
    count = lax.axis_size(axis)
    got = []
    for odd, value in enumerate(values):
        pairs = []
        for i in range(odd, count - 1, 2):
            pairs += [(i, i + 1), (i + 1, i)]
        got.append(lax.ppermute(value, axis, pairs) if pairs else jnp.zeros_like(value))
    return got


def by_side(index, low, high):
    even = index % 2 == 0
    return jnp.where(even, high, low), jnp.where(even, low, high)


def from_sides(index, first, second):
    high, low = by_side(index, second, first)
    return low, high


def dft_tables(length):
    indices = np.arange(length)
    phases = indices[:, None] * indices[None, :] % length
    angles = phases * (2.0 * math.pi / length)
    scaling = 1.0 / math.sqrt(length)
    re = (np.cos(angles) * scaling).astype(np.float32)
    im = (-np.sin(angles) * scaling).astype(np.float32)
    forward = np.block([[re, -im], [im, re]])
    inverse = np.block([[re, im], [-im, re]])
    return jnp.asarray(forward, jnp.bfloat16), jnp.asarray(inverse, jnp.bfloat16)


def transfer_order(count):
    half = count // 2
    return [half] * (half > 0) + list(range(1, half)) + list(range(half + 1, count))


def partners(axis):
    count = lax.axis_size(axis)
    steps = transfer_order(count)
    paired = count & (count - 1) == 0

    def goes_to(index, step):
        return index ^ step if paired else (index + step) % count

    def comes_from(index, step):
        return index ^ step if paired else (index - step + count) % count

    return steps, goes_to, comes_from


def call(body, outs, *operands, scratch=(), limit=20):
    arrays = [o[0] if isinstance(o, tuple) else o for o in operands]
    arrays = [
        pltpu.with_memory_space_constraint(a, pltpu.HBM)
        if isinstance(o, tuple) and o[1] is HBM
        else a
        for a, o in zip(arrays, operands)
    ]
    specs = [o[1] if isinstance(o, tuple) else VMEM for o in operands]
    outs = [jax.ShapeDtypeStruct(shape, dtype) for shape, dtype in outs]
    return pl.pallas_call(
        body,
        out_shape=tuple(outs),
        in_specs=specs,
        out_specs=tuple(VMEM for _ in outs),
        scratch_shapes=list(scratch),
        compiler_params=pltpu.CompilerParams(vmem_limit_bytes=limit * 1024 * 1024),
    )(*arrays)


def fetch(arrays, places, held, sem):
    copies = [
        pltpu.make_async_copy(arrays[i].at[block], held.at[at], sem.at[at])
        for at, (i, block) in enumerate(places)
    ]
    for copy in copies:
        copy.start()
    return copies


def held_weights(count, weights):
    shape = (count,) + weights.shape[1:]
    return [pltpu.SMEM(shape, jnp.float32), pltpu.SemaphoreType.DMA((count,))]


def slab_kernel(count, places, row, *refs):
    own, follower = refs[count : count + 2]
    outs = refs[count + 2 : -5]
    table, near, held, sem, near_sem = refs[-5:]
    copy_own = pltpu.make_async_copy(own, near, near_sem)
    copy_own.start()
    copies = fetch(refs[:count], places, held, sem)
    num_modes = own.shape[1]
    table[1] = follower[0].astype(jnp.float32)
    copy_own.wait()
    table[0] = near[0].astype(jnp.float32)
    next_row = (row[0] + 1).astype(jnp.float32)
    slots = outs[0].shape[0]
    for copy in copies:
        copy.wait()
    for at, out in enumerate(outs):

        def slot_step(slot, carry, at=at, out=out):
            region = held[at, slots, slot]
            which = jnp.where(region == next_row, 1, 0)
            known = jnp.where(jnp.abs(region - next_row + 0.5) < 1.0, 1.0, 0.0)
            scales = [held[at, slot, k] * known for k in range(num_modes)]
            for part in range(2):
                total = scales[0] * table[which, 0, part]
                for k in range(1, num_modes):
                    total += scales[k] * table[which, k, part]
                out[slot, part] = total.astype(jnp.bfloat16)
            return carry

        lax.fori_loop(0, out.shape[0], slot_step, 0)


def slabs(row, weights, places, own, follower):
    shape = (weights[0].shape[1] - 1,) + own.shape[2:]
    return call(
        functools.partial(slab_kernel, len(weights), places),
        [(shape, jnp.bfloat16)] * len(places),
        (row, SMEM),
        *weights,
        (own, HBM),
        follower,
        scratch=[pltpu.VMEM((2,) + own.shape[1:], jnp.float32), pltpu.VMEM(own.shape, own.dtype)]
        + held_weights(len(places), weights[0])
        + [pltpu.SemaphoreType.DMA],
    )


def prepare_kernel(
    me, coeffs, region, tile, payload, low, even, odd, coeffs_held, region_held, tile_held, sem
):
    slots, num_modes = coeffs.shape[2:]
    half = even.shape[2]
    copies = [
        pltpu.make_async_copy(source, held, sem.at[at])
        for at, (source, held) in enumerate(
            ((coeffs, coeffs_held), (region, region_held), (tile, tile_held))
        )
    ]
    for copy in copies:
        copy.start()
    payload[...] = jnp.zeros_like(payload)
    for copy in copies:
        copy.wait()
    payload[:slots, :num_modes] = coeffs_held[0, 0]
    payload[slots:, :slots] = region_held[0].astype(jnp.float32)
    low[...] = tile_held[...].astype(jnp.bfloat16)
    first, second = by_side(me[0], low[:, :, :half], low[:, :, low.shape[2] - half :])
    even[...] = first
    odd[...] = second


def pair_kernel(mine, across, out):
    out[0] = mine[...]
    out[1] = across[...]


def widen_kernel(row, me, tile, even, odd, first, second):
    half = even.shape[2]
    rows, _ = tile.shape[1:]

    def extended(start):
        left, right = from_sides(
            me[0], even[:, start : start + half], odd[:, start : start + half]
        )
        return jnp.concatenate([left, tile[:, start : start + half], right], axis=2)

    first[...], second[...] = by_side(row[0], extended(0), extended(rows - half))


def corner_of(corners, slot, half, limit):
    row = jnp.clip(corners[0, slot] + half, 0, limit)
    col = jnp.clip(corners[1, slot] + half, 0, limit)
    rest_row, rest_col = (row & (SUBLANES - 1), col & (LANES - 1))
    base_row = pl.multiple_of(row - rest_row, SUBLANES)
    base_col = pl.multiple_of(col - rest_col, LANES)
    return base_row, rest_row, base_col, rest_col


def window_kernel(
    row, me, corners, tile, side_even, side_odd, end_even, end_odd, intensity, out, measured, ext,
    held, sem,
):
    copy = pltpu.make_async_copy(intensity, held, sem)
    copy.start()
    size = out.shape[-1]
    half = side_even.shape[-1]
    rows, cols = tile.shape[1:]
    left, right = from_sides(me[0], side_even[...], side_odd[...])
    top, bottom = from_sides(row[0], end_even[...], end_odd[...])
    for part in range(2):
        ext[part, :half, : cols + 2 * half] = top[part].astype(jnp.float32)
        ext[part, half : half + rows, :half] = left[part].astype(jnp.float32)
        ext[part, half : half + rows, half : half + cols] = tile[part].astype(jnp.float32)
        ext[part, half : half + rows, half + cols : cols + 2 * half] = right[part].astype(jnp.float32)
        ext[part, half + rows : 2 * half + rows, : cols + 2 * half] = bottom[part].astype(jnp.float32)
    tall = size + SUBLANES
    wide = size + LANES

    def slot_step(slot, carry):
        base_row, rest_row, base_col, rest_col = corner_of(
            corners, slot, half, rows + 2 * half - size
        )
        for part in range(2):
            block = ext[part, pl.ds(base_row, tall), pl.ds(base_col, wide)]
            block = pltpu.roll(block, lax.rem(tall - rest_row, tall), 0)[:size]
            block = pltpu.roll(block, lax.rem(wide - rest_col, wide), 1)[:, :size]
            out[slot, part] = block.astype(jnp.bfloat16)
        return carry

    lax.fori_loop(0, out.shape[0], slot_step, 0)
    copy.wait()
    for slot in range(out.shape[0]):
        measured[slot] = jnp.sqrt(held[0, 0, slot].astype(jnp.float32))


def windows_of(row, me, corners, tile, sides, ends, intensity):
    slot_count = intensity.shape[2]
    size = intensity.shape[-1]
    half = sides[0].shape[-1]
    extent = (2, tile.shape[1] + 2 * half + SUBLANES, tile.shape[2] + 2 * half + LANES)
    return call(
        window_kernel,
        [((slot_count, 2, size, size), jnp.bfloat16), ((slot_count, size, size), jnp.float32)],
        (row, SMEM),
        (me, SMEM),
        (corners, SMEM),
        tile,
        *sides,
        *ends,
        (intensity, HBM),
        scratch=[
            pltpu.VMEM(extent, jnp.float32),
            pltpu.VMEM(intensity.shape, intensity.dtype),
            pltpu.SemaphoreType.DMA,
        ],
    )


def dft_kernel(goes_to, comes_from, steps, counts, me, *refs):
    blocks = refs[: len(steps)]
    windows, measured, forward, inverse = refs[len(steps) : len(steps) + 4]
    outs = refs[len(steps) + 4 : 2 * len(steps) + 4]
    placed, probes, terms = refs[2 * len(steps) + 4 :]
    size = windows.shape[-1]
    rows = blocks[0].shape[2]
    starts = [pl.multiple_of(comes_from(me[0], step) * rows, rows) for step in steps]
    targets = [pl.multiple_of(goes_to(me[0], step) * rows, rows) for step in steps]

    def dot(left, right):
        return jnp.dot(left, right, preferred_element_type=jnp.float32)

    for block, start in zip(blocks, starts):
        probes[:, :, pl.ds(start, rows)] = block[...]
    for slot in range(windows.shape[0]):
        probe_re = probes[slot, 0].astype(jnp.float32)
        probe_im = probes[slot, 1].astype(jnp.float32)
        window_re = windows[slot, 0].astype(jnp.float32)
        window_im = windows[slot, 1].astype(jnp.float32)
        leaving = jnp.concatenate(
            [
                (probe_re * window_re - probe_im * window_im).astype(jnp.bfloat16),
                (probe_re * window_im + probe_im * window_re).astype(jnp.bfloat16),
            ],
            axis=0,
        )
        half = dot(forward[...], leaving).astype(jnp.bfloat16)
        far = dot(jnp.concatenate([half[:size], half[size:]], axis=1), inverse[...])
        far_re, far_im = (far[:, :size], far[:, size:])
        power = jnp.maximum(far_re * far_re + far_im * far_im, FLOOR * FLOOR)
        live = jnp.where(slot < counts[0, 0], 1.0, 0.0).astype(jnp.float32)
        factor = (measured[slot] * lax.rsqrt(power) - 1.0) * live
        change = jnp.concatenate(
            [(far_re * factor).astype(jnp.bfloat16), (far_im * factor).astype(jnp.bfloat16)], axis=0
        )
        back = dot(inverse[...], change).astype(jnp.bfloat16)
        update = dot(jnp.concatenate([back[:size], back[size:]], axis=1), forward[...])
        update_re, update_im = (update[:, :size], update[:, size:])
        terms[slot, 0] = (window_re * update_re + window_im * update_im).astype(jnp.bfloat16)
        terms[slot, 1] = (window_re * update_im - window_im * update_re).astype(jnp.bfloat16)
        placed[slot, 0] = probe_re * update_re + probe_im * update_im
        placed[slot, 1] = probe_re * update_im - probe_im * update_re
    for out, start in zip(outs, targets):
        out[...] = terms[:, :, pl.ds(start, rows)]


def place_kernel(half, row, corners, pieces, first, middle, second, accum):
    size = pieces.shape[-1]
    rows = middle.shape[1]
    width = middle.shape[2]
    accum[...] = jnp.zeros_like(accum)
    for slot in range(pieces.shape[0]):
        base_row, rest_row, base_col, rest_col = corner_of(
            corners, slot, half, rows + 2 * half - size
        )
        for part in range(2):
            block = jnp.concatenate(
                [pieces[slot, part], jnp.zeros((size, LANES), jnp.float32)], axis=1
            )
            block = pltpu.roll(block, rest_col, 1)
            block = jnp.concatenate(
                [block, jnp.zeros((SUBLANES, size + LANES), jnp.float32)], axis=0
            )
            block = pltpu.roll(block, rest_row, 0)
            where = (part, pl.ds(base_row, size + SUBLANES), pl.ds(base_col, size + LANES))
            accum[where] += block
    middle[...] = accum[:, half : half + rows, :width]
    top = accum[:, :half, :width].astype(jnp.bfloat16)
    bottom = accum[:, half + rows : 2 * half + rows, :width].astype(jnp.bfloat16)
    first[...], second[...] = by_side(row[0], top, bottom)


def rows_kernel(row, me, middle, even, odd, first, center, second, total):
    half = even.shape[1]
    rows = middle.shape[1]
    cols = center.shape[2]
    got_top, got_bottom = from_sides(row[0], even[...], odd[...])
    total[...] = middle[...]
    total[:, :half] += got_top.astype(jnp.float32)
    total[:, rows - half :] += got_bottom.astype(jnp.float32)
    center[...] = total[:, :, half : half + cols]
    left = total[:, :, :half].astype(jnp.bfloat16)
    right = total[:, :, half + cols :].astype(jnp.bfloat16)
    first[...], second[...] = by_side(me[0], left, right)


def cols_kernel(me, center, even, odd, out):
    half = even.shape[2]
    cols = out.shape[2]
    got_left, got_right = from_sides(me[0], even[...], odd[...])
    out[...] = center[...]
    out[:, :, :half] += got_left.astype(jnp.float32)
    out[:, :, cols - half :] += got_right.astype(jnp.float32)


def sums_kernel(held_in, places, goals, row, *refs):
    count = len(places)
    received = refs[held_in : held_in + count]
    added = refs[held_in + count : held_in + count + sum(goal[2] for goal in goals)]
    outs = refs[held_in + count + len(added) : -3]
    terms, held, sem = refs[-3:]
    copies = fetch(refs[:held_in], places, held, sem)
    num_modes = outs[0].shape[-4]
    slot_count = received[0].shape[0]
    slots = slot_count
    first = min(goal[1] for goal in goals)
    for at in range(count):
        terms[at, first:] = received[at][first:].astype(jnp.float32)
    for copy in copies:
        copy.wait()

    def mode_step(k, carry):
        rest = list(added)
        for (step, first, adds), out in zip(goals, outs):
            region = (row[0] + step).astype(jnp.float32)
            addend = rest.pop(0) if adds else None
            scales = [
                jnp.where(held[at, slots, slot] == region, held[at, slot, k], 0.0)
                for at in range(count)
                for slot in range(first, slot_count)
            ]
            for part in range(2):
                pieces = [
                    terms[at, slot, part] for at in range(count) for slot in range(first, slot_count)
                ]
                total = scales[0] * pieces[0]
                for scale, piece in zip(scales[1:], pieces[1:]):
                    total += scale * piece
                if adds:
                    total += addend[k, part].astype(jnp.float32)
                out[k, part] = total.astype(out.dtype)
        return carry

    lax.fori_loop(0, num_modes, mode_step, 0)


def sums(row, goals, weights, places, received, added, num_modes, dtypes):
    shape = (num_modes,) + received[0].shape[1:]
    return call(
        functools.partial(sums_kernel, len(weights), places, goals),
        [(shape, dtype) for dtype in dtypes],
        (row, SMEM),
        *weights,
        *received,
        *added,
        scratch=[pltpu.VMEM((len(received),) + received[0].shape, jnp.float32)]
        + held_weights(len(places), weights[0]),
    )


def gradients(object_field, modes, coeffs, offsets, region, counts, intensity):
    size = modes.shape[-1]
    half = size // 2
    num_modes = modes.shape[1]
    slot_count = coeffs.shape[2]
    rows, cols = object_field.shape[1:]
    block = (slot_count,) + modes.shape[2:]
    row = lax.axis_index("row").reshape(1)
    me = lax.axis_index("col").reshape(1)
    steps, goes_to, comes_from = partners("col")
    every = [0] + steps
    count = lax.axis_size("col")
    middle_step = count // 2
    near = list(range(1, middle_step))
    crossing = list(range(max(middle_step, 1), count))

    def move(value, step):
        return lax.ppermute(value, "col", [(i, goes_to(i, step)) for i in range(count)])

    side = (2, rows, half)
    payload, low, *edges = call(
        prepare_kernel,
        [((slot_count + 1, LANES), jnp.float32), (object_field.shape, jnp.bfloat16)]
        + [(side, jnp.bfloat16)] * 2,
        (me, SMEM),
        (coeffs, HBM),
        (region, HBM),
        (object_field, HBM),
        scratch=[pltpu.VMEM(x.shape, x.dtype) for x in (coeffs, region, object_field)]
        + [pltpu.SemaphoreType.DMA((3,))],
    )
    if count > 1 and count & (count - 1) == 0:
        across = move(payload, middle_step)
        blocks_shape = (2,) + payload.shape
        (pair,) = call(pair_kernel, [(blocks_shape, jnp.float32)], payload, across)
        weights = [pair] + [move(pair, step) for step in near]

        def made_at(step):
            return step % middle_step, step // middle_step

        came_at = made_at
    else:
        weights = [payload[None]]
        weights += [move(payload[None], step) for step in range(1, count)]

        def made_at(step):
            return -step % count, 0

        def came_at(step):
            return step, 0

    follower = shift(modes, "row", -1)

    sides = swap(edges, "col")
    wide = (2, half, cols + 2 * half)
    ends = call(widen_kernel, [(wide, jnp.bfloat16)] * 2, (row, SMEM), (me, SMEM), low, *sides)
    ends = swap(ends, "row")

    blocks = {}
    made = slabs(row, weights, [made_at(step) for step in every], modes, follower)
    for step, slab in zip(every, made):
        blocks[step] = move(slab, step) if step else slab

    corners = pltpu.with_memory_space_constraint(offsets[0, 0].T, pltpu.HBM)
    windows, measured = windows_of(row, me, corners, low, sides, ends, intensity)
    whole = (slot_count, 2, size, size)
    *terms, placed = call(
        functools.partial(dft_kernel, goes_to, comes_from, every),
        [(block, jnp.bfloat16)] * count + [(whole, jnp.float32)],
        (counts, SMEM),
        (me, SMEM),
        *[blocks[step] for step in every],
        windows,
        measured,
        *dft_tables(size),
        scratch=[pltpu.VMEM(whole, jnp.bfloat16)] * 2,
        limit=32,
    )
    terms = dict(zip(every, terms))
    received = {step: move(terms[step], step) if step else terms[step] for step in every}

    extent = (2, rows + 2 * half + SUBLANES, cols + 2 * half + LANES)
    even, middle, odd = call(
        functools.partial(place_kernel, half),
        [(wide, jnp.bfloat16), ((2, rows, cols + 2 * half), jnp.float32), (wide, jnp.bfloat16)],
        (row, SMEM),
        (corners, SMEM),
        placed,
        scratch=[pltpu.VMEM(extent, jnp.float32)],
    )
    over_ends = swap([even, odd], "row")
    even, center, odd = call(
        rows_kernel,
        [(side, jnp.bfloat16), ((2, rows, cols), jnp.float32), (side, jnp.bfloat16)],
        (row, SMEM),
        (me, SMEM),
        middle,
        *over_ends,
        scratch=[pltpu.VMEM((2, rows, cols + 2 * half), jnp.float32)],
    )
    over_sides = swap([even, odd], "col")
    (object_grad,) = call(
        cols_kernel, [(object_field.shape, jnp.float32)], (me, SMEM), center, *over_sides
    )

    def add_up(group, goals, added, dtypes):
        return sums(
            row,
            goals,
            weights,
            [came_at(step) for step in group],
            [received[step] for step in group],
            added,
            num_modes,
            dtypes,
        )

    own, following = add_up(
        [0] + near, ((0, 0, False), (1, 1, False)), [], [jnp.float32, jnp.float32]
    )
    (following,) = add_up(crossing, ((1, 1, True),), [following], [jnp.bfloat16])
    passed = shift(following, "row", 1)
    (own,) = add_up(crossing, ((0, 0, True),), [own], [jnp.float32])
    mode_grad = (own + passed.astype(jnp.float32))[None]
    return (object_grad, mode_grad)


def solution(mesh):
    in_specs = (
        P(None, "row", "col"),
        P("row", None, None, "col", None),
        P("row", "col", None, None),
        P("row", "col", None, None),
        P("row", "col", None),
        P("row", "col"),
        P("row", "col", None, None, None),
    )
    out_specs = (P(None, "row", "col"), P("row", None, None, "col", None))
    return jax.shard_map(gradients, mesh=mesh, in_specs=in_specs, out_specs=out_specs, check_vma=False)
```

```python
import functools
import math

import jax
import jax.numpy as jnp
import numpy as np
from jax import lax
from jax.experimental import pallas as pl
from jax.experimental.pallas import tpu as pltpu
from jax.sharding import PartitionSpec as P


FLOOR = 0.25
LANES = 128
SUBLANES = 8

VMEM = pl.BlockSpec(memory_space=pltpu.VMEM)
SMEM = pl.BlockSpec(memory_space=pltpu.SMEM)
HBM = pl.BlockSpec(memory_space=pltpu.HBM)


def shift(value, axis, steps):
    count = lax.axis_size(axis)
    leading, last = (max(0, -steps), min(count, count - steps))
    pairs = [(source, source + steps) for source in range(leading, last)]
    return lax.ppermute(value, axis, pairs)


def swap(values, axis):
    count = lax.axis_size(axis)
    got = []
    for odd, value in enumerate(values):
        pairs = []
        for i in range(odd, count - 1, 2):
            pairs += [(i, i + 1), (i + 1, i)]
        got.append(lax.ppermute(value, axis, pairs) if pairs else jnp.zeros_like(value))
    return got


def by_side(index, low, high):
    even = index % 2 == 0
    return jnp.where(even, high, low), jnp.where(even, low, high)


def from_sides(index, first, second):
    high, low = by_side(index, second, first)
    return low, high


def dft_tables(length):
    indices = np.arange(length)
    phases = indices[:, None] * indices[None, :] % length
    angles = phases * (2.0 * math.pi / length)
    scaling = 1.0 / math.sqrt(length)
    re = (np.cos(angles) * scaling).astype(np.float32)
    im = (-np.sin(angles) * scaling).astype(np.float32)
    forward = np.block([[re, -im], [im, re]])
    inverse = np.block([[re, im], [-im, re]])
    return jnp.asarray(forward, jnp.bfloat16), jnp.asarray(inverse, jnp.bfloat16)


def transfer_order(count):
    half = count // 2
    return [half] * (half > 0) + list(range(1, half)) + list(range(half + 1, count))


def partners(axis):
    count = lax.axis_size(axis)
    steps = transfer_order(count)
    paired = count & (count - 1) == 0

    def goes_to(index, step):
        return index ^ step if paired else (index + step) % count

    def comes_from(index, step):
        return index ^ step if paired else (index - step + count) % count

    return steps, goes_to, comes_from


def call(body, outs, *operands, scratch=(), limit=20):
    arrays = [o[0] if isinstance(o, tuple) else o for o in operands]
    arrays = [
        pltpu.with_memory_space_constraint(a, pltpu.HBM)
        if isinstance(o, tuple) and o[1] is HBM
        else a
        for a, o in zip(arrays, operands)
    ]
    specs = [o[1] if isinstance(o, tuple) else VMEM for o in operands]
    outs = [jax.ShapeDtypeStruct(shape, dtype) for shape, dtype in outs]
    return pl.pallas_call(
        body,
        out_shape=tuple(outs),
        in_specs=specs,
        out_specs=tuple(VMEM for _ in outs),
        scratch_shapes=list(scratch),
        compiler_params=pltpu.CompilerParams(vmem_limit_bytes=limit * 1024 * 1024),
    )(*arrays)


def fetch(arrays, places, held, sem):
    copies = [
        pltpu.make_async_copy(arrays[i].at[block], held.at[at], sem.at[at])
        for at, (i, block) in enumerate(places)
    ]
    for copy in copies:
        copy.start()
    return copies


def held_weights(count, weights):
    shape = (count,) + weights.shape[1:]
    return [pltpu.SMEM(shape, jnp.float32), pltpu.SemaphoreType.DMA((count,))]


def slab_kernel(count, places, row, *refs):
    own, follower = refs[count : count + 2]
    outs = refs[count + 2 : -5]
    table, near, held, sem, near_sem = refs[-5:]
    copy_own = pltpu.make_async_copy(own, near, near_sem)
    copy_own.start()
    copies = fetch(refs[:count], places, held, sem)
    num_modes = own.shape[1]
    table[1] = follower[0].astype(jnp.float32)
    copy_own.wait()
    table[0] = near[0].astype(jnp.float32)
    next_row = (row[0] + 1).astype(jnp.float32)
    slots = outs[0].shape[0]
    for copy in copies:
        copy.wait()
    for at, out in enumerate(outs):

        def slot_step(slot, carry, at=at, out=out):
            region = held[at, slots, slot]
            which = jnp.where(region == next_row, 1, 0)
            known = jnp.where(jnp.abs(region - next_row + 0.5) < 1.0, 1.0, 0.0)
            scales = [held[at, slot, k] * known for k in range(num_modes)]
            for part in range(2):
                total = scales[0] * table[which, 0, part]
                for k in range(1, num_modes):
                    total += scales[k] * table[which, k, part]
                out[slot, part] = total.astype(jnp.bfloat16)
            return carry

        lax.fori_loop(0, out.shape[0], slot_step, 0)


def slabs(row, weights, places, own, follower):
    shape = (weights[0].shape[1] - 1,) + own.shape[2:]
    return call(
        functools.partial(slab_kernel, len(weights), places),
        [(shape, jnp.bfloat16)] * len(places),
        (row, SMEM),
        *weights,
        (own, HBM),
        follower,
        scratch=[pltpu.VMEM((2,) + own.shape[1:], jnp.float32), pltpu.VMEM(own.shape, own.dtype)]
        + held_weights(len(places), weights[0])
        + [pltpu.SemaphoreType.DMA],
    )


def prepare_kernel(me, tile, low, even, odd, held, sem):
    half = even.shape[2]
    copy = pltpu.make_async_copy(tile, held, sem)
    copy.start()
    copy.wait()
    low[...] = held[...].astype(jnp.bfloat16)
    first, second = by_side(me[0], low[:, :, :half], low[:, :, low.shape[2] - half :])
    even[...] = first
    odd[...] = second


def pair_kernel(coeffs, region, *refs):
    across = refs[:-4]
    out, coeffs_held, region_held, sem = refs[-4:]
    slots, num_modes = coeffs.shape[2:]
    copies = [
        pltpu.make_async_copy(coeffs, coeffs_held, sem.at[0]),
        pltpu.make_async_copy(region, region_held, sem.at[1]),
    ]
    for copy in copies:
        copy.start()
    out[...] = jnp.zeros_like(out)
    for copy in copies:
        copy.wait()
    for at, (weights, regions) in enumerate([(coeffs_held, region_held), across][: out.shape[0]]):
        out[at, :slots, :num_modes] = weights[0, 0]
        out[at, slots:, :slots] = regions[0].astype(jnp.float32)


def widen_kernel(row, me, tile, even, odd, first, second):
    half = even.shape[2]
    rows, _ = tile.shape[1:]

    def extended(start):
        left, right = from_sides(
            me[0], even[:, start : start + half], odd[:, start : start + half]
        )
        return jnp.concatenate([left, tile[:, start : start + half], right], axis=2)

    first[...], second[...] = by_side(row[0], extended(0), extended(rows - half))


def corner_of(corners, slot, half, limit):
    row = jnp.clip(corners[0, slot] + half, 0, limit)
    col = jnp.clip(corners[1, slot] + half, 0, limit)
    rest_row, rest_col = (row & (SUBLANES - 1), col & (LANES - 1))
    base_row = pl.multiple_of(row - rest_row, SUBLANES)
    base_col = pl.multiple_of(col - rest_col, LANES)
    return base_row, rest_row, base_col, rest_col


def window_kernel(
    row, me, corners, tile, side_even, side_odd, end_even, end_odd, intensity, out, measured, ext,
    held, sem,
):
    copy = pltpu.make_async_copy(intensity, held, sem)
    copy.start()
    size = out.shape[-1]
    half = side_even.shape[-1]
    rows, cols = tile.shape[1:]
    left, right = from_sides(me[0], side_even[...], side_odd[...])
    top, bottom = from_sides(row[0], end_even[...], end_odd[...])
    for part in range(2):
        ext[part, :half, : cols + 2 * half] = top[part].astype(jnp.float32)
        ext[part, half : half + rows, :half] = left[part].astype(jnp.float32)
        ext[part, half : half + rows, half : half + cols] = tile[part].astype(jnp.float32)
        ext[part, half : half + rows, half + cols : cols + 2 * half] = right[part].astype(jnp.float32)
        ext[part, half + rows : 2 * half + rows, : cols + 2 * half] = bottom[part].astype(jnp.float32)
    tall = size + SUBLANES
    wide = size + LANES

    def slot_step(slot, carry):
        base_row, rest_row, base_col, rest_col = corner_of(
            corners, slot, half, rows + 2 * half - size
        )
        for part in range(2):
            block = ext[part, pl.ds(base_row, tall), pl.ds(base_col, wide)]
            block = pltpu.roll(block, lax.rem(tall - rest_row, tall), 0)[:size]
            block = pltpu.roll(block, lax.rem(wide - rest_col, wide), 1)[:, :size]
            out[slot, part] = block.astype(jnp.bfloat16)
        return carry

    lax.fori_loop(0, out.shape[0], slot_step, 0)
    copy.wait()
    for slot in range(out.shape[0]):
        measured[slot] = jnp.sqrt(held[0, 0, slot].astype(jnp.float32))


def windows_of(row, me, corners, tile, sides, ends, intensity):
    slot_count = intensity.shape[2]
    size = intensity.shape[-1]
    half = sides[0].shape[-1]
    extent = (2, tile.shape[1] + 2 * half + SUBLANES, tile.shape[2] + 2 * half + LANES)
    return call(
        window_kernel,
        [((slot_count, 2, size, size), jnp.bfloat16), ((slot_count, size, size), jnp.float32)],
        (row, SMEM),
        (me, SMEM),
        (corners, SMEM),
        tile,
        *sides,
        *ends,
        (intensity, HBM),
        scratch=[
            pltpu.VMEM(extent, jnp.float32),
            pltpu.VMEM(intensity.shape, intensity.dtype),
            pltpu.SemaphoreType.DMA,
        ],
    )


def dft_kernel(goes_to, comes_from, steps, counts, me, *refs):
    blocks = refs[: len(steps)]
    windows, measured, forward, inverse = refs[len(steps) : len(steps) + 4]
    outs = refs[len(steps) + 4 : 2 * len(steps) + 4]
    placed, probes, terms = refs[2 * len(steps) + 4 :]
    size = windows.shape[-1]
    rows = blocks[0].shape[2]
    starts = [pl.multiple_of(comes_from(me[0], step) * rows, rows) for step in steps]
    targets = [pl.multiple_of(goes_to(me[0], step) * rows, rows) for step in steps]

    def dot(left, right):
        return jnp.dot(left, right, preferred_element_type=jnp.float32)

    for block, start in zip(blocks, starts):
        probes[:, :, pl.ds(start, rows)] = block[...]
    for slot in range(windows.shape[0]):
        probe_re = probes[slot, 0].astype(jnp.float32)
        probe_im = probes[slot, 1].astype(jnp.float32)
        window_re = windows[slot, 0].astype(jnp.float32)
        window_im = windows[slot, 1].astype(jnp.float32)
        leaving = jnp.concatenate(
            [
                (probe_re * window_re - probe_im * window_im).astype(jnp.bfloat16),
                (probe_re * window_im + probe_im * window_re).astype(jnp.bfloat16),
            ],
            axis=0,
        )
        half = dot(forward[...], leaving).astype(jnp.bfloat16)
        far = dot(jnp.concatenate([half[:size], half[size:]], axis=1), inverse[...])
        far_re, far_im = (far[:, :size], far[:, size:])
        power = jnp.maximum(far_re * far_re + far_im * far_im, FLOOR * FLOOR)
        live = jnp.where(slot < counts[0, 0], 1.0, 0.0).astype(jnp.float32)
        factor = (measured[slot] * lax.rsqrt(power) - 1.0) * live
        change = jnp.concatenate(
            [(far_re * factor).astype(jnp.bfloat16), (far_im * factor).astype(jnp.bfloat16)], axis=0
        )
        back = dot(inverse[...], change).astype(jnp.bfloat16)
        update = dot(jnp.concatenate([back[:size], back[size:]], axis=1), forward[...])
        update_re, update_im = (update[:, :size], update[:, size:])
        terms[slot, 0] = (window_re * update_re + window_im * update_im).astype(jnp.bfloat16)
        terms[slot, 1] = (window_re * update_im - window_im * update_re).astype(jnp.bfloat16)
        placed[slot, 0] = probe_re * update_re + probe_im * update_im
        placed[slot, 1] = probe_re * update_im - probe_im * update_re
    for out, start in zip(outs, targets):
        out[...] = terms[:, :, pl.ds(start, rows)]


def place_kernel(half, row, corners, pieces, first, middle, second, accum):
    size = pieces.shape[-1]
    rows = middle.shape[1]
    width = middle.shape[2]
    accum[...] = jnp.zeros_like(accum)
    for slot in range(pieces.shape[0]):
        base_row, rest_row, base_col, rest_col = corner_of(
            corners, slot, half, rows + 2 * half - size
        )
        for part in range(2):
            block = jnp.concatenate(
                [pieces[slot, part], jnp.zeros((size, LANES), jnp.float32)], axis=1
            )
            block = pltpu.roll(block, rest_col, 1)
            block = jnp.concatenate(
                [block, jnp.zeros((SUBLANES, size + LANES), jnp.float32)], axis=0
            )
            block = pltpu.roll(block, rest_row, 0)
            where = (part, pl.ds(base_row, size + SUBLANES), pl.ds(base_col, size + LANES))
            accum[where] += block
    middle[...] = accum[:, half : half + rows, :width]
    top = accum[:, :half, :width].astype(jnp.bfloat16)
    bottom = accum[:, half + rows : 2 * half + rows, :width].astype(jnp.bfloat16)
    first[...], second[...] = by_side(row[0], top, bottom)


def rows_kernel(row, me, middle, even, odd, first, center, second, total):
    half = even.shape[1]
    rows = middle.shape[1]
    cols = center.shape[2]
    got_top, got_bottom = from_sides(row[0], even[...], odd[...])
    total[...] = middle[...]
    total[:, :half] += got_top.astype(jnp.float32)
    total[:, rows - half :] += got_bottom.astype(jnp.float32)
    center[...] = total[:, :, half : half + cols]
    left = total[:, :, :half].astype(jnp.bfloat16)
    right = total[:, :, half + cols :].astype(jnp.bfloat16)
    first[...], second[...] = by_side(me[0], left, right)


def cols_kernel(me, center, even, odd, out):
    half = even.shape[2]
    cols = out.shape[2]
    got_left, got_right = from_sides(me[0], even[...], odd[...])
    out[...] = center[...]
    out[:, :, :half] += got_left.astype(jnp.float32)
    out[:, :, cols - half :] += got_right.astype(jnp.float32)


def sums_kernel(held_in, places, goals, start, num_modes, row, *refs):
    count = len(places)
    received = refs[held_in : held_in + count]
    added = refs[held_in + count : held_in + count + sum(goal[2] for goal in goals)]
    outs = refs[held_in + count + len(added) : -3]
    terms, held, sem = refs[-3:]
    copies = fetch(refs[:held_in], places, held, sem)
    slot_count = received[0].shape[0]
    slots = slot_count
    first = min(goal[1] for goal in goals)
    for at in range(count):
        terms[at, first:] = received[at][first:].astype(jnp.float32)
    for copy in copies:
        copy.wait()

    def mode_step(k, carry):
        rest = list(added)
        for (step, first, adds), out in zip(goals, outs):
            region = (row[0] + step).astype(jnp.float32)
            addend = rest.pop(0) if adds else None
            scales = [
                jnp.where(held[at, slots, slot] == region, held[at, slot, start + k], 0.0)
                for at in range(count)
                for slot in range(first, slot_count)
            ]
            for part in range(2):
                pieces = [
                    terms[at, slot, part] for at in range(count) for slot in range(first, slot_count)
                ]
                total = scales[0] * pieces[0]
                for scale, piece in zip(scales[1:], pieces[1:]):
                    total += scale * piece
                if adds:
                    total += addend[start + k, part].astype(jnp.float32)
                out[k, part] = total.astype(out.dtype)
        return carry

    lax.fori_loop(0, num_modes, mode_step, 0)


def halves(num_modes):
    half = num_modes // 2
    return [(0, half), (half, num_modes - half)] if half else [(0, num_modes)]


def last_kernel(own, *refs):
    out = refs[-1]
    start = 0
    for passed in refs[:-1]:
        modes = pl.ds(start, passed.shape[0])
        out[0, modes] = own[modes] + passed[...].astype(jnp.float32)
        start += passed.shape[0]


def sums(row, goals, weights, places, received, added, modes, dtypes):
    start, num_modes = modes
    shape = (num_modes,) + received[0].shape[1:]
    return call(
        functools.partial(sums_kernel, len(weights), places, goals, start, num_modes),
        [(shape, dtype) for dtype in dtypes],
        (row, SMEM),
        *weights,
        *received,
        *added,
        scratch=[pltpu.VMEM((len(received),) + received[0].shape, jnp.float32)]
        + held_weights(len(places), weights[0]),
    )


def gradients(object_field, modes, coeffs, offsets, region, counts, intensity):
    size = modes.shape[-1]
    half = size // 2
    num_modes = modes.shape[1]
    slot_count = coeffs.shape[2]
    rows, cols = object_field.shape[1:]
    block = (slot_count,) + modes.shape[2:]
    row = lax.axis_index("row").reshape(1)
    me = lax.axis_index("col").reshape(1)
    steps, goes_to, comes_from = partners("col")
    every = [0] + steps
    count = lax.axis_size("col")
    middle_step = count // 2
    near = list(range(1, middle_step))
    crossing = list(range(max(middle_step, 1), count))

    def move(value, step):
        return lax.ppermute(value, "col", [(i, goes_to(i, step)) for i in range(count)])

    side = (2, rows, half)
    low, *edges = call(
        prepare_kernel,
        [(object_field.shape, jnp.bfloat16)] + [(side, jnp.bfloat16)] * 2,
        (me, SMEM),
        (object_field, HBM),
        scratch=[pltpu.VMEM(object_field.shape, object_field.dtype), pltpu.SemaphoreType.DMA],
    )

    def paired(*across):
        return call(
            pair_kernel,
            [((1 + len(across) // 2, slot_count + 1, LANES), jnp.float32)],
            (coeffs, HBM),
            (region, HBM),
            *across,
            scratch=[pltpu.VMEM(x.shape, x.dtype) for x in (coeffs, region)]
            + [pltpu.SemaphoreType.DMA((2,))],
        )[0]

    if count > 1 and count & (count - 1) == 0:
        pair = paired(move(coeffs, middle_step), move(region, middle_step))
        weights = [pair] + [move(pair, step) for step in near]

        def made_at(step):
            return step % middle_step, step // middle_step

        came_at = made_at
    else:
        weights = [paired()]
        weights += [move(weights[0], step) for step in range(1, count)]

        def made_at(step):
            return -step % count, 0

        def came_at(step):
            return step, 0

    follower = shift(modes, "row", -1)

    sides = swap(edges, "col")
    wide = (2, half, cols + 2 * half)
    ends = call(widen_kernel, [(wide, jnp.bfloat16)] * 2, (row, SMEM), (me, SMEM), low, *sides)
    ends = swap(ends, "row")

    blocks = {}
    made = slabs(row, weights, [made_at(step) for step in every], modes, follower)
    for step, slab in zip(every, made):
        blocks[step] = move(slab, step) if step else slab

    corners = pltpu.with_memory_space_constraint(offsets[0, 0].T, pltpu.HBM)
    windows, measured = windows_of(row, me, corners, low, sides, ends, intensity)
    whole = (slot_count, 2, size, size)
    *terms, placed = call(
        functools.partial(dft_kernel, goes_to, comes_from, every),
        [(block, jnp.bfloat16)] * count + [(whole, jnp.float32)],
        (counts, SMEM),
        (me, SMEM),
        *[blocks[step] for step in every],
        windows,
        measured,
        *dft_tables(size),
        scratch=[pltpu.VMEM(whole, jnp.bfloat16)] * 2,
        limit=32,
    )
    terms = dict(zip(every, terms))
    received = {step: move(terms[step], step) if step else terms[step] for step in every}

    extent = (2, rows + 2 * half + SUBLANES, cols + 2 * half + LANES)
    even, middle, odd = call(
        functools.partial(place_kernel, half),
        [(wide, jnp.bfloat16), ((2, rows, cols + 2 * half), jnp.float32), (wide, jnp.bfloat16)],
        (row, SMEM),
        (corners, SMEM),
        placed,
        scratch=[pltpu.VMEM(extent, jnp.float32)],
    )
    over_ends = swap([even, odd], "row")
    even, center, odd = call(
        rows_kernel,
        [(side, jnp.bfloat16), ((2, rows, cols), jnp.float32), (side, jnp.bfloat16)],
        (row, SMEM),
        (me, SMEM),
        middle,
        *over_ends,
        scratch=[pltpu.VMEM((2, rows, cols + 2 * half), jnp.float32)],
    )
    over_sides = swap([even, odd], "col")
    (object_grad,) = call(
        cols_kernel, [(object_field.shape, jnp.float32)], (me, SMEM), center, *over_sides
    )

    def add_up(group, goals, added, modes, dtypes):
        return sums(
            row,
            goals,
            weights,
            [came_at(step) for step in group],
            [received[step] for step in group],
            added,
            modes,
            dtypes,
        )

    everything = (0, num_modes)
    (following,) = add_up([0] + near, ((1, 1, False),), [], everything, [jnp.float32])
    passed = []
    for modes_part in halves(num_modes):
        (part,) = add_up(crossing, ((1, 1, True),), [following], modes_part, [jnp.bfloat16])
        passed.append(shift(part, "row", 1))
    (own,) = add_up(every, ((0, 0, False),), [], everything, [jnp.float32])
    (mode_grad,) = call(last_kernel, [((1,) + own.shape, jnp.float32)], own, *passed)
    return (object_grad, mode_grad)


def solution(mesh):
    in_specs = (
        P(None, "row", "col"),
        P("row", None, None, "col", None),
        P("row", "col", None, None),
        P("row", "col", None, None),
        P("row", "col", None),
        P("row", "col"),
        P("row", "col", None, None, None),
    )
    out_specs = (P(None, "row", "col"), P("row", None, None, "col", None))
    return jax.shard_map(gradients, mesh=mesh, in_specs=in_specs, out_specs=out_specs, check_vma=False)
```

```python
import functools
import math

import jax
import jax.numpy as jnp
import numpy as np
from jax import lax
from jax.experimental import pallas as pl
from jax.experimental.pallas import tpu as pltpu
from jax.sharding import PartitionSpec as P


FLOOR = 0.25
LANES = 128
SUBLANES = 8

VMEM = pl.BlockSpec(memory_space=pltpu.VMEM)
SMEM = pl.BlockSpec(memory_space=pltpu.SMEM)
HBM = pl.BlockSpec(memory_space=pltpu.HBM)


def shift(value, axis, steps):
    count = lax.axis_size(axis)
    leading, last = (max(0, -steps), min(count, count - steps))
    pairs = [(source, source + steps) for source in range(leading, last)]
    return lax.ppermute(value, axis, pairs)


def swap(values, axis):
    count = lax.axis_size(axis)
    got = []
    for odd, value in enumerate(values):
        pairs = []
        for i in range(odd, count - 1, 2):
            pairs += [(i, i + 1), (i + 1, i)]
        got.append(lax.ppermute(value, axis, pairs) if pairs else jnp.zeros_like(value))
    return got


def by_side(index, low, high):
    even = index % 2 == 0
    return jnp.where(even, high, low), jnp.where(even, low, high)


def from_sides(index, first, second):
    high, low = by_side(index, second, first)
    return low, high


def dft_tables(length):
    indices = np.arange(length)
    phases = indices[:, None] * indices[None, :] % length
    angles = phases * (2.0 * math.pi / length)
    scaling = 1.0 / math.sqrt(length)
    re = (np.cos(angles) * scaling).astype(np.float32)
    im = (-np.sin(angles) * scaling).astype(np.float32)
    forward = np.block([[re, -im], [im, re]])
    inverse = np.block([[re, im], [-im, re]])
    return jnp.asarray(forward, jnp.bfloat16), jnp.asarray(inverse, jnp.bfloat16)


def transfer_order(count):
    half = count // 2
    return [half] * (half > 0) + list(range(1, half)) + list(range(half + 1, count))


def slab_order(count, paired):
    steps = transfer_order(count)
    return steps[:1] + [0] + steps[1:] if paired else [0] + steps


def partners(axis):
    count = lax.axis_size(axis)
    steps = transfer_order(count)
    paired = count & (count - 1) == 0

    def goes_to(index, step):
        return index ^ step if paired else (index + step) % count

    def comes_from(index, step):
        return index ^ step if paired else (index - step + count) % count

    return steps, goes_to, comes_from


def call(body, outs, *operands, scratch=(), limit=20):
    arrays = [o[0] if isinstance(o, tuple) else o for o in operands]
    arrays = [
        pltpu.with_memory_space_constraint(a, pltpu.HBM)
        if isinstance(o, tuple) and o[1] is HBM
        else a
        for a, o in zip(arrays, operands)
    ]
    specs = [o[1] if isinstance(o, tuple) else VMEM for o in operands]
    outs = [jax.ShapeDtypeStruct(shape, dtype) for shape, dtype in outs]
    return pl.pallas_call(
        body,
        out_shape=tuple(outs),
        in_specs=specs,
        out_specs=tuple(VMEM for _ in outs),
        scratch_shapes=list(scratch),
        compiler_params=pltpu.CompilerParams(vmem_limit_bytes=limit * 1024 * 1024),
    )(*arrays)


def fetch(arrays, places, held, sem):
    copies = [
        pltpu.make_async_copy(arrays[i].at[block], held.at[at], sem.at[at])
        for at, (i, block) in enumerate(places)
    ]
    for copy in copies:
        copy.start()
    return copies


def held_weights(count, weights):
    shape = (count,) + weights.shape[1:]
    return [pltpu.SMEM(shape, jnp.float32), pltpu.SemaphoreType.DMA((count,))]


def make_slabs(region_of, weight_of, num_modes, row, table, outs):
    next_row = (row[0] + 1).astype(jnp.float32)
    for at, out in enumerate(outs):

        def slot_step(slot, carry, at=at, out=out):
            region = region_of(at, slot)
            which = jnp.where(region == next_row, 1, 0)
            known = jnp.where(jnp.abs(region - next_row + 0.5) < 1.0, 1.0, 0.0)
            scales = [weight_of(at, slot, k) * known for k in range(num_modes)]
            for part in range(2):
                total = scales[0] * table[which, 0, part]
                for k in range(1, num_modes):
                    total += scales[k] * table[which, k, part]
                out[slot, part] = total.astype(jnp.bfloat16)
            return carry

        lax.fori_loop(0, out.shape[0], slot_step, 0)


def first_kernel(places, row, weights, own, follower, out, table, near, held, sem, near_sem):
    copy_own = pltpu.make_async_copy(own, near, near_sem)
    copy_own.start()
    copies = fetch([weights], places, held, sem)
    num_modes, slots = (own.shape[1], out.shape[0])
    table[1] = follower[0].astype(jnp.float32)
    copy_own.wait()
    table[0] = near[0].astype(jnp.float32)
    for copy in copies:
        copy.wait()
    make_slabs(
        lambda at, slot: held[at, slots, slot],
        lambda at, slot, k: held[at, slot, k],
        num_modes,
        row,
        table,
        [out],
    )


def slab_kernel(count, places, row, *refs):
    table = refs[count]
    outs = refs[count + 1 : -2]
    held, sem = refs[-2:]
    slots = outs[0].shape[0]
    for copy in fetch(refs[:count], places, held, sem):
        copy.wait()
    make_slabs(
        lambda at, slot: held[at, slots, slot],
        lambda at, slot, k: held[at, slot, k],
        table.shape[1],
        row,
        table,
        outs,
    )


def slabs(row, weights, places, own, follower):
    shape = (weights[0].shape[1] - 1,) + own.shape[2:]
    first, table = call(
        functools.partial(first_kernel, places[:1]),
        [(shape, jnp.bfloat16), ((2,) + own.shape[1:], jnp.float32)],
        (row, SMEM),
        weights[0],
        (own, HBM),
        follower,
        scratch=[pltpu.VMEM(own.shape, own.dtype)]
        + held_weights(1, weights[0])
        + [pltpu.SemaphoreType.DMA],
    )
    rest = call(
        functools.partial(slab_kernel, len(weights), places[1:]),
        [(shape, jnp.bfloat16)] * (len(places) - 1),
        (row, SMEM),
        *weights,
        table,
        scratch=held_weights(len(places) - 1, weights[0]),
    )
    return [first, *rest]


def prepare_kernel(
    me, coeffs, region, tile, payload, low, even, odd, coeffs_held, region_held, tile_held, sem
):
    slots, num_modes = coeffs.shape[2:]
    half = even.shape[2]
    copies = [
        pltpu.make_async_copy(source, held, sem.at[at])
        for at, (source, held) in enumerate(
            ((coeffs, coeffs_held), (region, region_held), (tile, tile_held))
        )
    ]
    for copy in copies:
        copy.start()
    payload[...] = jnp.zeros_like(payload)
    for copy in copies:
        copy.wait()
    payload[:slots, :num_modes] = coeffs_held[0, 0]
    payload[slots:, :slots] = region_held[0].astype(jnp.float32)
    low[...] = tile_held[...].astype(jnp.bfloat16)
    first, second = by_side(me[0], low[:, :, :half], low[:, :, low.shape[2] - half :])
    even[...] = first
    odd[...] = second


def pair_kernel(mine, across, out):
    out[0] = mine[...]
    out[1] = across[...]


def widen_kernel(row, me, tile, even, odd, first, second):
    half = even.shape[2]
    rows, _ = tile.shape[1:]

    def extended(start):
        left, right = from_sides(
            me[0], even[:, start : start + half], odd[:, start : start + half]
        )
        return jnp.concatenate([left, tile[:, start : start + half], right], axis=2)

    first[...], second[...] = by_side(row[0], extended(0), extended(rows - half))


def corner_of(corners, slot, half, limit):
    row = jnp.clip(corners[0, slot] + half, 0, limit)
    col = jnp.clip(corners[1, slot] + half, 0, limit)
    rest_row, rest_col = (row & (SUBLANES - 1), col & (LANES - 1))
    base_row = pl.multiple_of(row - rest_row, SUBLANES)
    base_col = pl.multiple_of(col - rest_col, LANES)
    return base_row, rest_row, base_col, rest_col


def window_kernel(
    row, me, corners, tile, side_even, side_odd, end_even, end_odd, intensity, out, measured, ext,
    held, sem,
):
    copy = pltpu.make_async_copy(intensity, held, sem)
    copy.start()
    size = out.shape[-1]
    half = side_even.shape[-1]
    rows, cols = tile.shape[1:]
    left, right = from_sides(me[0], side_even[...], side_odd[...])
    top, bottom = from_sides(row[0], end_even[...], end_odd[...])
    for part in range(2):
        ext[part, :half, : cols + 2 * half] = top[part].astype(jnp.float32)
        ext[part, half : half + rows, :half] = left[part].astype(jnp.float32)
        ext[part, half : half + rows, half : half + cols] = tile[part].astype(jnp.float32)
        ext[part, half : half + rows, half + cols : cols + 2 * half] = right[part].astype(jnp.float32)
        ext[part, half + rows : 2 * half + rows, : cols + 2 * half] = bottom[part].astype(jnp.float32)
    tall = size + SUBLANES
    wide = size + LANES

    def slot_step(slot, carry):
        base_row, rest_row, base_col, rest_col = corner_of(
            corners, slot, half, rows + 2 * half - size
        )
        for part in range(2):
            block = ext[part, pl.ds(base_row, tall), pl.ds(base_col, wide)]
            block = pltpu.roll(block, lax.rem(tall - rest_row, tall), 0)[:size]
            block = pltpu.roll(block, lax.rem(wide - rest_col, wide), 1)[:, :size]
            out[slot, part] = block.astype(jnp.bfloat16)
        return carry

    lax.fori_loop(0, out.shape[0], slot_step, 0)
    copy.wait()
    for slot in range(out.shape[0]):
        measured[slot] = jnp.sqrt(held[0, 0, slot].astype(jnp.float32))


def windows_of(row, me, corners, tile, sides, ends, intensity):
    slot_count = intensity.shape[2]
    size = intensity.shape[-1]
    half = sides[0].shape[-1]
    extent = (2, tile.shape[1] + 2 * half + SUBLANES, tile.shape[2] + 2 * half + LANES)
    return call(
        window_kernel,
        [((slot_count, 2, size, size), jnp.bfloat16), ((slot_count, size, size), jnp.float32)],
        (row, SMEM),
        (me, SMEM),
        (corners, SMEM),
        tile,
        *sides,
        *ends,
        (intensity, HBM),
        scratch=[
            pltpu.VMEM(extent, jnp.float32),
            pltpu.VMEM(intensity.shape, intensity.dtype),
            pltpu.SemaphoreType.DMA,
        ],
    )


def dft_kernel(goes_to, comes_from, steps, counts, me, *refs):
    blocks = refs[: len(steps)]
    windows, measured, forward, inverse = refs[len(steps) : len(steps) + 4]
    outs = refs[len(steps) + 4 : 2 * len(steps) + 4]
    placed, probes, terms = refs[2 * len(steps) + 4 :]
    size = windows.shape[-1]
    rows = blocks[0].shape[2]
    starts = [pl.multiple_of(comes_from(me[0], step) * rows, rows) for step in steps]
    targets = [pl.multiple_of(goes_to(me[0], step) * rows, rows) for step in steps]

    def dot(left, right):
        return jnp.dot(left, right, preferred_element_type=jnp.float32)

    for block, start in zip(blocks, starts):
        probes[:, :, pl.ds(start, rows)] = block[...]
    for slot in range(windows.shape[0]):
        probe_re = probes[slot, 0].astype(jnp.float32)
        probe_im = probes[slot, 1].astype(jnp.float32)
        window_re = windows[slot, 0].astype(jnp.float32)
        window_im = windows[slot, 1].astype(jnp.float32)
        leaving = jnp.concatenate(
            [
                (probe_re * window_re - probe_im * window_im).astype(jnp.bfloat16),
                (probe_re * window_im + probe_im * window_re).astype(jnp.bfloat16),
            ],
            axis=0,
        )
        half = dot(forward[...], leaving).astype(jnp.bfloat16)
        far = dot(jnp.concatenate([half[:size], half[size:]], axis=1), inverse[...])
        far_re, far_im = (far[:, :size], far[:, size:])
        power = jnp.maximum(far_re * far_re + far_im * far_im, FLOOR * FLOOR)
        live = jnp.where(slot < counts[0, 0], 1.0, 0.0).astype(jnp.float32)
        factor = (measured[slot] * lax.rsqrt(power) - 1.0) * live
        change = jnp.concatenate(
            [(far_re * factor).astype(jnp.bfloat16), (far_im * factor).astype(jnp.bfloat16)], axis=0
        )
        back = dot(inverse[...], change).astype(jnp.bfloat16)
        update = dot(jnp.concatenate([back[:size], back[size:]], axis=1), forward[...])
        update_re, update_im = (update[:, :size], update[:, size:])
        terms[slot, 0] = (window_re * update_re + window_im * update_im).astype(jnp.bfloat16)
        terms[slot, 1] = (window_re * update_im - window_im * update_re).astype(jnp.bfloat16)
        placed[slot, 0] = probe_re * update_re + probe_im * update_im
        placed[slot, 1] = probe_re * update_im - probe_im * update_re
    for out, start in zip(outs, targets):
        out[...] = terms[:, :, pl.ds(start, rows)]


def place_kernel(half, row, corners, pieces, first, middle, second, accum):
    size = pieces.shape[-1]
    rows = middle.shape[1]
    width = middle.shape[2]
    accum[...] = jnp.zeros_like(accum)
    for slot in range(pieces.shape[0]):
        base_row, rest_row, base_col, rest_col = corner_of(
            corners, slot, half, rows + 2 * half - size
        )
        for part in range(2):
            block = jnp.concatenate(
                [pieces[slot, part], jnp.zeros((size, LANES), jnp.float32)], axis=1
            )
            block = pltpu.roll(block, rest_col, 1)
            block = jnp.concatenate(
                [block, jnp.zeros((SUBLANES, size + LANES), jnp.float32)], axis=0
            )
            block = pltpu.roll(block, rest_row, 0)
            where = (part, pl.ds(base_row, size + SUBLANES), pl.ds(base_col, size + LANES))
            accum[where] += block
    middle[...] = accum[:, half : half + rows, :width]
    top = accum[:, :half, :width].astype(jnp.bfloat16)
    bottom = accum[:, half + rows : 2 * half + rows, :width].astype(jnp.bfloat16)
    first[...], second[...] = by_side(row[0], top, bottom)


def rows_kernel(row, me, middle, even, odd, first, center, second, total):
    half = even.shape[1]
    rows = middle.shape[1]
    cols = center.shape[2]
    got_top, got_bottom = from_sides(row[0], even[...], odd[...])
    total[...] = middle[...]
    total[:, :half] += got_top.astype(jnp.float32)
    total[:, rows - half :] += got_bottom.astype(jnp.float32)
    center[...] = total[:, :, half : half + cols]
    left = total[:, :, :half].astype(jnp.bfloat16)
    right = total[:, :, half + cols :].astype(jnp.bfloat16)
    first[...], second[...] = by_side(me[0], left, right)


def cols_kernel(me, center, even, odd, out):
    half = even.shape[2]
    cols = out.shape[2]
    got_left, got_right = from_sides(me[0], even[...], odd[...])
    out[...] = center[...]
    out[:, :, :half] += got_left.astype(jnp.float32)
    out[:, :, cols - half :] += got_right.astype(jnp.float32)


def sums_kernel(held_in, places, goals, row, *refs):
    count = len(places)
    received = refs[held_in : held_in + count]
    added = refs[held_in + count : held_in + count + sum(goal[2] for goal in goals)]
    outs = refs[held_in + count + len(added) : -3]
    terms, held, sem = refs[-3:]
    copies = fetch(refs[:held_in], places, held, sem)
    num_modes = outs[0].shape[-4]
    slot_count = received[0].shape[0]
    slots = slot_count
    first = min(goal[1] for goal in goals)
    for at in range(count):
        terms[at, first:] = received[at][first:].astype(jnp.float32)
    for copy in copies:
        copy.wait()

    def mode_step(k, carry):
        rest = list(added)
        for (step, first, adds), out in zip(goals, outs):
            region = (row[0] + step).astype(jnp.float32)
            addend = rest.pop(0) if adds else None
            scales = [
                jnp.where(held[at, slots, slot] == region, held[at, slot, k], 0.0)
                for at in range(count)
                for slot in range(first, slot_count)
            ]
            for part in range(2):
                pieces = [
                    terms[at, slot, part] for at in range(count) for slot in range(first, slot_count)
                ]
                total = scales[0] * pieces[0]
                for scale, piece in zip(scales[1:], pieces[1:]):
                    total += scale * piece
                if adds:
                    total += addend[k, part].astype(jnp.float32)
                out[k, part] = total.astype(out.dtype)
        return carry

    lax.fori_loop(0, num_modes, mode_step, 0)


def sums(row, goals, weights, places, received, added, num_modes, dtypes):
    shape = (num_modes,) + received[0].shape[1:]
    return call(
        functools.partial(sums_kernel, len(weights), places, goals),
        [(shape, dtype) for dtype in dtypes],
        (row, SMEM),
        *weights,
        *received,
        *added,
        scratch=[pltpu.VMEM((len(received),) + received[0].shape, jnp.float32)]
        + held_weights(len(places), weights[0]),
    )


def gradients(object_field, modes, coeffs, offsets, region, counts, intensity):
    size = modes.shape[-1]
    half = size // 2
    num_modes = modes.shape[1]
    slot_count = coeffs.shape[2]
    rows, cols = object_field.shape[1:]
    block = (slot_count,) + modes.shape[2:]
    row = lax.axis_index("row").reshape(1)
    me = lax.axis_index("col").reshape(1)
    steps, goes_to, comes_from = partners("col")
    every = [0] + steps
    count = lax.axis_size("col")
    middle_step = count // 2
    near = list(range(1, middle_step))
    crossing = list(range(max(middle_step, 1), count))

    def move(value, step):
        return lax.ppermute(value, "col", [(i, goes_to(i, step)) for i in range(count)])

    side = (2, rows, half)
    payload, low, *edges = call(
        prepare_kernel,
        [((slot_count + 1, LANES), jnp.float32), (object_field.shape, jnp.bfloat16)]
        + [(side, jnp.bfloat16)] * 2,
        (me, SMEM),
        (coeffs, HBM),
        (region, HBM),
        (object_field, HBM),
        scratch=[pltpu.VMEM(x.shape, x.dtype) for x in (coeffs, region, object_field)]
        + [pltpu.SemaphoreType.DMA((3,))],
    )
    paired = count > 1 and count & (count - 1) == 0
    if paired:
        across = move(payload, middle_step)
        blocks_shape = (2,) + payload.shape
        (pair,) = call(pair_kernel, [(blocks_shape, jnp.float32)], payload, across)
        weights = [pair] + [move(pair, step) for step in near]

        def made_at(step):
            return step % middle_step, step // middle_step

        came_at = made_at
    else:
        weights = [payload[None]]
        weights += [move(payload[None], step) for step in range(1, count)]

        def made_at(step):
            return -step % count, 0

        def came_at(step):
            return step, 0

    follower = shift(modes, "row", -1)

    sides = swap(edges, "col")
    wide = (2, half, cols + 2 * half)
    ends = call(widen_kernel, [(wide, jnp.bfloat16)] * 2, (row, SMEM), (me, SMEM), low, *sides)
    ends = swap(ends, "row")

    blocks = {}
    turns = slab_order(count, paired)
    made = slabs(row, weights, [made_at(step) for step in turns], modes, follower)
    for step, slab in zip(turns, made):
        blocks[step] = move(slab, step) if step else slab

    corners = pltpu.with_memory_space_constraint(offsets[0, 0].T, pltpu.HBM)
    windows, measured = windows_of(row, me, corners, low, sides, ends, intensity)
    whole = (slot_count, 2, size, size)
    *terms, placed = call(
        functools.partial(dft_kernel, goes_to, comes_from, every),
        [(block, jnp.bfloat16)] * count + [(whole, jnp.float32)],
        (counts, SMEM),
        (me, SMEM),
        *[blocks[step] for step in every],
        windows,
        measured,
        *dft_tables(size),
        scratch=[pltpu.VMEM(whole, jnp.bfloat16)] * 2,
        limit=32,
    )
    terms = dict(zip(every, terms))
    received = {step: move(terms[step], step) if step else terms[step] for step in every}

    extent = (2, rows + 2 * half + SUBLANES, cols + 2 * half + LANES)
    even, middle, odd = call(
        functools.partial(place_kernel, half),
        [(wide, jnp.bfloat16), ((2, rows, cols + 2 * half), jnp.float32), (wide, jnp.bfloat16)],
        (row, SMEM),
        (corners, SMEM),
        placed,
        scratch=[pltpu.VMEM(extent, jnp.float32)],
    )
    over_ends = swap([even, odd], "row")
    even, center, odd = call(
        rows_kernel,
        [(side, jnp.bfloat16), ((2, rows, cols), jnp.float32), (side, jnp.bfloat16)],
        (row, SMEM),
        (me, SMEM),
        middle,
        *over_ends,
        scratch=[pltpu.VMEM((2, rows, cols + 2 * half), jnp.float32)],
    )
    over_sides = swap([even, odd], "col")
    (object_grad,) = call(
        cols_kernel, [(object_field.shape, jnp.float32)], (me, SMEM), center, *over_sides
    )

    def add_up(group, goals, added, dtypes):
        return sums(
            row,
            goals,
            weights,
            [came_at(step) for step in group],
            [received[step] for step in group],
            added,
            num_modes,
            dtypes,
        )

    own, following = add_up(
        [0] + near, ((0, 0, False), (1, 1, False)), [], [jnp.float32, jnp.float32]
    )
    (following,) = add_up(crossing, ((1, 1, True),), [following], [jnp.bfloat16])
    passed = shift(following, "row", 1)
    (own,) = add_up(crossing, ((0, 0, True),), [own], [jnp.float32])
    mode_grad = (own + passed.astype(jnp.float32))[None]
    return (object_grad, mode_grad)


def solution(mesh):
    in_specs = (
        P(None, "row", "col"),
        P("row", None, None, "col", None),
        P("row", "col", None, None),
        P("row", "col", None, None),
        P("row", "col", None),
        P("row", "col"),
        P("row", "col", None, None, None),
    )
    out_specs = (P(None, "row", "col"), P("row", None, None, "col", None))
    return jax.shard_map(gradients, mesh=mesh, in_specs=in_specs, out_specs=out_specs, check_vma=False)
```

```python
import functools
import math

import jax
import jax.numpy as jnp
import numpy as np
from jax import lax
from jax.experimental import pallas as pl
from jax.experimental.pallas import tpu as pltpu
from jax.sharding import PartitionSpec as P


FLOOR = 0.25
LANES = 128
SUBLANES = 8

VMEM = pl.BlockSpec(memory_space=pltpu.VMEM)
SMEM = pl.BlockSpec(memory_space=pltpu.SMEM)
HBM = pl.BlockSpec(memory_space=pltpu.HBM)


def shift(value, axis, steps):
    count = lax.axis_size(axis)
    leading, last = (max(0, -steps), min(count, count - steps))
    pairs = [(source, source + steps) for source in range(leading, last)]
    return lax.ppermute(value, axis, pairs)


def swap(values, axis):
    count = lax.axis_size(axis)
    got = []
    for odd, value in enumerate(values):
        pairs = []
        for i in range(odd, count - 1, 2):
            pairs += [(i, i + 1), (i + 1, i)]
        got.append(lax.ppermute(value, axis, pairs) if pairs else jnp.zeros_like(value))
    return got


def by_side(index, low, high):
    even = index % 2 == 0
    return jnp.where(even, high, low), jnp.where(even, low, high)


def from_sides(index, first, second):
    high, low = by_side(index, second, first)
    return low, high


def dft_tables(length):
    indices = np.arange(length)
    phases = indices[:, None] * indices[None, :] % length
    angles = phases * (2.0 * math.pi / length)
    scaling = 1.0 / math.sqrt(length)
    re = (np.cos(angles) * scaling).astype(np.float32)
    im = (-np.sin(angles) * scaling).astype(np.float32)
    forward = np.block([[re, -im], [im, re]])
    inverse = np.block([[re, im], [-im, re]])
    return jnp.asarray(forward, jnp.bfloat16), jnp.asarray(inverse, jnp.bfloat16)


def transfer_order(count):
    half = count // 2
    return [half] * (half > 0) + list(range(1, half)) + list(range(half + 1, count))


def slab_order(count, paired):
    steps = transfer_order(count)
    return steps[:1] + [0] + steps[1:] if paired else [0] + steps


def partners(axis):
    count = lax.axis_size(axis)
    steps = transfer_order(count)
    paired = count & (count - 1) == 0

    def goes_to(index, step):
        return index ^ step if paired else (index + step) % count

    def comes_from(index, step):
        return index ^ step if paired else (index - step + count) % count

    return steps, goes_to, comes_from


def call(body, outs, *operands, scratch=(), limit=20):
    arrays = [o[0] if isinstance(o, tuple) else o for o in operands]
    arrays = [
        pltpu.with_memory_space_constraint(a, pltpu.HBM)
        if isinstance(o, tuple) and o[1] is HBM
        else a
        for a, o in zip(arrays, operands)
    ]
    specs = [o[1] if isinstance(o, tuple) else VMEM for o in operands]
    outs = [jax.ShapeDtypeStruct(shape, dtype) for shape, dtype in outs]
    return pl.pallas_call(
        body,
        out_shape=tuple(outs),
        in_specs=specs,
        out_specs=tuple(VMEM for _ in outs),
        scratch_shapes=list(scratch),
        compiler_params=pltpu.CompilerParams(vmem_limit_bytes=limit * 1024 * 1024),
    )(*arrays)


def fetch(arrays, places, held, sem):
    copies = [
        pltpu.make_async_copy(arrays[i].at[block], held.at[at], sem.at[at])
        for at, (i, block) in enumerate(places)
    ]
    for copy in copies:
        copy.start()
    return copies


def held_weights(count, weights):
    shape = (count,) + weights.shape[1:]
    return [pltpu.SMEM(shape, jnp.float32), pltpu.SemaphoreType.DMA((count,))]


def make_slabs(region_of, weight_of, num_modes, row, table, outs):
    next_row = (row[0] + 1).astype(jnp.float32)
    for at, out in enumerate(outs):

        def slot_step(slot, carry, at=at, out=out):
            region = region_of(at, slot)
            which = jnp.where(region == next_row, 1, 0)
            known = jnp.where(jnp.abs(region - next_row + 0.5) < 1.0, 1.0, 0.0)
            scales = [weight_of(at, slot, k) * known for k in range(num_modes)]
            for part in range(2):
                total = scales[0] * table[which, 0, part]
                for k in range(1, num_modes):
                    total += scales[k] * table[which, k, part]
                out[slot, part] = total.astype(jnp.bfloat16)
            return carry

        lax.fori_loop(0, out.shape[0], slot_step, 0)


def first_kernel(places, row, weights, own, follower, out, table, near, held, sem, near_sem):
    copy_own = pltpu.make_async_copy(own, near, near_sem)
    copy_own.start()
    copies = fetch([weights], places, held, sem)
    num_modes, slots = (own.shape[1], out.shape[0])
    table[1] = follower[0].astype(jnp.float32)
    copy_own.wait()
    table[0] = near[0].astype(jnp.float32)
    for copy in copies:
        copy.wait()
    make_slabs(
        lambda at, slot: held[at, slots, slot],
        lambda at, slot, k: held[at, slot, k],
        num_modes,
        row,
        table,
        [out],
    )


def slab_kernel(count, places, row, *refs):
    table = refs[count]
    outs = refs[count + 1 : -2]
    held, sem = refs[-2:]
    slots = outs[0].shape[0]
    for copy in fetch(refs[:count], places, held, sem):
        copy.wait()
    make_slabs(
        lambda at, slot: held[at, slots, slot],
        lambda at, slot, k: held[at, slot, k],
        table.shape[1],
        row,
        table,
        outs,
    )


def slabs(row, weights, places, own, follower):
    shape = (weights[0].shape[1] - 1,) + own.shape[2:]
    first, table = call(
        functools.partial(first_kernel, places[:1]),
        [(shape, jnp.bfloat16), ((2,) + own.shape[1:], jnp.float32)],
        (row, SMEM),
        weights[0],
        (own, HBM),
        follower,
        scratch=[pltpu.VMEM(own.shape, own.dtype)]
        + held_weights(1, weights[0])
        + [pltpu.SemaphoreType.DMA],
    )
    rest = call(
        functools.partial(slab_kernel, len(weights), places[1:]),
        [(shape, jnp.bfloat16)] * (len(places) - 1),
        (row, SMEM),
        *weights,
        table,
        scratch=held_weights(len(places) - 1, weights[0]),
    )
    return [first, *rest]


def prepare_kernel(
    me, coeffs, region, tile, payload, low, even, odd, coeffs_held, region_held, tile_held, sem
):
    slots, num_modes = coeffs.shape[2:]
    half = even.shape[2]
    copies = [
        pltpu.make_async_copy(source, held, sem.at[at])
        for at, (source, held) in enumerate(
            ((coeffs, coeffs_held), (region, region_held), (tile, tile_held))
        )
    ]
    for copy in copies:
        copy.start()
    payload[...] = jnp.zeros_like(payload)
    for copy in copies:
        copy.wait()
    payload[:slots, :num_modes] = coeffs_held[0, 0]
    payload[slots:, :slots] = region_held[0].astype(jnp.float32)
    low[...] = tile_held[...].astype(jnp.bfloat16)
    first, second = by_side(me[0], low[:, :, :half], low[:, :, low.shape[2] - half :])
    even[...] = first
    odd[...] = second


def pair_kernel(mine, across, out):
    out[0] = mine[...]
    out[1] = across[...]


def widen_kernel(row, me, tile, even, odd, first, second):
    half = even.shape[2]
    rows, _ = tile.shape[1:]

    def extended(start):
        left, right = from_sides(
            me[0], even[:, start : start + half], odd[:, start : start + half]
        )
        return jnp.concatenate([left, tile[:, start : start + half], right], axis=2)

    first[...], second[...] = by_side(row[0], extended(0), extended(rows - half))


def corner_of(corners, slot, half, limit):
    row = jnp.clip(corners[0, slot] + half, 0, limit)
    col = jnp.clip(corners[1, slot] + half, 0, limit)
    rest_row, rest_col = (row & (SUBLANES - 1), col & (LANES - 1))
    base_row = pl.multiple_of(row - rest_row, SUBLANES)
    base_col = pl.multiple_of(col - rest_col, LANES)
    return base_row, rest_row, base_col, rest_col


def window_kernel(
    row, me, corners, tile, side_even, side_odd, end_even, end_odd, intensity, out, measured, ext,
    held, sem,
):
    copy = pltpu.make_async_copy(intensity, held, sem)
    copy.start()
    size = out.shape[-1]
    half = side_even.shape[-1]
    rows, cols = tile.shape[1:]
    left, right = from_sides(me[0], side_even[...], side_odd[...])
    top, bottom = from_sides(row[0], end_even[...], end_odd[...])
    for part in range(2):
        ext[part, :half, : cols + 2 * half] = top[part].astype(jnp.float32)
        ext[part, half : half + rows, :half] = left[part].astype(jnp.float32)
        ext[part, half : half + rows, half : half + cols] = tile[part].astype(jnp.float32)
        ext[part, half : half + rows, half + cols : cols + 2 * half] = right[part].astype(jnp.float32)
        ext[part, half + rows : 2 * half + rows, : cols + 2 * half] = bottom[part].astype(jnp.float32)
    tall = size + SUBLANES
    wide = size + LANES

    def slot_step(slot, carry):
        base_row, rest_row, base_col, rest_col = corner_of(
            corners, slot, half, rows + 2 * half - size
        )
        for part in range(2):
            block = ext[part, pl.ds(base_row, tall), pl.ds(base_col, wide)]
            block = pltpu.roll(block, lax.rem(tall - rest_row, tall), 0)[:size]
            block = pltpu.roll(block, lax.rem(wide - rest_col, wide), 1)[:, :size]
            out[slot, part] = block.astype(jnp.bfloat16)
        return carry

    lax.fori_loop(0, out.shape[0], slot_step, 0)
    copy.wait()
    for slot in range(out.shape[0]):
        measured[slot] = jnp.sqrt(held[0, 0, slot].astype(jnp.float32))


def windows_of(row, me, corners, tile, sides, ends, intensity):
    slot_count = intensity.shape[2]
    size = intensity.shape[-1]
    half = sides[0].shape[-1]
    extent = (2, tile.shape[1] + 2 * half + SUBLANES, tile.shape[2] + 2 * half + LANES)
    return call(
        window_kernel,
        [((slot_count, 2, size, size), jnp.bfloat16), ((slot_count, size, size), jnp.float32)],
        (row, SMEM),
        (me, SMEM),
        (corners, SMEM),
        tile,
        *sides,
        *ends,
        (intensity, HBM),
        scratch=[
            pltpu.VMEM(extent, jnp.float32),
            pltpu.VMEM(intensity.shape, intensity.dtype),
            pltpu.SemaphoreType.DMA,
        ],
    )


def dft_kernel(goes_to, comes_from, steps, counts, me, *refs):
    blocks = refs[: len(steps)]
    windows, measured, forward, inverse = refs[len(steps) : len(steps) + 4]
    outs = refs[len(steps) + 4 : 2 * len(steps) + 4]
    placed, probes, terms = refs[2 * len(steps) + 4 :]
    size = windows.shape[-1]
    rows = blocks[0].shape[2]
    starts = [pl.multiple_of(comes_from(me[0], step) * rows, rows) for step in steps]
    targets = [pl.multiple_of(goes_to(me[0], step) * rows, rows) for step in steps]

    def dot(left, right):
        return jnp.dot(left, right, preferred_element_type=jnp.float32)

    for block, start in zip(blocks, starts):
        probes[:, :, pl.ds(start, rows)] = block[...]
    for slot in range(windows.shape[0]):
        probe_re = probes[slot, 0].astype(jnp.float32)
        probe_im = probes[slot, 1].astype(jnp.float32)
        window_re = windows[slot, 0].astype(jnp.float32)
        window_im = windows[slot, 1].astype(jnp.float32)
        leaving = jnp.concatenate(
            [
                (probe_re * window_re - probe_im * window_im).astype(jnp.bfloat16),
                (probe_re * window_im + probe_im * window_re).astype(jnp.bfloat16),
            ],
            axis=0,
        )
        half = dot(forward[...], leaving).astype(jnp.bfloat16)
        far = dot(jnp.concatenate([half[:size], half[size:]], axis=1), inverse[...])
        far_re, far_im = (far[:, :size], far[:, size:])
        power = jnp.maximum(far_re * far_re + far_im * far_im, FLOOR * FLOOR)
        live = jnp.where(slot < counts[0, 0], 1.0, 0.0).astype(jnp.float32)
        factor = (measured[slot] * lax.rsqrt(power) - 1.0) * live
        change = jnp.concatenate(
            [(far_re * factor).astype(jnp.bfloat16), (far_im * factor).astype(jnp.bfloat16)], axis=0
        )
        back = dot(inverse[...], change).astype(jnp.bfloat16)
        update = dot(jnp.concatenate([back[:size], back[size:]], axis=1), forward[...])
        update_re, update_im = (update[:, :size], update[:, size:])
        terms[slot, 0] = (window_re * update_re + window_im * update_im).astype(jnp.bfloat16)
        terms[slot, 1] = (window_re * update_im - window_im * update_re).astype(jnp.bfloat16)
        placed[slot, 0] = probe_re * update_re + probe_im * update_im
        placed[slot, 1] = probe_re * update_im - probe_im * update_re
    for out, start in zip(outs, targets):
        out[...] = terms[:, :, pl.ds(start, rows)]


def place_kernel(half, row, corners, pieces, first, middle, second, accum):
    size = pieces.shape[-1]
    rows = middle.shape[1]
    width = middle.shape[2]
    accum[...] = jnp.zeros_like(accum)
    for slot in range(pieces.shape[0]):
        base_row, rest_row, base_col, rest_col = corner_of(
            corners, slot, half, rows + 2 * half - size
        )
        for part in range(2):
            block = jnp.concatenate(
                [pieces[slot, part], jnp.zeros((size, LANES), jnp.float32)], axis=1
            )
            block = pltpu.roll(block, rest_col, 1)
            block = jnp.concatenate(
                [block, jnp.zeros((SUBLANES, size + LANES), jnp.float32)], axis=0
            )
            block = pltpu.roll(block, rest_row, 0)
            where = (part, pl.ds(base_row, size + SUBLANES), pl.ds(base_col, size + LANES))
            accum[where] += block
    middle[...] = accum[:, half : half + rows, :width]
    top = accum[:, :half, :width].astype(jnp.bfloat16)
    bottom = accum[:, half + rows : 2 * half + rows, :width].astype(jnp.bfloat16)
    first[...], second[...] = by_side(row[0], top, bottom)


def rows_kernel(row, me, middle, even, odd, first, center, second, total):
    half = even.shape[1]
    rows = middle.shape[1]
    cols = center.shape[2]
    got_top, got_bottom = from_sides(row[0], even[...], odd[...])
    total[...] = middle[...]
    total[:, :half] += got_top.astype(jnp.float32)
    total[:, rows - half :] += got_bottom.astype(jnp.float32)
    center[...] = total[:, :, half : half + cols]
    left = total[:, :, :half].astype(jnp.bfloat16)
    right = total[:, :, half + cols :].astype(jnp.bfloat16)
    first[...], second[...] = by_side(me[0], left, right)


def cols_kernel(me, center, even, odd, out):
    half = even.shape[2]
    cols = out.shape[2]
    got_left, got_right = from_sides(me[0], even[...], odd[...])
    out[...] = center[...]
    out[:, :, :half] += got_left.astype(jnp.float32)
    out[:, :, cols - half :] += got_right.astype(jnp.float32)


def sums_kernel(held_in, places, goals, row, *refs):
    count = len(places)
    received = refs[held_in : held_in + count]
    added = refs[held_in + count : held_in + count + sum(goal[2] for goal in goals)]
    outs = refs[held_in + count + len(added) : -3]
    terms, held, sem = refs[-3:]
    copies = fetch(refs[:held_in], places, held, sem)
    num_modes = outs[0].shape[-4]
    slot_count = received[0].shape[0]
    slots = slot_count
    first = min(goal[1] for goal in goals)
    for at in range(count):
        terms[at, first:] = received[at][first:].astype(jnp.float32)
    for copy in copies:
        copy.wait()

    def mode_step(k, carry):
        rest = list(added)
        for (step, first, adds), out in zip(goals, outs):
            region = (row[0] + step).astype(jnp.float32)
            addend = rest.pop(0) if adds else None
            scales = [
                jnp.where(held[at, slots, slot] == region, held[at, slot, k], 0.0)
                for at in range(count)
                for slot in range(first, slot_count)
            ]
            for part in range(2):
                pieces = [
                    terms[at, slot, part] for at in range(count) for slot in range(first, slot_count)
                ]
                total = scales[0] * pieces[0]
                for scale, piece in zip(scales[1:], pieces[1:]):
                    total += scale * piece
                if adds:
                    total += addend[k, part].astype(jnp.float32)
                out[k, part] = total.astype(out.dtype)
        return carry

    lax.fori_loop(0, num_modes, mode_step, 0)


def sums(row, goals, weights, places, received, added, num_modes, dtypes):
    shape = (num_modes,) + received[0].shape[1:]
    return call(
        functools.partial(sums_kernel, len(weights), places, goals),
        [(shape, dtype) for dtype in dtypes],
        (row, SMEM),
        *weights,
        *received,
        *added,
        scratch=[pltpu.VMEM((len(received),) + received[0].shape, jnp.float32)]
        + held_weights(len(places), weights[0]),
    )


def gradients(object_field, modes, coeffs, offsets, region, counts, intensity):
    size = modes.shape[-1]
    half = size // 2
    num_modes = modes.shape[1]
    slot_count = coeffs.shape[2]
    rows, cols = object_field.shape[1:]
    block = (slot_count,) + modes.shape[2:]
    row = lax.axis_index("row").reshape(1)
    me = lax.axis_index("col").reshape(1)
    steps, goes_to, comes_from = partners("col")
    every = [0] + steps
    count = lax.axis_size("col")
    middle_step = count // 2
    near = list(range(1, middle_step))
    crossing = list(range(max(middle_step, 1), count))

    def move(value, step):
        return lax.ppermute(value, "col", [(i, goes_to(i, step)) for i in range(count)])

    side = (2, rows, half)
    payload, low, *edges = call(
        prepare_kernel,
        [((slot_count + 1, LANES), jnp.float32), (object_field.shape, jnp.bfloat16)]
        + [(side, jnp.bfloat16)] * 2,
        (me, SMEM),
        (coeffs, HBM),
        (region, HBM),
        (object_field, HBM),
        scratch=[pltpu.VMEM(x.shape, x.dtype) for x in (coeffs, region, object_field)]
        + [pltpu.SemaphoreType.DMA((3,))],
    )
    paired = count > 1 and count & (count - 1) == 0
    if paired:
        across = move(payload, middle_step)
        blocks_shape = (2,) + payload.shape
        (pair,) = call(pair_kernel, [(blocks_shape, jnp.float32)], payload, across)
        weights = [pair] + [move(pair, step) for step in near]

        def made_at(step):
            return step % middle_step, step // middle_step

        came_at = made_at
    else:
        weights = [payload[None]]
        weights += [move(payload[None], step) for step in range(1, count)]

        def made_at(step):
            return -step % count, 0

        def came_at(step):
            return step, 0

    follower = shift(modes, "row", -1)

    sides = swap(edges, "col")
    wide = (2, half, cols + 2 * half)
    ends = call(widen_kernel, [(wide, jnp.bfloat16)] * 2, (row, SMEM), (me, SMEM), low, *sides)
    ends = swap(ends, "row")

    blocks = {}
    turns = slab_order(count, paired)
    made = slabs(row, weights, [made_at(step) for step in turns], modes, follower)
    for step, slab in zip(turns, made):
        blocks[step] = move(slab, step) if step else slab

    corners = pltpu.with_memory_space_constraint(offsets[0, 0].T, pltpu.HBM)
    windows, measured = windows_of(row, me, corners, low, sides, ends, intensity)
    whole = (slot_count, 2, size, size)
    *terms, placed = call(
        functools.partial(dft_kernel, goes_to, comes_from, every),
        [(block, jnp.bfloat16)] * count + [(whole, jnp.float32)],
        (counts, SMEM),
        (me, SMEM),
        *[blocks[step] for step in every],
        windows,
        measured,
        *dft_tables(size),
        scratch=[pltpu.VMEM(whole, jnp.bfloat16)] * 2,
        limit=32,
    )
    terms = dict(zip(every, terms))
    received = {step: move(terms[step], step) if step else terms[step] for step in every}

    extent = (2, rows + 2 * half + SUBLANES, cols + 2 * half + LANES)
    even, middle, odd = call(
        functools.partial(place_kernel, half),
        [(wide, jnp.bfloat16), ((2, rows, cols + 2 * half), jnp.float32), (wide, jnp.bfloat16)],
        (row, SMEM),
        (corners, SMEM),
        placed,
        scratch=[pltpu.VMEM(extent, jnp.float32)],
    )
    over_ends = swap([even, odd], "row")
    even, center, odd = call(
        rows_kernel,
        [(side, jnp.bfloat16), ((2, rows, cols), jnp.float32), (side, jnp.bfloat16)],
        (row, SMEM),
        (me, SMEM),
        middle,
        *over_ends,
        scratch=[pltpu.VMEM((2, rows, cols + 2 * half), jnp.float32)],
    )
    over_sides = swap([even, odd], "col")
    (object_grad,) = call(
        cols_kernel, [(object_field.shape, jnp.float32)], (me, SMEM), center, *over_sides
    )

    def add_up(group, goals, added, dtypes):
        return sums(
            row,
            goals,
            weights,
            [came_at(step) for step in group],
            [received[step] for step in group],
            added,
            num_modes,
            dtypes,
        )

    (following,) = add_up([0] + near, ((1, 1, False),), [], [jnp.float32])
    (following,) = add_up(crossing, ((1, 1, True),), [following], [jnp.bfloat16])
    passed = shift(following, "row", 1)
    (own,) = add_up(every, ((0, 0, False),), [], [jnp.float32])
    mode_grad = (own + passed.astype(jnp.float32))[None]
    return (object_grad, mode_grad)


def solution(mesh):
    in_specs = (
        P(None, "row", "col"),
        P("row", None, None, "col", None),
        P("row", "col", None, None),
        P("row", "col", None, None),
        P("row", "col", None),
        P("row", "col"),
        P("row", "col", None, None, None),
    )
    out_specs = (P(None, "row", "col"), P("row", None, None, "col", None))
    return jax.shard_map(gradients, mesh=mesh, in_specs=in_specs, out_specs=out_specs, check_vma=False)
```

```python
import functools
import math

import jax
import jax.numpy as jnp
import numpy as np
from jax import lax
from jax.experimental import pallas as pl
from jax.experimental.pallas import tpu as pltpu
from jax.sharding import PartitionSpec as P


FLOOR = 0.25
LANES = 128
SUBLANES = 8

VMEM = pl.BlockSpec(memory_space=pltpu.VMEM)
SMEM = pl.BlockSpec(memory_space=pltpu.SMEM)
HBM = pl.BlockSpec(memory_space=pltpu.HBM)


def shift(value, axis, steps):
    count = lax.axis_size(axis)
    leading, last = (max(0, -steps), min(count, count - steps))
    pairs = [(source, source + steps) for source in range(leading, last)]
    return lax.ppermute(value, axis, pairs)


def swap(values, axis):
    count = lax.axis_size(axis)
    got = []
    for odd, value in enumerate(values):
        pairs = []
        for i in range(odd, count - 1, 2):
            pairs += [(i, i + 1), (i + 1, i)]
        got.append(lax.ppermute(value, axis, pairs) if pairs else jnp.zeros_like(value))
    return got


def by_side(index, low, high):
    even = index % 2 == 0
    return jnp.where(even, high, low), jnp.where(even, low, high)


def from_sides(index, first, second):
    high, low = by_side(index, second, first)
    return low, high


def dft_tables(length):
    indices = np.arange(length)
    phases = indices[:, None] * indices[None, :] % length
    angles = phases * (2.0 * math.pi / length)
    scaling = 1.0 / math.sqrt(length)
    re = (np.cos(angles) * scaling).astype(np.float32)
    im = (-np.sin(angles) * scaling).astype(np.float32)
    forward = np.block([[re, -im], [im, re]])
    inverse = np.block([[re, im], [-im, re]])
    return jnp.asarray(forward, jnp.bfloat16), jnp.asarray(inverse, jnp.bfloat16)


def transfer_order(count):
    half = count // 2
    return [half] * (half > 0) + list(range(1, half)) + list(range(half + 1, count))


def slab_order(count, paired):
    steps = transfer_order(count)
    return steps[:1] + [0] + steps[1:] if paired else [0] + steps


def partners(axis):
    count = lax.axis_size(axis)
    steps = transfer_order(count)
    paired = count & (count - 1) == 0

    def goes_to(index, step):
        return index ^ step if paired else (index + step) % count

    def comes_from(index, step):
        return index ^ step if paired else (index - step + count) % count

    return steps, goes_to, comes_from


def call(body, outs, *operands, scratch=(), limit=20):
    arrays = [o[0] if isinstance(o, tuple) else o for o in operands]
    arrays = [
        pltpu.with_memory_space_constraint(a, pltpu.HBM)
        if isinstance(o, tuple) and o[1] is HBM
        else a
        for a, o in zip(arrays, operands)
    ]
    specs = [o[1] if isinstance(o, tuple) else VMEM for o in operands]
    outs = [jax.ShapeDtypeStruct(shape, dtype) for shape, dtype in outs]
    return pl.pallas_call(
        body,
        out_shape=tuple(outs),
        in_specs=specs,
        out_specs=tuple(VMEM for _ in outs),
        scratch_shapes=list(scratch),
        compiler_params=pltpu.CompilerParams(vmem_limit_bytes=limit * 1024 * 1024),
    )(*arrays)


def fetch(arrays, places, held, sem):
    copies = [
        pltpu.make_async_copy(arrays[i].at[block], held.at[at], sem.at[at])
        for at, (i, block) in enumerate(places)
    ]
    for copy in copies:
        copy.start()
    return copies


def held_weights(count, weights):
    shape = (count,) + weights.shape[1:]
    return [pltpu.SMEM(shape, jnp.float32), pltpu.SemaphoreType.DMA((count,))]


def make_slabs(region_of, weight_of, num_modes, row, table, outs):
    next_row = (row[0] + 1).astype(jnp.float32)
    for at, out in enumerate(outs):

        def slot_step(slot, carry, at=at, out=out):
            region = region_of(at, slot)
            which = jnp.where(region == next_row, 1, 0)
            known = jnp.where(jnp.abs(region - next_row + 0.5) < 1.0, 1.0, 0.0)
            scales = [weight_of(at, slot, k) * known for k in range(num_modes)]
            for part in range(2):
                total = scales[0] * table[which, 0, part]
                for k in range(1, num_modes):
                    total += scales[k] * table[which, k, part]
                out[slot, part] = total.astype(jnp.bfloat16)
            return carry

        lax.fori_loop(0, out.shape[0], slot_step, 0)


def first_kernel(places, row, weights, own, follower, out, table, near, held, sem, near_sem):
    copy_own = pltpu.make_async_copy(own, near, near_sem)
    copy_own.start()
    copies = fetch([weights], places, held, sem)
    num_modes, slots = (own.shape[1], out.shape[0])
    table[1] = follower[0].astype(jnp.float32)
    copy_own.wait()
    table[0] = near[0].astype(jnp.float32)
    for copy in copies:
        copy.wait()
    make_slabs(
        lambda at, slot: held[at, slots, slot],
        lambda at, slot, k: held[at, slot, k],
        num_modes,
        row,
        table,
        [out],
    )


def slab_kernel(count, places, row, *refs):
    table = refs[count]
    outs = refs[count + 1 : -2]
    held, sem = refs[-2:]
    slots = outs[0].shape[0]
    for copy in fetch(refs[:count], places, held, sem):
        copy.wait()
    make_slabs(
        lambda at, slot: held[at, slots, slot],
        lambda at, slot, k: held[at, slot, k],
        table.shape[1],
        row,
        table,
        outs,
    )


def slabs(row, weights, places, own, follower):
    shape = (weights[0].shape[1] - 1,) + own.shape[2:]
    first, table = call(
        functools.partial(first_kernel, places[:1]),
        [(shape, jnp.bfloat16), ((2,) + own.shape[1:], jnp.float32)],
        (row, SMEM),
        weights[0],
        (own, HBM),
        follower,
        scratch=[pltpu.VMEM(own.shape, own.dtype)]
        + held_weights(1, weights[0])
        + [pltpu.SemaphoreType.DMA],
    )
    rest = call(
        functools.partial(slab_kernel, len(weights), places[1:]),
        [(shape, jnp.bfloat16)] * (len(places) - 1),
        (row, SMEM),
        *weights,
        table,
        scratch=held_weights(len(places) - 1, weights[0]),
    )
    return [first, *rest]


def prepare_kernel(
    me, coeffs, region, tile, payload, low, even, odd, coeffs_held, region_held, tile_held, sem
):
    slots, num_modes = coeffs.shape[2:]
    half = even.shape[2]
    copies = [
        pltpu.make_async_copy(source, held, sem.at[at])
        for at, (source, held) in enumerate(
            ((coeffs, coeffs_held), (region, region_held), (tile, tile_held))
        )
    ]
    for copy in copies:
        copy.start()
    payload[...] = jnp.zeros_like(payload)
    for copy in copies:
        copy.wait()
    payload[:slots, :num_modes] = coeffs_held[0, 0]
    payload[slots:, :slots] = region_held[0].astype(jnp.float32)
    low[...] = tile_held[...].astype(jnp.bfloat16)
    first, second = by_side(me[0], low[:, :, :half], low[:, :, low.shape[2] - half :])
    even[...] = first
    odd[...] = second


def pair_kernel(mine, across, out):
    out[0] = mine[...]
    out[1] = across[...]


def widen_kernel(row, me, tile, even, odd, first, second):
    half = even.shape[2]
    rows, _ = tile.shape[1:]

    def extended(start):
        left, right = from_sides(
            me[0], even[:, start : start + half], odd[:, start : start + half]
        )
        return jnp.concatenate([left, tile[:, start : start + half], right], axis=2)

    first[...], second[...] = by_side(row[0], extended(0), extended(rows - half))


def corner_of(corners, slot, half, limit):
    row = jnp.clip(corners[0, slot] + half, 0, limit)
    col = jnp.clip(corners[1, slot] + half, 0, limit)
    rest_row, rest_col = (row & (SUBLANES - 1), col & (LANES - 1))
    base_row = pl.multiple_of(row - rest_row, SUBLANES)
    base_col = pl.multiple_of(col - rest_col, LANES)
    return base_row, rest_row, base_col, rest_col


def window_kernel(
    row, me, corners, tile, side_even, side_odd, end_even, end_odd, intensity, out, measured, ext,
    held, sem,
):
    copy = pltpu.make_async_copy(intensity, held, sem)
    copy.start()
    size = out.shape[-1]
    half = side_even.shape[-1]
    rows, cols = tile.shape[1:]
    left, right = from_sides(me[0], side_even[...], side_odd[...])
    top, bottom = from_sides(row[0], end_even[...], end_odd[...])
    for part in range(2):
        ext[part, :half, : cols + 2 * half] = top[part].astype(jnp.float32)
        ext[part, half : half + rows, :half] = left[part].astype(jnp.float32)
        ext[part, half : half + rows, half : half + cols] = tile[part].astype(jnp.float32)
        ext[part, half : half + rows, half + cols : cols + 2 * half] = right[part].astype(jnp.float32)
        ext[part, half + rows : 2 * half + rows, : cols + 2 * half] = bottom[part].astype(jnp.float32)
    tall = size + SUBLANES
    wide = size + LANES

    def slot_step(slot, carry):
        base_row, rest_row, base_col, rest_col = corner_of(
            corners, slot, half, rows + 2 * half - size
        )
        for part in range(2):
            block = ext[part, pl.ds(base_row, tall), pl.ds(base_col, wide)]
            block = pltpu.roll(block, lax.rem(tall - rest_row, tall), 0)[:size]
            block = pltpu.roll(block, lax.rem(wide - rest_col, wide), 1)[:, :size]
            out[slot, part] = block.astype(jnp.bfloat16)
        return carry

    lax.fori_loop(0, out.shape[0], slot_step, 0)
    copy.wait()
    for slot in range(out.shape[0]):
        measured[slot] = jnp.sqrt(held[0, 0, slot].astype(jnp.float32))


def windows_of(row, me, corners, tile, sides, ends, intensity):
    slot_count = intensity.shape[2]
    size = intensity.shape[-1]
    half = sides[0].shape[-1]
    extent = (2, tile.shape[1] + 2 * half + SUBLANES, tile.shape[2] + 2 * half + LANES)
    return call(
        window_kernel,
        [((slot_count, 2, size, size), jnp.bfloat16), ((slot_count, size, size), jnp.float32)],
        (row, SMEM),
        (me, SMEM),
        (corners, SMEM),
        tile,
        *sides,
        *ends,
        (intensity, HBM),
        scratch=[
            pltpu.VMEM(extent, jnp.float32),
            pltpu.VMEM(intensity.shape, intensity.dtype),
            pltpu.SemaphoreType.DMA,
        ],
    )


def dft_kernel(goes_to, comes_from, steps, counts, me, *refs):
    blocks = refs[: len(steps)]
    windows, measured, forward, inverse = refs[len(steps) : len(steps) + 4]
    outs = refs[len(steps) + 4 : 2 * len(steps) + 4]
    placed, probes, terms = refs[2 * len(steps) + 4 :]
    size = windows.shape[-1]
    rows = blocks[0].shape[2]
    starts = [pl.multiple_of(comes_from(me[0], step) * rows, rows) for step in steps]
    targets = [pl.multiple_of(goes_to(me[0], step) * rows, rows) for step in steps]

    def dot(left, right):
        return jnp.dot(left, right, preferred_element_type=jnp.float32)

    for block, start in zip(blocks, starts):
        probes[:, :, pl.ds(start, rows)] = block[...]
    slots = range(windows.shape[0])

    def held(ref, slot):
        return ref[slot, 0].astype(jnp.float32), ref[slot, 1].astype(jnp.float32)

    def stacked(re, im):
        return jnp.concatenate([re.astype(jnp.bfloat16), im.astype(jnp.bfloat16)], axis=0)

    def beside(products):
        columns = [products[:, slot * size : (slot + 1) * size] for slot in slots]
        turned = [jnp.concatenate([c[:size], c[size:]], axis=1) for c in columns]
        return jnp.concatenate(turned, axis=0)

    def parts(products, slot):
        block = products[slot * size : (slot + 1) * size]
        return block[:, :size], block[:, size:]

    leaving = []
    for slot in slots:
        probe_re, probe_im = held(probes, slot)
        window_re, window_im = held(windows, slot)
        leaving.append(
            stacked(
                probe_re * window_re - probe_im * window_im,
                probe_re * window_im + probe_im * window_re,
            )
        )
    half = dot(forward[...], jnp.concatenate(leaving, axis=1)).astype(jnp.bfloat16)
    far = dot(beside(half), inverse[...])
    changes = []
    for slot in slots:
        far_re, far_im = parts(far, slot)
        power = jnp.maximum(far_re * far_re + far_im * far_im, FLOOR * FLOOR)
        live = jnp.where(slot < counts[0, 0], 1.0, 0.0).astype(jnp.float32)
        factor = (measured[slot] * lax.rsqrt(power) - 1.0) * live
        changes.append(stacked(far_re * factor, far_im * factor))
    back = dot(inverse[...], jnp.concatenate(changes, axis=1)).astype(jnp.bfloat16)
    update = dot(beside(back), forward[...])
    for slot in slots:
        update_re, update_im = parts(update, slot)
        probe_re, probe_im = held(probes, slot)
        window_re, window_im = held(windows, slot)
        terms[slot, 0] = (window_re * update_re + window_im * update_im).astype(jnp.bfloat16)
        terms[slot, 1] = (window_re * update_im - window_im * update_re).astype(jnp.bfloat16)
        placed[slot, 0] = probe_re * update_re + probe_im * update_im
        placed[slot, 1] = probe_re * update_im - probe_im * update_re
    for out, start in zip(outs, targets):
        out[...] = terms[:, :, pl.ds(start, rows)]


def place_kernel(half, row, corners, pieces, first, middle, second, accum):
    size = pieces.shape[-1]
    rows = middle.shape[1]
    width = middle.shape[2]
    accum[...] = jnp.zeros_like(accum)
    for slot in range(pieces.shape[0]):
        base_row, rest_row, base_col, rest_col = corner_of(
            corners, slot, half, rows + 2 * half - size
        )
        for part in range(2):
            block = jnp.concatenate(
                [pieces[slot, part], jnp.zeros((size, LANES), jnp.float32)], axis=1
            )
            block = pltpu.roll(block, rest_col, 1)
            block = jnp.concatenate(
                [block, jnp.zeros((SUBLANES, size + LANES), jnp.float32)], axis=0
            )
            block = pltpu.roll(block, rest_row, 0)
            where = (part, pl.ds(base_row, size + SUBLANES), pl.ds(base_col, size + LANES))
            accum[where] += block
    middle[...] = accum[:, half : half + rows, :width]
    top = accum[:, :half, :width].astype(jnp.bfloat16)
    bottom = accum[:, half + rows : 2 * half + rows, :width].astype(jnp.bfloat16)
    first[...], second[...] = by_side(row[0], top, bottom)


def rows_kernel(row, me, middle, even, odd, first, center, second, total):
    half = even.shape[1]
    rows = middle.shape[1]
    cols = center.shape[2]
    got_top, got_bottom = from_sides(row[0], even[...], odd[...])
    total[...] = middle[...]
    total[:, :half] += got_top.astype(jnp.float32)
    total[:, rows - half :] += got_bottom.astype(jnp.float32)
    center[...] = total[:, :, half : half + cols]
    left = total[:, :, :half].astype(jnp.bfloat16)
    right = total[:, :, half + cols :].astype(jnp.bfloat16)
    first[...], second[...] = by_side(me[0], left, right)


def cols_kernel(me, center, even, odd, out):
    half = even.shape[2]
    cols = out.shape[2]
    got_left, got_right = from_sides(me[0], even[...], odd[...])
    out[...] = center[...]
    out[:, :, :half] += got_left.astype(jnp.float32)
    out[:, :, cols - half :] += got_right.astype(jnp.float32)


def sums_kernel(held_in, places, goals, row, *refs):
    count = len(places)
    received = refs[held_in : held_in + count]
    added = refs[held_in + count : held_in + count + sum(goal[2] for goal in goals)]
    outs = refs[held_in + count + len(added) : -3]
    terms, held, sem = refs[-3:]
    copies = fetch(refs[:held_in], places, held, sem)
    num_modes = outs[0].shape[-4]
    slot_count = received[0].shape[0]
    slots = slot_count
    first = min(goal[1] for goal in goals)
    for at in range(count):
        terms[at, first:] = received[at][first:].astype(jnp.float32)
    for copy in copies:
        copy.wait()

    def mode_step(k, carry):
        rest = list(added)
        for (step, first, adds), out in zip(goals, outs):
            region = (row[0] + step).astype(jnp.float32)
            addend = rest.pop(0) if adds else None
            scales = [
                jnp.where(held[at, slots, slot] == region, held[at, slot, k], 0.0)
                for at in range(count)
                for slot in range(first, slot_count)
            ]
            for part in range(2):
                pieces = [
                    terms[at, slot, part] for at in range(count) for slot in range(first, slot_count)
                ]
                total = scales[0] * pieces[0]
                for scale, piece in zip(scales[1:], pieces[1:]):
                    total += scale * piece
                if adds:
                    total += addend[k, part].astype(jnp.float32)
                out[k, part] = total.astype(out.dtype)
        return carry

    lax.fori_loop(0, num_modes, mode_step, 0)


def sums(row, goals, weights, places, received, added, num_modes, dtypes):
    shape = (num_modes,) + received[0].shape[1:]
    return call(
        functools.partial(sums_kernel, len(weights), places, goals),
        [(shape, dtype) for dtype in dtypes],
        (row, SMEM),
        *weights,
        *received,
        *added,
        scratch=[pltpu.VMEM((len(received),) + received[0].shape, jnp.float32)]
        + held_weights(len(places), weights[0]),
    )


def gradients(object_field, modes, coeffs, offsets, region, counts, intensity):
    size = modes.shape[-1]
    half = size // 2
    num_modes = modes.shape[1]
    slot_count = coeffs.shape[2]
    rows, cols = object_field.shape[1:]
    block = (slot_count,) + modes.shape[2:]
    row = lax.axis_index("row").reshape(1)
    me = lax.axis_index("col").reshape(1)
    steps, goes_to, comes_from = partners("col")
    every = [0] + steps
    count = lax.axis_size("col")
    middle_step = count // 2
    near = list(range(1, middle_step))
    crossing = list(range(max(middle_step, 1), count))

    def move(value, step):
        return lax.ppermute(value, "col", [(i, goes_to(i, step)) for i in range(count)])

    side = (2, rows, half)
    payload, low, *edges = call(
        prepare_kernel,
        [((slot_count + 1, LANES), jnp.float32), (object_field.shape, jnp.bfloat16)]
        + [(side, jnp.bfloat16)] * 2,
        (me, SMEM),
        (coeffs, HBM),
        (region, HBM),
        (object_field, HBM),
        scratch=[pltpu.VMEM(x.shape, x.dtype) for x in (coeffs, region, object_field)]
        + [pltpu.SemaphoreType.DMA((3,))],
    )
    paired = count > 1 and count & (count - 1) == 0
    if paired:
        across = move(payload, middle_step)
        blocks_shape = (2,) + payload.shape
        (pair,) = call(pair_kernel, [(blocks_shape, jnp.float32)], payload, across)
        weights = [pair] + [move(pair, step) for step in near]

        def made_at(step):
            return step % middle_step, step // middle_step

        came_at = made_at
    else:
        weights = [payload[None]]
        weights += [move(payload[None], step) for step in range(1, count)]

        def made_at(step):
            return -step % count, 0

        def came_at(step):
            return step, 0

    follower = shift(modes, "row", -1)

    sides = swap(edges, "col")
    wide = (2, half, cols + 2 * half)
    ends = call(widen_kernel, [(wide, jnp.bfloat16)] * 2, (row, SMEM), (me, SMEM), low, *sides)
    ends = swap(ends, "row")

    blocks = {}
    turns = slab_order(count, paired)
    made = slabs(row, weights, [made_at(step) for step in turns], modes, follower)
    for step, slab in zip(turns, made):
        blocks[step] = move(slab, step) if step else slab

    corners = pltpu.with_memory_space_constraint(offsets[0, 0].T, pltpu.HBM)
    windows, measured = windows_of(row, me, corners, low, sides, ends, intensity)
    whole = (slot_count, 2, size, size)
    *terms, placed = call(
        functools.partial(dft_kernel, goes_to, comes_from, every),
        [(block, jnp.bfloat16)] * count + [(whole, jnp.float32)],
        (counts, SMEM),
        (me, SMEM),
        *[blocks[step] for step in every],
        windows,
        measured,
        *dft_tables(size),
        scratch=[pltpu.VMEM(whole, jnp.bfloat16)] * 2,
        limit=32,
    )
    terms = dict(zip(every, terms))
    received = {step: move(terms[step], step) if step else terms[step] for step in every}

    extent = (2, rows + 2 * half + SUBLANES, cols + 2 * half + LANES)
    even, middle, odd = call(
        functools.partial(place_kernel, half),
        [(wide, jnp.bfloat16), ((2, rows, cols + 2 * half), jnp.float32), (wide, jnp.bfloat16)],
        (row, SMEM),
        (corners, SMEM),
        placed,
        scratch=[pltpu.VMEM(extent, jnp.float32)],
    )
    over_ends = swap([even, odd], "row")
    even, center, odd = call(
        rows_kernel,
        [(side, jnp.bfloat16), ((2, rows, cols), jnp.float32), (side, jnp.bfloat16)],
        (row, SMEM),
        (me, SMEM),
        middle,
        *over_ends,
        scratch=[pltpu.VMEM((2, rows, cols + 2 * half), jnp.float32)],
    )
    over_sides = swap([even, odd], "col")
    (object_grad,) = call(
        cols_kernel, [(object_field.shape, jnp.float32)], (me, SMEM), center, *over_sides
    )

    def add_up(group, goals, added, dtypes):
        return sums(
            row,
            goals,
            weights,
            [came_at(step) for step in group],
            [received[step] for step in group],
            added,
            num_modes,
            dtypes,
        )

    (following,) = add_up([0] + near, ((1, 1, False),), [], [jnp.float32])
    (following,) = add_up(crossing, ((1, 1, True),), [following], [jnp.bfloat16])
    passed = shift(following, "row", 1)
    (own,) = add_up(every, ((0, 0, False),), [], [jnp.float32])
    mode_grad = (own + passed.astype(jnp.float32))[None]
    return (object_grad, mode_grad)


def solution(mesh):
    in_specs = (
        P(None, "row", "col"),
        P("row", None, None, "col", None),
        P("row", "col", None, None),
        P("row", "col", None, None),
        P("row", "col", None),
        P("row", "col"),
        P("row", "col", None, None, None),
    )
    out_specs = (P(None, "row", "col"), P("row", None, None, "col", None))
    return jax.shard_map(gradients, mesh=mesh, in_specs=in_specs, out_specs=out_specs, check_vma=False)
```

```python
import functools
import math

import jax
import jax.numpy as jnp
import numpy as np
from jax import lax
from jax.experimental import pallas as pl
from jax.experimental.pallas import tpu as pltpu
from jax.sharding import PartitionSpec as P


FLOOR = 0.25
LANES = 128
SUBLANES = 8

VMEM = pl.BlockSpec(memory_space=pltpu.VMEM)
SMEM = pl.BlockSpec(memory_space=pltpu.SMEM)
HBM = pl.BlockSpec(memory_space=pltpu.HBM)


def shift(value, axis, steps):
    count = lax.axis_size(axis)
    leading, last = (max(0, -steps), min(count, count - steps))
    pairs = [(source, source + steps) for source in range(leading, last)]
    return lax.ppermute(value, axis, pairs)


def swap(values, axis):
    count = lax.axis_size(axis)
    got = []
    for odd, value in enumerate(values):
        pairs = []
        for i in range(odd, count - 1, 2):
            pairs += [(i, i + 1), (i + 1, i)]
        got.append(lax.ppermute(value, axis, pairs) if pairs else jnp.zeros_like(value))
    return got


def by_side(index, low, high):
    even = index % 2 == 0
    return jnp.where(even, high, low), jnp.where(even, low, high)


def from_sides(index, first, second):
    high, low = by_side(index, second, first)
    return low, high


def dft_tables(length):
    indices = np.arange(length)
    phases = indices[:, None] * indices[None, :] % length
    angles = phases * (2.0 * math.pi / length)
    scaling = 1.0 / math.sqrt(length)
    re = (np.cos(angles) * scaling).astype(np.float32)
    im = (-np.sin(angles) * scaling).astype(np.float32)
    forward = np.block([[re, -im], [im, re]])
    inverse = np.block([[re, im], [-im, re]])
    return jnp.asarray(forward, jnp.bfloat16), jnp.asarray(inverse, jnp.bfloat16)


def transfer_order(count):
    half = count // 2
    return [half] * (half > 0) + list(range(1, half)) + list(range(half + 1, count))


def slab_order(count, paired):
    steps = transfer_order(count)
    return steps[:1] + [0] + steps[1:] if paired else [0] + steps


def partners(axis):
    count = lax.axis_size(axis)
    steps = transfer_order(count)
    paired = count & (count - 1) == 0

    def goes_to(index, step):
        return index ^ step if paired else (index + step) % count

    def comes_from(index, step):
        return index ^ step if paired else (index - step + count) % count

    return steps, goes_to, comes_from


def call(body, outs, *operands, scratch=(), limit=20):
    arrays = [o[0] if isinstance(o, tuple) else o for o in operands]
    arrays = [
        pltpu.with_memory_space_constraint(a, pltpu.HBM)
        if isinstance(o, tuple) and o[1] is HBM
        else a
        for a, o in zip(arrays, operands)
    ]
    specs = [o[1] if isinstance(o, tuple) else VMEM for o in operands]
    outs = [jax.ShapeDtypeStruct(shape, dtype) for shape, dtype in outs]
    return pl.pallas_call(
        body,
        out_shape=tuple(outs),
        in_specs=specs,
        out_specs=tuple(VMEM for _ in outs),
        scratch_shapes=list(scratch),
        compiler_params=pltpu.CompilerParams(vmem_limit_bytes=limit * 1024 * 1024),
    )(*arrays)


def fetch(arrays, places, held, sem):
    copies = [
        pltpu.make_async_copy(arrays[i].at[block], held.at[at], sem.at[at])
        for at, (i, block) in enumerate(places)
    ]
    for copy in copies:
        copy.start()
    return copies


def held_weights(count, weights):
    shape = (count,) + weights.shape[1:]
    return [pltpu.SMEM(shape, jnp.float32), pltpu.SemaphoreType.DMA((count,))]


def make_slabs(region_of, weight_of, num_modes, row, table, outs):
    next_row = (row[0] + 1).astype(jnp.float32)
    for at, out in enumerate(outs):

        def slot_step(slot, carry, at=at, out=out):
            region = region_of(at, slot)
            which = jnp.where(region == next_row, 1, 0)
            known = jnp.where(jnp.abs(region - next_row + 0.5) < 1.0, 1.0, 0.0)
            scales = [weight_of(at, slot, k) * known for k in range(num_modes)]
            for part in range(2):
                total = scales[0] * table[which, 0, part]
                for k in range(1, num_modes):
                    total += scales[k] * table[which, k, part]
                out[slot, part] = total.astype(jnp.bfloat16)
            return carry

        lax.fori_loop(0, out.shape[0], slot_step, 0)


def first_kernel(places, row, weights, own, follower, out, table, near, held, sem, near_sem):
    copy_own = pltpu.make_async_copy(own, near, near_sem)
    copy_own.start()
    copies = fetch([weights], places, held, sem)
    num_modes, slots = (own.shape[1], out.shape[0])
    table[1] = follower[0].astype(jnp.float32)
    copy_own.wait()
    table[0] = near[0].astype(jnp.float32)
    for copy in copies:
        copy.wait()
    make_slabs(
        lambda at, slot: held[at, slots, slot],
        lambda at, slot, k: held[at, slot, k],
        num_modes,
        row,
        table,
        [out],
    )


def slab_kernel(count, places, row, *refs):
    table = refs[count]
    outs = refs[count + 1 : -2]
    held, sem = refs[-2:]
    slots = outs[0].shape[0]
    for copy in fetch(refs[:count], places, held, sem):
        copy.wait()
    make_slabs(
        lambda at, slot: held[at, slots, slot],
        lambda at, slot, k: held[at, slot, k],
        table.shape[1],
        row,
        table,
        outs,
    )


def slabs(row, weights, places, own, follower):
    shape = (weights[0].shape[1] - 1,) + own.shape[2:]
    first, table = call(
        functools.partial(first_kernel, places[:1]),
        [(shape, jnp.bfloat16), ((2,) + own.shape[1:], jnp.float32)],
        (row, SMEM),
        weights[0],
        (own, HBM),
        follower,
        scratch=[pltpu.VMEM(own.shape, own.dtype)]
        + held_weights(1, weights[0])
        + [pltpu.SemaphoreType.DMA],
    )
    rest = call(
        functools.partial(slab_kernel, len(weights), places[1:]),
        [(shape, jnp.bfloat16)] * (len(places) - 1),
        (row, SMEM),
        *weights,
        table,
        scratch=held_weights(len(places) - 1, weights[0]),
    )
    return [first, *rest]


def payload_kernel(coeffs, region, payload, coeffs_held, region_held, sem):
    slots, num_modes = coeffs.shape[2:]
    copies = [
        pltpu.make_async_copy(coeffs, coeffs_held, sem.at[0]),
        pltpu.make_async_copy(region, region_held, sem.at[1]),
    ]
    for copy in copies:
        copy.start()
    payload[...] = jnp.zeros_like(payload)
    for copy in copies:
        copy.wait()
    payload[:slots, :num_modes] = coeffs_held[0, 0]
    payload[slots:, :slots] = region_held[0].astype(jnp.float32)


def edges_kernel(me, tile, low, even, odd, held, sem):
    half = even.shape[2]
    copy = pltpu.make_async_copy(tile, held, sem)
    copy.start()
    copy.wait()
    low[...] = held[...].astype(jnp.bfloat16)
    first, second = by_side(me[0], low[:, :, :half], low[:, :, low.shape[2] - half :])
    even[...] = first
    odd[...] = second


def pair_kernel(mine, across, out):
    out[0] = mine[...]
    out[1] = across[...]


def widen_kernel(row, me, tile, even, odd, first, second):
    half = even.shape[2]
    rows, _ = tile.shape[1:]

    def extended(start):
        left, right = from_sides(
            me[0], even[:, start : start + half], odd[:, start : start + half]
        )
        return jnp.concatenate([left, tile[:, start : start + half], right], axis=2)

    first[...], second[...] = by_side(row[0], extended(0), extended(rows - half))


def corner_of(corners, slot, half, limit):
    row = jnp.clip(corners[0, slot] + half, 0, limit)
    col = jnp.clip(corners[1, slot] + half, 0, limit)
    rest_row, rest_col = (row & (SUBLANES - 1), col & (LANES - 1))
    base_row = pl.multiple_of(row - rest_row, SUBLANES)
    base_col = pl.multiple_of(col - rest_col, LANES)
    return base_row, rest_row, base_col, rest_col


def window_kernel(
    row, me, corners, tile, side_even, side_odd, end_even, end_odd, out, ext
):
    size = out.shape[-1]
    half = side_even.shape[-1]
    rows, cols = tile.shape[1:]
    left, right = from_sides(me[0], side_even[...], side_odd[...])
    top, bottom = from_sides(row[0], end_even[...], end_odd[...])
    for part in range(2):
        ext[part, :half, : cols + 2 * half] = top[part].astype(jnp.float32)
        ext[part, half : half + rows, :half] = left[part].astype(jnp.float32)
        ext[part, half : half + rows, half : half + cols] = tile[part].astype(jnp.float32)
        ext[part, half : half + rows, half + cols : cols + 2 * half] = right[part].astype(jnp.float32)
        ext[part, half + rows : 2 * half + rows, : cols + 2 * half] = bottom[part].astype(jnp.float32)
    tall = size + SUBLANES
    wide = size + LANES

    def slot_step(slot, carry):
        base_row, rest_row, base_col, rest_col = corner_of(
            corners, slot, half, rows + 2 * half - size
        )
        for part in range(2):
            block = ext[part, pl.ds(base_row, tall), pl.ds(base_col, wide)]
            block = pltpu.roll(block, lax.rem(tall - rest_row, tall), 0)[:size]
            block = pltpu.roll(block, lax.rem(wide - rest_col, wide), 1)[:, :size]
            out[slot, part] = block.astype(jnp.bfloat16)
        return carry

    lax.fori_loop(0, out.shape[0], slot_step, 0)


def levels_kernel(intensity, measured, held, sem):
    copy = pltpu.make_async_copy(intensity, held, sem)
    copy.start()
    copy.wait()
    for slot in range(measured.shape[0]):
        measured[slot] = jnp.sqrt(held[0, 0, slot].astype(jnp.float32))


def windows_of(row, me, corners, tile, sides, ends, slot_count, size):
    half = sides[0].shape[-1]
    extent = (2, tile.shape[1] + 2 * half + SUBLANES, tile.shape[2] + 2 * half + LANES)
    return call(
        window_kernel,
        [((slot_count, 2, size, size), jnp.bfloat16)],
        (row, SMEM),
        (me, SMEM),
        (corners, SMEM),
        tile,
        *sides,
        *ends,
        scratch=[pltpu.VMEM(extent, jnp.float32)],
    )[0]


def dft_kernel(goes_to, comes_from, steps, counts, me, *refs):
    blocks = refs[: len(steps)]
    windows, measured, forward, inverse = refs[len(steps) : len(steps) + 4]
    outs = refs[len(steps) + 4 : 2 * len(steps) + 4]
    placed, probes, terms = refs[2 * len(steps) + 4 :]
    size = windows.shape[-1]
    rows = blocks[0].shape[2]
    starts = [pl.multiple_of(comes_from(me[0], step) * rows, rows) for step in steps]
    targets = [pl.multiple_of(goes_to(me[0], step) * rows, rows) for step in steps]

    def dot(left, right):
        return jnp.dot(left, right, preferred_element_type=jnp.float32)

    for block, start in zip(blocks, starts):
        probes[:, :, pl.ds(start, rows)] = block[...]
    slots = range(windows.shape[0])

    def held(ref, slot):
        return ref[slot, 0].astype(jnp.float32), ref[slot, 1].astype(jnp.float32)

    def stacked(re, im):
        return jnp.concatenate([re.astype(jnp.bfloat16), im.astype(jnp.bfloat16)], axis=0)

    def beside(products):
        columns = [products[:, slot * size : (slot + 1) * size] for slot in slots]
        turned = [jnp.concatenate([c[:size], c[size:]], axis=1) for c in columns]
        return jnp.concatenate(turned, axis=0)

    def parts(products, slot):
        block = products[slot * size : (slot + 1) * size]
        return block[:, :size], block[:, size:]

    leaving = []
    for slot in slots:
        probe_re, probe_im = held(probes, slot)
        window_re, window_im = held(windows, slot)
        leaving.append(
            stacked(
                probe_re * window_re - probe_im * window_im,
                probe_re * window_im + probe_im * window_re,
            )
        )
    half = dot(forward[...], jnp.concatenate(leaving, axis=1)).astype(jnp.bfloat16)
    far = dot(beside(half), inverse[...])
    changes = []
    for slot in slots:
        far_re, far_im = parts(far, slot)
        power = jnp.maximum(far_re * far_re + far_im * far_im, FLOOR * FLOOR)
        live = jnp.where(slot < counts[0, 0], 1.0, 0.0).astype(jnp.float32)
        factor = (measured[slot] * lax.rsqrt(power) - 1.0) * live
        changes.append(stacked(far_re * factor, far_im * factor))
    back = dot(inverse[...], jnp.concatenate(changes, axis=1)).astype(jnp.bfloat16)
    update = dot(beside(back), forward[...])
    for slot in slots:
        update_re, update_im = parts(update, slot)
        probe_re, probe_im = held(probes, slot)
        window_re, window_im = held(windows, slot)
        terms[slot, 0] = (window_re * update_re + window_im * update_im).astype(jnp.bfloat16)
        terms[slot, 1] = (window_re * update_im - window_im * update_re).astype(jnp.bfloat16)
        placed[slot, 0] = probe_re * update_re + probe_im * update_im
        placed[slot, 1] = probe_re * update_im - probe_im * update_re
    for out, start in zip(outs, targets):
        out[...] = terms[:, :, pl.ds(start, rows)]


def place_kernel(half, row, corners, pieces, first, middle, second, accum):
    size = pieces.shape[-1]
    rows = middle.shape[1]
    width = middle.shape[2]
    accum[...] = jnp.zeros_like(accum)
    for slot in range(pieces.shape[0]):
        base_row, rest_row, base_col, rest_col = corner_of(
            corners, slot, half, rows + 2 * half - size
        )
        for part in range(2):
            block = jnp.concatenate(
                [pieces[slot, part], jnp.zeros((size, LANES), jnp.float32)], axis=1
            )
            block = pltpu.roll(block, rest_col, 1)
            block = jnp.concatenate(
                [block, jnp.zeros((SUBLANES, size + LANES), jnp.float32)], axis=0
            )
            block = pltpu.roll(block, rest_row, 0)
            where = (part, pl.ds(base_row, size + SUBLANES), pl.ds(base_col, size + LANES))
            accum[where] += block
    middle[...] = accum[:, half : half + rows, :width]
    top = accum[:, :half, :width].astype(jnp.bfloat16)
    bottom = accum[:, half + rows : 2 * half + rows, :width].astype(jnp.bfloat16)
    first[...], second[...] = by_side(row[0], top, bottom)


def rows_kernel(row, me, middle, even, odd, first, center, second, total):
    half = even.shape[1]
    rows = middle.shape[1]
    cols = center.shape[2]
    got_top, got_bottom = from_sides(row[0], even[...], odd[...])
    total[...] = middle[...]
    total[:, :half] += got_top.astype(jnp.float32)
    total[:, rows - half :] += got_bottom.astype(jnp.float32)
    center[...] = total[:, :, half : half + cols]
    left = total[:, :, :half].astype(jnp.bfloat16)
    right = total[:, :, half + cols :].astype(jnp.bfloat16)
    first[...], second[...] = by_side(me[0], left, right)


def cols_kernel(me, center, even, odd, out):
    half = even.shape[2]
    cols = out.shape[2]
    got_left, got_right = from_sides(me[0], even[...], odd[...])
    out[...] = center[...]
    out[:, :, :half] += got_left.astype(jnp.float32)
    out[:, :, cols - half :] += got_right.astype(jnp.float32)


def sums_kernel(held_in, places, goals, row, *refs):
    count = len(places)
    received = refs[held_in : held_in + count]
    added = refs[held_in + count : held_in + count + sum(goal[2] for goal in goals)]
    outs = refs[held_in + count + len(added) : -3]
    terms, held, sem = refs[-3:]
    copies = fetch(refs[:held_in], places, held, sem)
    num_modes = outs[0].shape[-4]
    slot_count = received[0].shape[0]
    slots = slot_count
    first = min(goal[1] for goal in goals)
    for at in range(count):
        terms[at, first:] = received[at][first:].astype(jnp.float32)
    for copy in copies:
        copy.wait()

    def mode_step(k, carry):
        rest = list(added)
        for (step, first, adds), out in zip(goals, outs):
            region = (row[0] + step).astype(jnp.float32)
            addend = rest.pop(0) if adds else None
            scales = [
                jnp.where(held[at, slots, slot] == region, held[at, slot, k], 0.0)
                for at in range(count)
                for slot in range(first, slot_count)
            ]
            for part in range(2):
                pieces = [
                    terms[at, slot, part] for at in range(count) for slot in range(first, slot_count)
                ]
                total = scales[0] * pieces[0]
                for scale, piece in zip(scales[1:], pieces[1:]):
                    total += scale * piece
                if adds:
                    total += addend[k, part].astype(jnp.float32)
                out[k, part] = total.astype(out.dtype)
        return carry

    lax.fori_loop(0, num_modes, mode_step, 0)


def sums(row, goals, weights, places, received, added, num_modes, dtypes):
    shape = (num_modes,) + received[0].shape[1:]
    return call(
        functools.partial(sums_kernel, len(weights), places, goals),
        [(shape, dtype) for dtype in dtypes],
        (row, SMEM),
        *weights,
        *received,
        *added,
        scratch=[pltpu.VMEM((len(received),) + received[0].shape, jnp.float32)]
        + held_weights(len(places), weights[0]),
    )


def gradients(object_field, modes, coeffs, offsets, region, counts, intensity):
    size = modes.shape[-1]
    half = size // 2
    num_modes = modes.shape[1]
    slot_count = coeffs.shape[2]
    rows, cols = object_field.shape[1:]
    block = (slot_count,) + modes.shape[2:]
    row = lax.axis_index("row").reshape(1)
    me = lax.axis_index("col").reshape(1)
    steps, goes_to, comes_from = partners("col")
    every = [0] + steps
    count = lax.axis_size("col")
    middle_step = count // 2
    near = list(range(1, middle_step))
    crossing = list(range(max(middle_step, 1), count))

    def move(value, step):
        return lax.ppermute(value, "col", [(i, goes_to(i, step)) for i in range(count)])

    side = (2, rows, half)
    (payload,) = call(
        payload_kernel,
        [((slot_count + 1, LANES), jnp.float32)],
        (coeffs, HBM),
        (region, HBM),
        scratch=[pltpu.VMEM(x.shape, x.dtype) for x in (coeffs, region)]
        + [pltpu.SemaphoreType.DMA((2,))],
    )
    low, *edges = call(
        edges_kernel,
        [(object_field.shape, jnp.bfloat16)] + [(side, jnp.bfloat16)] * 2,
        (me, SMEM),
        (object_field, HBM),
        scratch=[pltpu.VMEM(object_field.shape, object_field.dtype), pltpu.SemaphoreType.DMA],
    )
    paired = count > 1 and count & (count - 1) == 0
    if paired:
        across = move(payload, middle_step)
        blocks_shape = (2,) + payload.shape
        (pair,) = call(pair_kernel, [(blocks_shape, jnp.float32)], payload, across)
        weights = [pair] + [move(pair, step) for step in near]

        def made_at(step):
            return step % middle_step, step // middle_step

        came_at = made_at
    else:
        weights = [payload[None]]
        weights += [move(payload[None], step) for step in range(1, count)]

        def made_at(step):
            return -step % count, 0

        def came_at(step):
            return step, 0

    follower = shift(modes, "row", -1)

    sides = swap(edges, "col")
    wide = (2, half, cols + 2 * half)
    ends = call(widen_kernel, [(wide, jnp.bfloat16)] * 2, (row, SMEM), (me, SMEM), low, *sides)
    ends = swap(ends, "row")

    blocks = {}
    turns = slab_order(count, paired)
    made = slabs(row, weights, [made_at(step) for step in turns], modes, follower)
    for step, slab in zip(turns, made):
        blocks[step] = move(slab, step) if step else slab

    corners = pltpu.with_memory_space_constraint(offsets[0, 0].T, pltpu.HBM)
    (measured,) = call(
        levels_kernel,
        [((slot_count, size, size), jnp.float32)],
        (intensity, HBM),
        scratch=[pltpu.VMEM(intensity.shape, intensity.dtype), pltpu.SemaphoreType.DMA],
    )
    windows = windows_of(row, me, corners, low, sides, ends, slot_count, size)
    whole = (slot_count, 2, size, size)
    *terms, placed = call(
        functools.partial(dft_kernel, goes_to, comes_from, every),
        [(block, jnp.bfloat16)] * count + [(whole, jnp.float32)],
        (counts, SMEM),
        (me, SMEM),
        *[blocks[step] for step in every],
        windows,
        measured,
        *dft_tables(size),
        scratch=[pltpu.VMEM(whole, jnp.bfloat16)] * 2,
        limit=32,
    )
    terms = dict(zip(every, terms))
    received = {step: move(terms[step], step) if step else terms[step] for step in every}

    extent = (2, rows + 2 * half + SUBLANES, cols + 2 * half + LANES)
    even, middle, odd = call(
        functools.partial(place_kernel, half),
        [(wide, jnp.bfloat16), ((2, rows, cols + 2 * half), jnp.float32), (wide, jnp.bfloat16)],
        (row, SMEM),
        (corners, SMEM),
        placed,
        scratch=[pltpu.VMEM(extent, jnp.float32)],
    )
    over_ends = swap([even, odd], "row")
    even, center, odd = call(
        rows_kernel,
        [(side, jnp.bfloat16), ((2, rows, cols), jnp.float32), (side, jnp.bfloat16)],
        (row, SMEM),
        (me, SMEM),
        middle,
        *over_ends,
        scratch=[pltpu.VMEM((2, rows, cols + 2 * half), jnp.float32)],
    )
    over_sides = swap([even, odd], "col")
    (object_grad,) = call(
        cols_kernel, [(object_field.shape, jnp.float32)], (me, SMEM), center, *over_sides
    )

    def add_up(group, goals, added, dtypes):
        return sums(
            row,
            goals,
            weights,
            [came_at(step) for step in group],
            [received[step] for step in group],
            added,
            num_modes,
            dtypes,
        )

    (following,) = add_up([0] + near, ((1, 1, False),), [], [jnp.float32])
    if len(crossing) > 1:
        (following,) = add_up(crossing[:-1], ((1, 1, True),), [following], [jnp.float32])
    (following,) = add_up(crossing[-1:], ((1, 1, True),), [following], [jnp.bfloat16])
    passed = shift(following, "row", 1)
    (own,) = add_up(every, ((0, 0, False),), [], [jnp.float32])
    mode_grad = (own + passed.astype(jnp.float32))[None]
    return (object_grad, mode_grad)


def solution(mesh):
    in_specs = (
        P(None, "row", "col"),
        P("row", None, None, "col", None),
        P("row", "col", None, None),
        P("row", "col", None, None),
        P("row", "col", None),
        P("row", "col"),
        P("row", "col", None, None, None),
    )
    out_specs = (P(None, "row", "col"), P("row", None, None, "col", None))
    return jax.shard_map(gradients, mesh=mesh, in_specs=in_specs, out_specs=out_specs, check_vma=False)
```

```python
import functools
import math

import jax
import jax.numpy as jnp
import numpy as np
from jax import lax
from jax.experimental import pallas as pl
from jax.experimental.pallas import tpu as pltpu
from jax.sharding import PartitionSpec as P


FLOOR = 0.25
LANES = 128
SUBLANES = 8

VMEM = pl.BlockSpec(memory_space=pltpu.VMEM)
SMEM = pl.BlockSpec(memory_space=pltpu.SMEM)
HBM = pl.BlockSpec(memory_space=pltpu.HBM)


def shift(value, axis, steps):
    count = lax.axis_size(axis)
    leading, last = (max(0, -steps), min(count, count - steps))
    pairs = [(source, source + steps) for source in range(leading, last)]
    return lax.ppermute(value, axis, pairs)


def swap(values, axis):
    count = lax.axis_size(axis)
    got = []
    for odd, value in enumerate(values):
        pairs = []
        for i in range(odd, count - 1, 2):
            pairs += [(i, i + 1), (i + 1, i)]
        got.append(lax.ppermute(value, axis, pairs) if pairs else jnp.zeros_like(value))
    return got


def by_side(index, low, high):
    even = index % 2 == 0
    return jnp.where(even, high, low), jnp.where(even, low, high)


def from_sides(index, first, second):
    high, low = by_side(index, second, first)
    return low, high


def dft_tables(length):
    indices = np.arange(length)
    phases = indices[:, None] * indices[None, :] % length
    angles = phases * (2.0 * math.pi / length)
    scaling = 1.0 / math.sqrt(length)
    re = (np.cos(angles) * scaling).astype(np.float32)
    im = (-np.sin(angles) * scaling).astype(np.float32)
    forward = np.block([[re, -im], [im, re]])
    inverse = np.block([[re, im], [-im, re]])
    return jnp.asarray(forward, jnp.bfloat16), jnp.asarray(inverse, jnp.bfloat16)


def transfer_order(count):
    half = count // 2
    return [half] * (half > 0) + list(range(1, half)) + list(range(half + 1, count))


def slab_order(count, paired):
    steps = transfer_order(count)
    return steps[:1] + [0] + steps[1:] if paired else [0] + steps


def partners(axis):
    count = lax.axis_size(axis)
    steps = transfer_order(count)
    paired = count & (count - 1) == 0

    def goes_to(index, step):
        return index ^ step if paired else (index + step) % count

    def comes_from(index, step):
        return index ^ step if paired else (index - step + count) % count

    return steps, goes_to, comes_from


def call(body, outs, *operands, scratch=(), limit=20, aliases={}):
    arrays = [o[0] if isinstance(o, tuple) else o for o in operands]
    arrays = [
        pltpu.with_memory_space_constraint(a, pltpu.HBM)
        if isinstance(o, tuple) and o[1] is HBM
        else a
        for a, o in zip(arrays, operands)
    ]
    specs = [o[1] if isinstance(o, tuple) else VMEM for o in operands]
    outs = [jax.ShapeDtypeStruct(shape, dtype) for shape, dtype in outs]
    return pl.pallas_call(
        body,
        out_shape=tuple(outs),
        in_specs=specs,
        out_specs=tuple(VMEM for _ in outs),
        scratch_shapes=list(scratch),
        input_output_aliases=aliases,
        compiler_params=pltpu.CompilerParams(vmem_limit_bytes=limit * 1024 * 1024),
    )(*arrays)


def fetch(arrays, places, held, sem):
    copies = [
        pltpu.make_async_copy(arrays[i].at[block], held.at[at], sem.at[at])
        for at, (i, block) in enumerate(places)
    ]
    for copy in copies:
        copy.start()
    return copies


def held_weights(count, weights):
    shape = (count,) + weights.shape[1:]
    return [pltpu.SMEM(shape, jnp.float32), pltpu.SemaphoreType.DMA((count,))]


def make_slabs(region_of, weight_of, num_modes, row, table, outs):
    next_row = (row[0] + 1).astype(jnp.float32)
    for at, out in enumerate(outs):

        def slot_step(slot, carry, at=at, out=out):
            region = region_of(at, slot)
            which = jnp.where(region == next_row, 1, 0)
            known = jnp.where(jnp.abs(region - next_row + 0.5) < 1.0, 1.0, 0.0)
            scales = [weight_of(at, slot, k) * known for k in range(num_modes)]
            for part in range(2):
                total = scales[0] * table[which, 0, part]
                for k in range(1, num_modes):
                    total += scales[k] * table[which, k, part]
                out[slot, part] = total.astype(jnp.bfloat16)
            return carry

        lax.fori_loop(0, out.shape[0], slot_step, 0)


def first_kernel(places, row, weights, own, follower, out, table, near, held, sem, near_sem):
    copy_own = pltpu.make_async_copy(own, near, near_sem)
    copy_own.start()
    copies = fetch([weights], places, held, sem)
    num_modes, slots = (own.shape[1], out.shape[0])
    table[1] = follower[0].astype(jnp.float32)
    copy_own.wait()
    table[0] = near[0].astype(jnp.float32)
    for copy in copies:
        copy.wait()
    make_slabs(
        lambda at, slot: held[at, slots, slot],
        lambda at, slot, k: held[at, slot, k],
        num_modes,
        row,
        table,
        [out],
    )


def slab_kernel(count, places, row, *refs):
    table = refs[count]
    outs = refs[count + 1 : -2]
    held, sem = refs[-2:]
    slots = outs[0].shape[0]
    for copy in fetch(refs[:count], places, held, sem):
        copy.wait()
    make_slabs(
        lambda at, slot: held[at, slots, slot],
        lambda at, slot, k: held[at, slot, k],
        table.shape[1],
        row,
        table,
        outs,
    )


def slabs(row, weights, places, own, follower):
    shape = (weights[0].shape[1] - 1,) + own.shape[2:]
    first, table = call(
        functools.partial(first_kernel, places[:1]),
        [(shape, jnp.bfloat16), ((2,) + own.shape[1:], jnp.float32)],
        (row, SMEM),
        weights[0],
        (own, HBM),
        follower,
        scratch=[pltpu.VMEM(own.shape, own.dtype)]
        + held_weights(1, weights[0])
        + [pltpu.SemaphoreType.DMA],
    )
    rest = call(
        functools.partial(slab_kernel, len(weights), places[1:]),
        [(shape, jnp.bfloat16)] * (len(places) - 1),
        (row, SMEM),
        *weights,
        table,
        scratch=held_weights(len(places) - 1, weights[0]),
    )
    return [first, *rest]


def payload_kernel(coeffs, region, payload, coeffs_held, region_held, sem):
    slots, num_modes = coeffs.shape[2:]
    copies = [
        pltpu.make_async_copy(coeffs, coeffs_held, sem.at[0]),
        pltpu.make_async_copy(region, region_held, sem.at[1]),
    ]
    for copy in copies:
        copy.start()
    payload[...] = jnp.zeros_like(payload)
    for copy in copies:
        copy.wait()
    payload[:slots, :num_modes] = coeffs_held[0, 0]
    payload[slots:, :slots] = region_held[0].astype(jnp.float32)


def edges_kernel(me, tile, low, even, odd, held, sem):
    half = even.shape[2]
    copy = pltpu.make_async_copy(tile, held, sem)
    copy.start()
    copy.wait()
    low[...] = held[...].astype(jnp.bfloat16)
    first, second = by_side(me[0], low[:, :, :half], low[:, :, low.shape[2] - half :])
    even[...] = first
    odd[...] = second


def pair_kernel(mine, across, out):
    out[0] = mine[...]
    out[1] = across[...]


def widen_kernel(row, me, tile, even, odd, first, second):
    half = even.shape[2]
    rows, _ = tile.shape[1:]

    def extended(start):
        left, right = from_sides(
            me[0], even[:, start : start + half], odd[:, start : start + half]
        )
        return jnp.concatenate([left, tile[:, start : start + half], right], axis=2)

    first[...], second[...] = by_side(row[0], extended(0), extended(rows - half))


def corner_of(corners, slot, half, limit):
    row = jnp.clip(corners[0, slot] + half, 0, limit)
    col = jnp.clip(corners[1, slot] + half, 0, limit)
    rest_row, rest_col = (row & (SUBLANES - 1), col & (LANES - 1))
    base_row = pl.multiple_of(row - rest_row, SUBLANES)
    base_col = pl.multiple_of(col - rest_col, LANES)
    return base_row, rest_row, base_col, rest_col


def window_kernel(
    row, me, corners, tile, side_even, side_odd, end_even, end_odd, out, ext
):
    size = out.shape[-1]
    half = side_even.shape[-1]
    rows, cols = tile.shape[1:]
    left, right = from_sides(me[0], side_even[...], side_odd[...])
    top, bottom = from_sides(row[0], end_even[...], end_odd[...])
    for part in range(2):
        ext[part, :half, : cols + 2 * half] = top[part].astype(jnp.float32)
        ext[part, half : half + rows, :half] = left[part].astype(jnp.float32)
        ext[part, half : half + rows, half : half + cols] = tile[part].astype(jnp.float32)
        ext[part, half : half + rows, half + cols : cols + 2 * half] = right[part].astype(jnp.float32)
        ext[part, half + rows : 2 * half + rows, : cols + 2 * half] = bottom[part].astype(jnp.float32)
    tall = size + SUBLANES
    wide = size + LANES

    def slot_step(slot, carry):
        base_row, rest_row, base_col, rest_col = corner_of(
            corners, slot, half, rows + 2 * half - size
        )
        for part in range(2):
            block = ext[part, pl.ds(base_row, tall), pl.ds(base_col, wide)]
            block = pltpu.roll(block, lax.rem(tall - rest_row, tall), 0)[:size]
            block = pltpu.roll(block, lax.rem(wide - rest_col, wide), 1)[:, :size]
            out[slot, part] = block.astype(jnp.bfloat16)
        return carry

    lax.fori_loop(0, out.shape[0], slot_step, 0)


def levels_kernel(intensity, measured, zeros, held, sem):
    copy = pltpu.make_async_copy(intensity, held, sem)
    copy.start()
    zeros[...] = jnp.zeros_like(zeros)
    copy.wait()
    for slot in range(measured.shape[0]):
        measured[slot] = jnp.sqrt(held[0, 0, slot].astype(jnp.float32))


def windows_of(row, me, corners, tile, sides, ends, slot_count, size):
    half = sides[0].shape[-1]
    extent = (2, tile.shape[1] + 2 * half + SUBLANES, tile.shape[2] + 2 * half + LANES)
    return call(
        window_kernel,
        [((slot_count, 2, size, size), jnp.bfloat16)],
        (row, SMEM),
        (me, SMEM),
        (corners, SMEM),
        tile,
        *sides,
        *ends,
        scratch=[pltpu.VMEM(extent, jnp.float32)],
    )[0]


def dft_kernel(goes_to, comes_from, steps, counts, me, *refs):
    blocks = refs[: len(steps)]
    windows, measured, forward, inverse = refs[len(steps) : len(steps) + 4]
    outs = refs[len(steps) + 4 : 2 * len(steps) + 4]
    placed, probes, terms = refs[2 * len(steps) + 4 :]
    size = windows.shape[-1]
    rows = blocks[0].shape[2]
    starts = [pl.multiple_of(comes_from(me[0], step) * rows, rows) for step in steps]
    targets = [pl.multiple_of(goes_to(me[0], step) * rows, rows) for step in steps]

    def dot(left, right):
        return jnp.dot(left, right, preferred_element_type=jnp.float32)

    for block, start in zip(blocks, starts):
        probes[:, :, pl.ds(start, rows)] = block[...]
    slots = range(windows.shape[0])

    def held(ref, slot):
        return ref[slot, 0].astype(jnp.float32), ref[slot, 1].astype(jnp.float32)

    def stacked(re, im):
        return jnp.concatenate([re.astype(jnp.bfloat16), im.astype(jnp.bfloat16)], axis=0)

    def beside(products):
        columns = [products[:, slot * size : (slot + 1) * size] for slot in slots]
        turned = [jnp.concatenate([c[:size], c[size:]], axis=1) for c in columns]
        return jnp.concatenate(turned, axis=0)

    def parts(products, slot):
        block = products[slot * size : (slot + 1) * size]
        return block[:, :size], block[:, size:]

    leaving = []
    for slot in slots:
        probe_re, probe_im = held(probes, slot)
        window_re, window_im = held(windows, slot)
        leaving.append(
            stacked(
                probe_re * window_re - probe_im * window_im,
                probe_re * window_im + probe_im * window_re,
            )
        )
    half = dot(forward[...], jnp.concatenate(leaving, axis=1)).astype(jnp.bfloat16)
    far = dot(beside(half), inverse[...])
    changes = []
    for slot in slots:
        far_re, far_im = parts(far, slot)
        power = jnp.maximum(far_re * far_re + far_im * far_im, FLOOR * FLOOR)
        live = jnp.where(slot < counts[0, 0], 1.0, 0.0).astype(jnp.float32)
        factor = (measured[slot] * lax.rsqrt(power) - 1.0) * live
        changes.append(stacked(far_re * factor, far_im * factor))
    back = dot(inverse[...], jnp.concatenate(changes, axis=1)).astype(jnp.bfloat16)
    update = dot(beside(back), forward[...])
    for slot in slots:
        update_re, update_im = parts(update, slot)
        probe_re, probe_im = held(probes, slot)
        window_re, window_im = held(windows, slot)
        terms[slot, 0] = (window_re * update_re + window_im * update_im).astype(jnp.bfloat16)
        terms[slot, 1] = (window_re * update_im - window_im * update_re).astype(jnp.bfloat16)
        placed[slot, 0] = probe_re * update_re + probe_im * update_im
        placed[slot, 1] = probe_re * update_im - probe_im * update_re
    for out, start in zip(outs, targets):
        out[...] = terms[:, :, pl.ds(start, rows)]


def place_kernel(half, row, corners, pieces, zeros, first, accum, second):
    size = pieces.shape[-1]
    rows = accum.shape[1] - SUBLANES - 2 * half
    width = first.shape[2]
    for slot in range(pieces.shape[0]):
        base_row, rest_row, base_col, rest_col = corner_of(
            corners, slot, half, rows + 2 * half - size
        )
        for part in range(2):
            block = jnp.concatenate(
                [pieces[slot, part], jnp.zeros((size, LANES), jnp.float32)], axis=1
            )
            block = pltpu.roll(block, rest_col, 1)
            block = jnp.concatenate(
                [block, jnp.zeros((SUBLANES, size + LANES), jnp.float32)], axis=0
            )
            block = pltpu.roll(block, rest_row, 0)
            where = (part, pl.ds(base_row, size + SUBLANES), pl.ds(base_col, size + LANES))
            accum[where] += block
    top = accum[:, :half, :width].astype(jnp.bfloat16)
    bottom = accum[:, half + rows : 2 * half + rows, :width].astype(jnp.bfloat16)
    first[...], second[...] = by_side(row[0], top, bottom)


def rows_kernel(row, me, accum, even, odd, first, center, second, total):
    half = even.shape[1]
    rows, cols = center.shape[1:]
    got_top, got_bottom = from_sides(row[0], even[...], odd[...])
    total[...] = accum[:, half : half + rows, : cols + 2 * half]
    total[:, :half] += got_top.astype(jnp.float32)
    total[:, rows - half :] += got_bottom.astype(jnp.float32)
    center[...] = total[:, :, half : half + cols]
    left = total[:, :, :half].astype(jnp.bfloat16)
    right = total[:, :, half + cols :].astype(jnp.bfloat16)
    first[...], second[...] = by_side(me[0], left, right)


def cols_kernel(me, center, even, odd, out):
    half = even.shape[2]
    cols = out.shape[2]
    got_left, got_right = from_sides(me[0], even[...], odd[...])
    out[...] = center[...]
    out[:, :, :half] += got_left.astype(jnp.float32)
    out[:, :, cols - half :] += got_right.astype(jnp.float32)


def sums_kernel(held_in, places, goals, row, *refs):
    count = len(places)
    received = refs[held_in : held_in + count]
    added = refs[held_in + count : held_in + count + sum(goal[2] for goal in goals)]
    outs = refs[held_in + count + len(added) : -3]
    terms, held, sem = refs[-3:]
    copies = fetch(refs[:held_in], places, held, sem)
    num_modes = outs[0].shape[-4]
    slot_count = received[0].shape[0]
    slots = slot_count
    first = min(goal[1] for goal in goals)
    for at in range(count):
        terms[at, first:] = received[at][first:].astype(jnp.float32)
    for copy in copies:
        copy.wait()

    def mode_step(k, carry):
        rest = list(added)
        for (step, first, adds), out in zip(goals, outs):
            region = (row[0] + step).astype(jnp.float32)
            addend = rest.pop(0) if adds else None
            scales = [
                jnp.where(held[at, slots, slot] == region, held[at, slot, k], 0.0)
                for at in range(count)
                for slot in range(first, slot_count)
            ]
            for part in range(2):
                pieces = [
                    terms[at, slot, part] for at in range(count) for slot in range(first, slot_count)
                ]
                total = scales[0] * pieces[0]
                for scale, piece in zip(scales[1:], pieces[1:]):
                    total += scale * piece
                if adds:
                    total += addend[k, part].astype(jnp.float32)
                out[k, part] = total.astype(out.dtype)
        return carry

    lax.fori_loop(0, num_modes, mode_step, 0)


def sums(row, goals, weights, places, received, added, num_modes, dtypes):
    shape = (num_modes,) + received[0].shape[1:]
    return call(
        functools.partial(sums_kernel, len(weights), places, goals),
        [(shape, dtype) for dtype in dtypes],
        (row, SMEM),
        *weights,
        *received,
        *added,
        scratch=[pltpu.VMEM((len(received),) + received[0].shape, jnp.float32)]
        + held_weights(len(places), weights[0]),
    )


def gradients(object_field, modes, coeffs, offsets, region, counts, intensity):
    size = modes.shape[-1]
    half = size // 2
    num_modes = modes.shape[1]
    slot_count = coeffs.shape[2]
    rows, cols = object_field.shape[1:]
    block = (slot_count,) + modes.shape[2:]
    row = lax.axis_index("row").reshape(1)
    me = lax.axis_index("col").reshape(1)
    steps, goes_to, comes_from = partners("col")
    every = [0] + steps
    count = lax.axis_size("col")
    middle_step = count // 2
    near = list(range(1, middle_step))
    crossing = list(range(max(middle_step, 1), count))

    def move(value, step):
        return lax.ppermute(value, "col", [(i, goes_to(i, step)) for i in range(count)])

    side = (2, rows, half)
    (payload,) = call(
        payload_kernel,
        [((slot_count + 1, LANES), jnp.float32)],
        (coeffs, HBM),
        (region, HBM),
        scratch=[pltpu.VMEM(x.shape, x.dtype) for x in (coeffs, region)]
        + [pltpu.SemaphoreType.DMA((2,))],
    )
    low, *edges = call(
        edges_kernel,
        [(object_field.shape, jnp.bfloat16)] + [(side, jnp.bfloat16)] * 2,
        (me, SMEM),
        (object_field, HBM),
        scratch=[pltpu.VMEM(object_field.shape, object_field.dtype), pltpu.SemaphoreType.DMA],
    )
    paired = count > 1 and count & (count - 1) == 0
    if paired:
        across = move(payload, middle_step)
        blocks_shape = (2,) + payload.shape
        (pair,) = call(pair_kernel, [(blocks_shape, jnp.float32)], payload, across)
        weights = [pair] + [move(pair, step) for step in near]

        def made_at(step):
            return step % middle_step, step // middle_step

        came_at = made_at
    else:
        weights = [payload[None]]
        weights += [move(payload[None], step) for step in range(1, count)]

        def made_at(step):
            return -step % count, 0

        def came_at(step):
            return step, 0

    follower = shift(modes, "row", -1)

    sides = swap(edges, "col")
    wide = (2, half, cols + 2 * half)
    ends = call(widen_kernel, [(wide, jnp.bfloat16)] * 2, (row, SMEM), (me, SMEM), low, *sides)
    ends = swap(ends, "row")

    blocks = {}
    turns = slab_order(count, paired)
    made = slabs(row, weights, [made_at(step) for step in turns], modes, follower)
    for step, slab in zip(turns, made):
        blocks[step] = move(slab, step) if step else slab

    corners = pltpu.with_memory_space_constraint(offsets[0, 0].T, pltpu.HBM)
    extent = (2, rows + 2 * half + SUBLANES, cols + 2 * half + LANES)
    measured, zeros = call(
        levels_kernel,
        [((slot_count, size, size), jnp.float32), (extent, jnp.float32)],
        (intensity, HBM),
        scratch=[pltpu.VMEM(intensity.shape, intensity.dtype), pltpu.SemaphoreType.DMA],
    )
    windows = windows_of(row, me, corners, low, sides, ends, slot_count, size)
    whole = (slot_count, 2, size, size)
    *terms, placed = call(
        functools.partial(dft_kernel, goes_to, comes_from, every),
        [(block, jnp.bfloat16)] * count + [(whole, jnp.float32)],
        (counts, SMEM),
        (me, SMEM),
        *[blocks[step] for step in every],
        windows,
        measured,
        *dft_tables(size),
        scratch=[pltpu.VMEM(whole, jnp.bfloat16)] * 2,
        limit=32,
    )
    terms = dict(zip(every, terms))
    received = {step: move(terms[step], step) if step else terms[step] for step in every}

    even, accum, odd = call(
        functools.partial(place_kernel, half),
        [(wide, jnp.bfloat16), (extent, jnp.float32), (wide, jnp.bfloat16)],
        (row, SMEM),
        (corners, SMEM),
        placed,
        zeros,
        aliases={3: 1},
    )
    over_ends = swap([even, odd], "row")
    even, center, odd = call(
        rows_kernel,
        [(side, jnp.bfloat16), ((2, rows, cols), jnp.float32), (side, jnp.bfloat16)],
        (row, SMEM),
        (me, SMEM),
        accum,
        *over_ends,
        scratch=[pltpu.VMEM((2, rows, cols + 2 * half), jnp.float32)],
    )
    over_sides = swap([even, odd], "col")
    (object_grad,) = call(
        cols_kernel, [(object_field.shape, jnp.float32)], (me, SMEM), center, *over_sides
    )

    def add_up(group, goals, added, dtypes):
        return sums(
            row,
            goals,
            weights,
            [came_at(step) for step in group],
            [received[step] for step in group],
            added,
            num_modes,
            dtypes,
        )

    (following,) = add_up([0] + near, ((1, 1, False),), [], [jnp.float32])
    (following,) = add_up(crossing, ((1, 1, True),), [following], [jnp.bfloat16])
    passed = shift(following, "row", 1)
    (own,) = add_up(every, ((0, 0, False),), [], [jnp.float32])
    mode_grad = (own + passed.astype(jnp.float32))[None]
    return (object_grad, mode_grad)


def solution(mesh):
    in_specs = (
        P(None, "row", "col"),
        P("row", None, None, "col", None),
        P("row", "col", None, None),
        P("row", "col", None, None),
        P("row", "col", None),
        P("row", "col"),
        P("row", "col", None, None, None),
    )
    out_specs = (P(None, "row", "col"), P("row", None, None, "col", None))
    return jax.shard_map(gradients, mesh=mesh, in_specs=in_specs, out_specs=out_specs, check_vma=False)
```

```python
import functools
import math

import jax
import jax.numpy as jnp
import numpy as np
from jax import lax
from jax.experimental import pallas as pl
from jax.experimental.pallas import tpu as pltpu
from jax.sharding import PartitionSpec as P


FLOOR = 0.25
LANES = 128
SUBLANES = 8

VMEM = pl.BlockSpec(memory_space=pltpu.VMEM)
SMEM = pl.BlockSpec(memory_space=pltpu.SMEM)
HBM = pl.BlockSpec(memory_space=pltpu.HBM)


def shift(value, axis, steps):
    count = lax.axis_size(axis)
    leading, last = (max(0, -steps), min(count, count - steps))
    pairs = [(source, source + steps) for source in range(leading, last)]
    return lax.ppermute(value, axis, pairs)


def swap(values, axis):
    count = lax.axis_size(axis)
    got = []
    for odd, value in enumerate(values):
        pairs = []
        for i in range(odd, count - 1, 2):
            pairs += [(i, i + 1), (i + 1, i)]
        got.append(lax.ppermute(value, axis, pairs) if pairs else jnp.zeros_like(value))
    return got


def by_side(index, low, high):
    even = index % 2 == 0
    return jnp.where(even, high, low), jnp.where(even, low, high)


def from_sides(index, first, second):
    high, low = by_side(index, second, first)
    return low, high


def dft_tables(length):
    indices = np.arange(length)
    phases = indices[:, None] * indices[None, :] % length
    angles = phases * (2.0 * math.pi / length)
    scaling = 1.0 / math.sqrt(length)
    re = (np.cos(angles) * scaling).astype(np.float32)
    im = (-np.sin(angles) * scaling).astype(np.float32)
    forward = np.block([[re, -im], [im, re]])
    inverse = np.block([[re, im], [-im, re]])
    return jnp.asarray(forward, jnp.bfloat16), jnp.asarray(inverse, jnp.bfloat16)


def transfer_order(count):
    half = count // 2
    far = list(range(half + 1, count))
    return [half] * (half > 0) + list(range(1, half)) + far[:-2] + far[:-3:-1]


def slab_order(count, paired):
    steps = transfer_order(count)
    return steps[:1] + [0] + steps[1:] if paired else [0] + steps


def partners(axis):
    count = lax.axis_size(axis)
    steps = transfer_order(count)
    paired = count & (count - 1) == 0

    def goes_to(index, step):
        return index ^ step if paired else (index + step) % count

    def comes_from(index, step):
        return index ^ step if paired else (index - step + count) % count

    return steps, goes_to, comes_from


def call(body, outs, *operands, scratch=(), limit=20, aliases={}):
    arrays = [o[0] if isinstance(o, tuple) else o for o in operands]
    arrays = [
        pltpu.with_memory_space_constraint(a, pltpu.HBM)
        if isinstance(o, tuple) and o[1] is HBM
        else a
        for a, o in zip(arrays, operands)
    ]
    specs = [o[1] if isinstance(o, tuple) else VMEM for o in operands]
    outs = [jax.ShapeDtypeStruct(shape, dtype) for shape, dtype in outs]
    return pl.pallas_call(
        body,
        out_shape=tuple(outs),
        in_specs=specs,
        out_specs=tuple(VMEM for _ in outs),
        scratch_shapes=list(scratch),
        input_output_aliases=aliases,
        compiler_params=pltpu.CompilerParams(vmem_limit_bytes=limit * 1024 * 1024),
    )(*arrays)


def fetch(arrays, places, held, sem):
    copies = [
        pltpu.make_async_copy(arrays[i].at[block], held.at[at], sem.at[at])
        for at, (i, block) in enumerate(places)
    ]
    for copy in copies:
        copy.start()
    return copies


def held_weights(count, weights):
    shape = (count,) + weights.shape[1:]
    return [pltpu.SMEM(shape, jnp.float32), pltpu.SemaphoreType.DMA((count,))]


def make_slabs(region_of, weight_of, num_modes, row, table, outs):
    next_row = (row[0] + 1).astype(jnp.float32)
    for at, out in enumerate(outs):

        def slot_step(slot, carry, at=at, out=out):
            region = region_of(at, slot)
            which = jnp.where(region == next_row, 1, 0)
            known = jnp.where(jnp.abs(region - next_row + 0.5) < 1.0, 1.0, 0.0)
            scales = [weight_of(at, slot, k) * known for k in range(num_modes)]
            for part in range(2):
                total = scales[0] * table[which, 0, part]
                for k in range(1, num_modes):
                    total += scales[k] * table[which, k, part]
                out[slot, part] = total.astype(jnp.bfloat16)
            return carry

        lax.fori_loop(0, out.shape[0], slot_step, 0)


def first_kernel(places, row, weights, own, follower, out, table, near, held, sem, near_sem):
    copy_own = pltpu.make_async_copy(own, near, near_sem)
    copy_own.start()
    copies = fetch([weights], places, held, sem)
    num_modes, slots = (own.shape[1], out.shape[0])
    table[1] = follower[0].astype(jnp.float32)
    copy_own.wait()
    table[0] = near[0].astype(jnp.float32)
    for copy in copies:
        copy.wait()
    make_slabs(
        lambda at, slot: held[at, slots, slot],
        lambda at, slot, k: held[at, slot, k],
        num_modes,
        row,
        table,
        [out],
    )


def slab_kernel(count, places, row, *refs):
    table = refs[count]
    outs = refs[count + 1 : -2]
    held, sem = refs[-2:]
    slots = outs[0].shape[0]
    for copy in fetch(refs[:count], places, held, sem):
        copy.wait()
    make_slabs(
        lambda at, slot: held[at, slots, slot],
        lambda at, slot, k: held[at, slot, k],
        table.shape[1],
        row,
        table,
        outs,
    )


def slabs(row, weights, places, own, follower):
    shape = (weights[0].shape[1] - 1,) + own.shape[2:]
    first, table = call(
        functools.partial(first_kernel, places[:1]),
        [(shape, jnp.bfloat16), ((2,) + own.shape[1:], jnp.float32)],
        (row, SMEM),
        weights[0],
        (own, HBM),
        follower,
        scratch=[pltpu.VMEM(own.shape, own.dtype)]
        + held_weights(1, weights[0])
        + [pltpu.SemaphoreType.DMA],
    )
    rest = call(
        functools.partial(slab_kernel, len(weights), places[1:]),
        [(shape, jnp.bfloat16)] * (len(places) - 1),
        (row, SMEM),
        *weights,
        table,
        scratch=held_weights(len(places) - 1, weights[0]),
    )
    return [first, *rest]


def payload_kernel(coeffs, region, payload, coeffs_held, region_held, sem):
    slots, num_modes = coeffs.shape[2:]
    copies = [
        pltpu.make_async_copy(coeffs, coeffs_held, sem.at[0]),
        pltpu.make_async_copy(region, region_held, sem.at[1]),
    ]
    for copy in copies:
        copy.start()
    payload[...] = jnp.zeros_like(payload)
    for copy in copies:
        copy.wait()
    payload[:slots, :num_modes] = coeffs_held[0, 0]
    payload[slots:, :slots] = region_held[0].astype(jnp.float32)


def edges_kernel(me, tile, low, even, odd, held, sem):
    half = even.shape[2]
    copy = pltpu.make_async_copy(tile, held, sem)
    copy.start()
    copy.wait()
    low[...] = held[...].astype(jnp.bfloat16)
    first, second = by_side(me[0], low[:, :, :half], low[:, :, low.shape[2] - half :])
    even[...] = first
    odd[...] = second


def pair_kernel(mine, across, out):
    out[0] = mine[...]
    out[1] = across[...]


def widen_kernel(row, me, tile, even, odd, first, second):
    half = even.shape[2]
    rows, _ = tile.shape[1:]

    def extended(start):
        left, right = from_sides(
            me[0], even[:, start : start + half], odd[:, start : start + half]
        )
        return jnp.concatenate([left, tile[:, start : start + half], right], axis=2)

    first[...], second[...] = by_side(row[0], extended(0), extended(rows - half))


def corner_of(corners, slot, half, limit):
    row = jnp.clip(corners[0, slot] + half, 0, limit)
    col = jnp.clip(corners[1, slot] + half, 0, limit)
    rest_row, rest_col = (row & (SUBLANES - 1), col & (LANES - 1))
    base_row = pl.multiple_of(row - rest_row, SUBLANES)
    base_col = pl.multiple_of(col - rest_col, LANES)
    return base_row, rest_row, base_col, rest_col


def beyond(shape, dim, bound):
    return lax.broadcasted_iota(jnp.int32, shape, dim) >= bound


def pushed(block, down, across):
    rows, cols = block.shape
    edge = jnp.zeros((rows, LANES), block.dtype)
    tiles = [block[:, start : start + LANES] for start in range(0, cols, LANES)]
    tiles = [pltpu.roll(tile, across, 1) for tile in tiles]
    kept = beyond((rows, LANES), 1, across)
    pairs = zip(tiles + [edge], [edge] + tiles)
    block = jnp.concatenate([jnp.where(kept, tile, before) for tile, before in pairs], axis=1)
    cols += LANES
    tall = block.reshape(rows // SUBLANES, SUBLANES, cols)
    tall = pltpu.roll(tall, down, 1)
    edge = jnp.zeros((1, SUBLANES, cols), block.dtype)
    below = jnp.concatenate([tall, edge], axis=0)
    above = jnp.concatenate([edge, tall], axis=0)
    tall = jnp.where(beyond(below.shape, 1, down), below, above)
    return tall.reshape(rows + SUBLANES, cols)


def pulled(block, up, back):
    rows, cols = block.shape
    tall = block.reshape(rows // SUBLANES, SUBLANES, cols)
    tall = pltpu.roll(tall, (SUBLANES - up) & (SUBLANES - 1), 1)
    kept = beyond(tall[1:].shape, 1, SUBLANES - up)
    block = jnp.where(kept, tall[1:], tall[:-1]).reshape(rows - SUBLANES, cols)
    tiles = [block[:, start : start + LANES] for start in range(0, cols, LANES)]
    tiles = [pltpu.roll(tile, (LANES - back) & (LANES - 1), 1) for tile in tiles]
    kept = beyond((rows - SUBLANES, LANES), 1, LANES - back)
    pairs = zip(tiles[1:], tiles[:-1])
    return jnp.concatenate([jnp.where(kept, after, tile) for after, tile in pairs], axis=1)


def window_kernel(
    row, me, corners, tile, side_even, side_odd, end_even, end_odd, out, ext
):
    size = out.shape[-1]
    half = side_even.shape[-1]
    rows, cols = tile.shape[1:]
    left, right = from_sides(me[0], side_even[...], side_odd[...])
    top, bottom = from_sides(row[0], end_even[...], end_odd[...])
    for part in range(2):
        ext[part, :half, : cols + 2 * half] = top[part].astype(jnp.float32)
        ext[part, half : half + rows, :half] = left[part].astype(jnp.float32)
        ext[part, half : half + rows, half : half + cols] = tile[part].astype(jnp.float32)
        ext[part, half : half + rows, half + cols : cols + 2 * half] = right[part].astype(jnp.float32)
        ext[part, half + rows : 2 * half + rows, : cols + 2 * half] = bottom[part].astype(jnp.float32)
    tall = size + SUBLANES
    wide = size + LANES

    def slot_step(slot, carry):
        base_row, rest_row, base_col, rest_col = corner_of(
            corners, slot, half, rows + 2 * half - size
        )
        for part in range(2):
            block = ext[part, pl.ds(base_row, tall), pl.ds(base_col, wide)]
            out[slot, part] = pulled(block, rest_row, rest_col).astype(jnp.bfloat16)
        return carry

    lax.fori_loop(0, out.shape[0], slot_step, 0)


def levels_kernel(intensity, measured, zeros, held, sem):
    copy = pltpu.make_async_copy(intensity, held, sem)
    copy.start()
    zeros[...] = jnp.zeros_like(zeros)
    copy.wait()
    for slot in range(measured.shape[0]):
        measured[slot] = jnp.sqrt(held[0, 0, slot].astype(jnp.float32))


def windows_of(row, me, corners, tile, sides, ends, slot_count, size):
    half = sides[0].shape[-1]
    extent = (2, tile.shape[1] + 2 * half + SUBLANES, tile.shape[2] + 2 * half + LANES)
    return call(
        window_kernel,
        [((slot_count, 2, size, size), jnp.bfloat16)],
        (row, SMEM),
        (me, SMEM),
        (corners, SMEM),
        tile,
        *sides,
        *ends,
        scratch=[pltpu.VMEM(extent, jnp.float32)],
    )[0]


def dft_kernel(goes_to, comes_from, steps, counts, me, *refs):
    blocks = refs[: len(steps)]
    windows, measured, forward, inverse = refs[len(steps) : len(steps) + 4]
    outs = refs[len(steps) + 4 : 2 * len(steps) + 4]
    placed, probes, terms = refs[2 * len(steps) + 4 :]
    size = windows.shape[-1]
    rows = blocks[0].shape[2]
    starts = [pl.multiple_of(comes_from(me[0], step) * rows, rows) for step in steps]
    targets = [pl.multiple_of(goes_to(me[0], step) * rows, rows) for step in steps]

    def dot(left, right):
        return jnp.dot(left, right, preferred_element_type=jnp.float32)

    for block, start in zip(blocks, starts):
        probes[:, :, pl.ds(start, rows)] = block[...]
    slots = range(windows.shape[0])

    def held(ref, slot):
        return ref[slot, 0].astype(jnp.float32), ref[slot, 1].astype(jnp.float32)

    def stacked(re, im):
        return jnp.concatenate([re.astype(jnp.bfloat16), im.astype(jnp.bfloat16)], axis=0)

    def beside(products):
        columns = [products[:, slot * size : (slot + 1) * size] for slot in slots]
        turned = [jnp.concatenate([c[:size], c[size:]], axis=1) for c in columns]
        return jnp.concatenate(turned, axis=0)

    def parts(products, slot):
        block = products[slot * size : (slot + 1) * size]
        return block[:, :size], block[:, size:]

    leaving = []
    for slot in slots:
        probe_re, probe_im = held(probes, slot)
        window_re, window_im = held(windows, slot)
        leaving.append(
            stacked(
                probe_re * window_re - probe_im * window_im,
                probe_re * window_im + probe_im * window_re,
            )
        )
    half = dot(forward[...], jnp.concatenate(leaving, axis=1)).astype(jnp.bfloat16)
    far = dot(beside(half), inverse[...])
    changes = []
    for slot in slots:
        far_re, far_im = parts(far, slot)
        power = jnp.maximum(far_re * far_re + far_im * far_im, FLOOR * FLOOR)
        live = jnp.where(slot < counts[0, 0], 1.0, 0.0).astype(jnp.float32)
        factor = (measured[slot] * lax.rsqrt(power) - 1.0) * live
        changes.append(stacked(far_re * factor, far_im * factor))
    back = dot(inverse[...], jnp.concatenate(changes, axis=1)).astype(jnp.bfloat16)
    update = dot(beside(back), forward[...])
    for slot in slots:
        update_re, update_im = parts(update, slot)
        probe_re, probe_im = held(probes, slot)
        window_re, window_im = held(windows, slot)
        terms[slot, 0] = (window_re * update_re + window_im * update_im).astype(jnp.bfloat16)
        terms[slot, 1] = (window_re * update_im - window_im * update_re).astype(jnp.bfloat16)
        placed[slot, 0] = probe_re * update_re + probe_im * update_im
        placed[slot, 1] = probe_re * update_im - probe_im * update_re
    for out, start in zip(outs, targets):
        out[...] = terms[:, :, pl.ds(start, rows)]


def place_kernel(half, row, corners, pieces, zeros, first, accum, second):
    size = pieces.shape[-1]
    rows = accum.shape[1] - SUBLANES - 2 * half
    width = first.shape[2]
    for slot in range(pieces.shape[0]):
        base_row, rest_row, base_col, rest_col = corner_of(
            corners, slot, half, rows + 2 * half - size
        )
        for part in range(2):
            block = pushed(pieces[slot, part], rest_row, rest_col)
            where = (part, pl.ds(base_row, size + SUBLANES), pl.ds(base_col, size + LANES))
            accum[where] += block
    top = accum[:, :half, :width].astype(jnp.bfloat16)
    bottom = accum[:, half + rows : 2 * half + rows, :width].astype(jnp.bfloat16)
    first[...], second[...] = by_side(row[0], top, bottom)


def rows_kernel(row, me, accum, even, odd, first, center, second, total):
    half = even.shape[1]
    rows, cols = center.shape[1:]
    got_top, got_bottom = from_sides(row[0], even[...], odd[...])
    total[...] = accum[:, half : half + rows, : cols + 2 * half]
    total[:, :half] += got_top.astype(jnp.float32)
    total[:, rows - half :] += got_bottom.astype(jnp.float32)
    center[...] = total[:, :, half : half + cols]
    left = total[:, :, :half].astype(jnp.bfloat16)
    right = total[:, :, half + cols :].astype(jnp.bfloat16)
    first[...], second[...] = by_side(me[0], left, right)


def cols_kernel(me, center, even, odd, out):
    half = even.shape[2]
    cols = out.shape[2]
    got_left, got_right = from_sides(me[0], even[...], odd[...])
    out[...] = center[...]
    out[:, :, :half] += got_left.astype(jnp.float32)
    out[:, :, cols - half :] += got_right.astype(jnp.float32)


def sums_kernel(held_in, places, goals, row, *refs):
    count = len(places)
    received = refs[held_in : held_in + count]
    added = refs[held_in + count : held_in + count + sum(goal[2] for goal in goals)]
    outs = refs[held_in + count + len(added) : -3]
    terms, held, sem = refs[-3:]
    copies = fetch(refs[:held_in], places, held, sem)
    num_modes = outs[0].shape[-4]
    slot_count = received[0].shape[0]
    slots = slot_count
    first = min(goal[1] for goal in goals)
    for at in range(count):
        terms[at, first:] = received[at][first:].astype(jnp.float32)
    for copy in copies:
        copy.wait()

    def mode_step(k, carry):
        rest = list(added)
        for (step, first, adds), out in zip(goals, outs):
            region = (row[0] + step).astype(jnp.float32)
            addend = rest.pop(0) if adds else None
            scales = [
                jnp.where(held[at, slots, slot] == region, held[at, slot, k], 0.0)
                for at in range(count)
                for slot in range(first, slot_count)
            ]
            for part in range(2):
                pieces = [
                    terms[at, slot, part] for at in range(count) for slot in range(first, slot_count)
                ]
                total = scales[0] * pieces[0]
                for scale, piece in zip(scales[1:], pieces[1:]):
                    total += scale * piece
                if adds:
                    total += addend[k, part].astype(jnp.float32)
                out[k, part] = total.astype(out.dtype)
        return carry

    lax.fori_loop(0, num_modes, mode_step, 0)


def sums(row, goals, weights, places, received, added, num_modes, dtypes):
    shape = (num_modes,) + received[0].shape[1:]
    return call(
        functools.partial(sums_kernel, len(weights), places, goals),
        [(shape, dtype) for dtype in dtypes],
        (row, SMEM),
        *weights,
        *received,
        *added,
        scratch=[pltpu.VMEM((len(received),) + received[0].shape, jnp.float32)]
        + held_weights(len(places), weights[0]),
    )


def gradients(object_field, modes, coeffs, offsets, region, counts, intensity):
    size = modes.shape[-1]
    half = size // 2
    num_modes = modes.shape[1]
    slot_count = coeffs.shape[2]
    rows, cols = object_field.shape[1:]
    block = (slot_count,) + modes.shape[2:]
    row = lax.axis_index("row").reshape(1)
    me = lax.axis_index("col").reshape(1)
    steps, goes_to, comes_from = partners("col")
    every = [0] + steps
    count = lax.axis_size("col")
    middle_step = count // 2
    near = list(range(1, middle_step))
    crossing = [step for step in steps if step >= middle_step]

    def move(value, step):
        return lax.ppermute(value, "col", [(i, goes_to(i, step)) for i in range(count)])

    side = (2, rows, half)
    (payload,) = call(
        payload_kernel,
        [((slot_count + 1, LANES), jnp.float32)],
        (coeffs, HBM),
        (region, HBM),
        scratch=[pltpu.VMEM(x.shape, x.dtype) for x in (coeffs, region)]
        + [pltpu.SemaphoreType.DMA((2,))],
    )
    low, *edges = call(
        edges_kernel,
        [(object_field.shape, jnp.bfloat16)] + [(side, jnp.bfloat16)] * 2,
        (me, SMEM),
        (object_field, HBM),
        scratch=[pltpu.VMEM(object_field.shape, object_field.dtype), pltpu.SemaphoreType.DMA],
    )
    paired = count > 1 and count & (count - 1) == 0
    if paired:
        across = move(payload, middle_step)
        blocks_shape = (2,) + payload.shape
        (pair,) = call(pair_kernel, [(blocks_shape, jnp.float32)], payload, across)
        weights = [pair] + [move(pair, step) for step in near]

        def made_at(step):
            return step % middle_step, step // middle_step

        came_at = made_at
    else:
        weights = [payload[None]]
        weights += [move(payload[None], step) for step in range(1, count)]

        def made_at(step):
            return -step % count, 0

        def came_at(step):
            return step, 0

    follower = shift(modes, "row", -1)

    sides = swap(edges, "col")
    wide = (2, half, cols + 2 * half)
    ends = call(widen_kernel, [(wide, jnp.bfloat16)] * 2, (row, SMEM), (me, SMEM), low, *sides)
    ends = swap(ends, "row")

    blocks = {}
    turns = slab_order(count, paired)
    made = slabs(row, weights, [made_at(step) for step in turns], modes, follower)
    for step, slab in zip(turns, made):
        blocks[step] = move(slab, step) if step else slab

    corners = pltpu.with_memory_space_constraint(offsets[0, 0].T, pltpu.HBM)
    extent = (2, rows + 2 * half + SUBLANES, cols + 2 * half + LANES)
    measured, zeros = call(
        levels_kernel,
        [((slot_count, size, size), jnp.float32), (extent, jnp.float32)],
        (intensity, HBM),
        scratch=[pltpu.VMEM(intensity.shape, intensity.dtype), pltpu.SemaphoreType.DMA],
    )
    windows = windows_of(row, me, corners, low, sides, ends, slot_count, size)
    whole = (slot_count, 2, size, size)
    *terms, placed = call(
        functools.partial(dft_kernel, goes_to, comes_from, every),
        [(block, jnp.bfloat16)] * count + [(whole, jnp.float32)],
        (counts, SMEM),
        (me, SMEM),
        *[blocks[step] for step in every],
        windows,
        measured,
        *dft_tables(size),
        scratch=[pltpu.VMEM(whole, jnp.bfloat16)] * 2,
        limit=32,
    )
    terms = dict(zip(every, terms))
    received = {step: move(terms[step], step) if step else terms[step] for step in every}

    even, accum, odd = call(
        functools.partial(place_kernel, half),
        [(wide, jnp.bfloat16), (extent, jnp.float32), (wide, jnp.bfloat16)],
        (row, SMEM),
        (corners, SMEM),
        placed,
        zeros,
        aliases={3: 1},
    )
    over_ends = swap([even, odd], "row")
    even, center, odd = call(
        rows_kernel,
        [(side, jnp.bfloat16), ((2, rows, cols), jnp.float32), (side, jnp.bfloat16)],
        (row, SMEM),
        (me, SMEM),
        accum,
        *over_ends,
        scratch=[pltpu.VMEM((2, rows, cols + 2 * half), jnp.float32)],
    )
    over_sides = swap([even, odd], "col")
    (object_grad,) = call(
        cols_kernel, [(object_field.shape, jnp.float32)], (me, SMEM), center, *over_sides
    )

    def add_up(group, goals, added, dtypes):
        return sums(
            row,
            goals,
            weights,
            [came_at(step) for step in group],
            [received[step] for step in group],
            added,
            num_modes,
            dtypes,
        )

    (following,) = add_up([0] + near, ((1, 1, False),), [], [jnp.float32])
    if len(crossing) > 1:
        (following,) = add_up(crossing[:-1], ((1, 1, True),), [following], [jnp.float32])
    (following,) = add_up(crossing[-1:], ((1, 1, True),), [following], [jnp.bfloat16])
    passed = shift(following, "row", 1)
    (own,) = add_up(every, ((0, 0, False),), [], [jnp.float32])
    mode_grad = (own + passed.astype(jnp.float32))[None]
    return (object_grad, mode_grad)


def solution(mesh):
    in_specs = (
        P(None, "row", "col"),
        P("row", None, None, "col", None),
        P("row", "col", None, None),
        P("row", "col", None, None),
        P("row", "col", None),
        P("row", "col"),
        P("row", "col", None, None, None),
    )
    out_specs = (P(None, "row", "col"), P("row", None, None, "col", None))
    return jax.shard_map(gradients, mesh=mesh, in_specs=in_specs, out_specs=out_specs, check_vma=False)
```

```python
import functools
import math

import jax
import jax.numpy as jnp
import numpy as np
from jax import lax
from jax.experimental import pallas as pl
from jax.experimental.pallas import tpu as pltpu
from jax.sharding import PartitionSpec as P


FLOOR = 0.25
LANES = 128
SUBLANES = 8

VMEM = pl.BlockSpec(memory_space=pltpu.VMEM)
SMEM = pl.BlockSpec(memory_space=pltpu.SMEM)
HBM = pl.BlockSpec(memory_space=pltpu.HBM)


def shift(value, axis, steps):
    count = lax.axis_size(axis)
    leading, last = (max(0, -steps), min(count, count - steps))
    pairs = [(source, source + steps) for source in range(leading, last)]
    return lax.ppermute(value, axis, pairs)


def swap(values, axis):
    count = lax.axis_size(axis)
    got = []
    for odd, value in enumerate(values):
        pairs = []
        for i in range(odd, count - 1, 2):
            pairs += [(i, i + 1), (i + 1, i)]
        got.append(lax.ppermute(value, axis, pairs) if pairs else jnp.zeros_like(value))
    return got


def by_side(index, low, high):
    even = index % 2 == 0
    return jnp.where(even, high, low), jnp.where(even, low, high)


def from_sides(index, first, second):
    high, low = by_side(index, second, first)
    return low, high


def dft_tables(length):
    indices = np.arange(length)
    phases = indices[:, None] * indices[None, :] % length
    angles = phases * (2.0 * math.pi / length)
    scaling = 1.0 / math.sqrt(length)
    re = (np.cos(angles) * scaling).astype(np.float32)
    im = (-np.sin(angles) * scaling).astype(np.float32)
    forward = np.block([[re, -im], [im, re]])
    inverse = np.block([[re, im], [-im, re]])
    return jnp.asarray(forward, jnp.bfloat16), jnp.asarray(inverse, jnp.bfloat16)


def transfer_order(count):
    half = count // 2
    return [half] * (half > 0) + list(range(1, half)) + list(range(half + 1, count))


def slab_order(count, paired):
    steps = transfer_order(count)
    return steps[:1] + [0] + steps[1:] if paired else [0] + steps


def partners(axis):
    count = lax.axis_size(axis)
    steps = transfer_order(count)
    paired = count & (count - 1) == 0

    def goes_to(index, step):
        return index ^ step if paired else (index + step) % count

    def comes_from(index, step):
        return index ^ step if paired else (index - step + count) % count

    return steps, goes_to, comes_from


def call(body, outs, *operands, scratch=(), limit=20, aliases={}):
    arrays = [o[0] if isinstance(o, tuple) else o for o in operands]
    arrays = [
        pltpu.with_memory_space_constraint(a, pltpu.HBM)
        if isinstance(o, tuple) and o[1] is HBM
        else a
        for a, o in zip(arrays, operands)
    ]
    specs = [o[1] if isinstance(o, tuple) else VMEM for o in operands]
    outs = [jax.ShapeDtypeStruct(shape, dtype) for shape, dtype in outs]
    return pl.pallas_call(
        body,
        out_shape=tuple(outs),
        in_specs=specs,
        out_specs=tuple(VMEM for _ in outs),
        scratch_shapes=list(scratch),
        input_output_aliases=aliases,
        compiler_params=pltpu.CompilerParams(vmem_limit_bytes=limit * 1024 * 1024),
    )(*arrays)


def fetch(arrays, places, held, sem):
    copies = [
        pltpu.make_async_copy(arrays[i].at[block], held.at[at], sem.at[at])
        for at, (i, block) in enumerate(places)
    ]
    for copy in copies:
        copy.start()
    return copies


def held_weights(count, weights):
    shape = (count,) + weights.shape[1:]
    return [pltpu.SMEM(shape, jnp.float32), pltpu.SemaphoreType.DMA((count,))]


def make_slabs(region_of, weight_of, num_modes, row, table, outs):
    next_row = (row[0] + 1).astype(jnp.float32)
    for at, out in enumerate(outs):

        def slot_step(slot, carry, at=at, out=out):
            region = region_of(at, slot)
            which = jnp.where(region == next_row, 1, 0)
            known = jnp.where(jnp.abs(region - next_row + 0.5) < 1.0, 1.0, 0.0)
            scales = [weight_of(at, slot, k) * known for k in range(num_modes)]
            for part in range(2):
                total = scales[0] * table[which, 0, part]
                for k in range(1, num_modes):
                    total += scales[k] * table[which, k, part]
                out[slot, part] = total.astype(jnp.bfloat16)
            return carry

        lax.fori_loop(0, out.shape[0], slot_step, 0)


def first_kernel(places, row, weights, own, follower, out, table, near, held, sem, near_sem):
    copy_own = pltpu.make_async_copy(own, near, near_sem)
    copy_own.start()
    copies = fetch([weights], places, held, sem)
    num_modes, slots = (own.shape[1], out.shape[0])
    table[1] = follower[0].astype(jnp.float32)
    copy_own.wait()
    table[0] = near[0].astype(jnp.float32)
    for copy in copies:
        copy.wait()
    make_slabs(
        lambda at, slot: held[at, slots, slot],
        lambda at, slot, k: held[at, slot, k],
        num_modes,
        row,
        table,
        [out],
    )


def slab_kernel(count, places, row, *refs):
    table = refs[count]
    outs = refs[count + 1 : -2]
    held, sem = refs[-2:]
    slots = outs[0].shape[0]
    for copy in fetch(refs[:count], places, held, sem):
        copy.wait()
    make_slabs(
        lambda at, slot: held[at, slots, slot],
        lambda at, slot, k: held[at, slot, k],
        table.shape[1],
        row,
        table,
        outs,
    )


def slabs(row, weights, places, own, follower):
    shape = (weights[0].shape[1] - 1,) + own.shape[2:]
    first, table = call(
        functools.partial(first_kernel, places[:1]),
        [(shape, jnp.bfloat16), ((2,) + own.shape[1:], jnp.float32)],
        (row, SMEM),
        weights[0],
        (own, HBM),
        follower,
        scratch=[pltpu.VMEM(own.shape, own.dtype)]
        + held_weights(1, weights[0])
        + [pltpu.SemaphoreType.DMA],
    )
    rest = call(
        functools.partial(slab_kernel, len(weights), places[1:]),
        [(shape, jnp.bfloat16)] * (len(places) - 1),
        (row, SMEM),
        *weights,
        table,
        scratch=held_weights(len(places) - 1, weights[0]),
    )
    return [first, *rest]


def payload_kernel(coeffs, region, payload, coeffs_held, region_held, sem):
    slots, num_modes = coeffs.shape[2:]
    copies = [
        pltpu.make_async_copy(coeffs, coeffs_held, sem.at[0]),
        pltpu.make_async_copy(region, region_held, sem.at[1]),
    ]
    for copy in copies:
        copy.start()
    payload[...] = jnp.zeros_like(payload)
    for copy in copies:
        copy.wait()
    payload[:slots, :num_modes] = coeffs_held[0, 0]
    payload[slots:, :slots] = region_held[0].astype(jnp.float32)


def edges_kernel(me, tile, low, even, odd, held, sem):
    half = even.shape[2]
    copy = pltpu.make_async_copy(tile, held, sem)
    copy.start()
    copy.wait()
    low[...] = held[...].astype(jnp.bfloat16)
    first, second = by_side(me[0], low[:, :, :half], low[:, :, low.shape[2] - half :])
    even[...] = first
    odd[...] = second


def pair_kernel(mine, across, out):
    out[0] = mine[...]
    out[1] = across[...]


def widen_kernel(row, me, tile, even, odd, first, second):
    half = even.shape[2]
    rows, _ = tile.shape[1:]

    def extended(start):
        left, right = from_sides(
            me[0], even[:, start : start + half], odd[:, start : start + half]
        )
        return jnp.concatenate([left, tile[:, start : start + half], right], axis=2)

    first[...], second[...] = by_side(row[0], extended(0), extended(rows - half))


def corner_of(corners, slot, half, limit):
    row = jnp.clip(corners[0, slot] + half, 0, limit)
    col = jnp.clip(corners[1, slot] + half, 0, limit)
    rest_row, rest_col = (row & (SUBLANES - 1), col & (LANES - 1))
    base_row = pl.multiple_of(row - rest_row, SUBLANES)
    base_col = pl.multiple_of(col - rest_col, LANES)
    return base_row, rest_row, base_col, rest_col


def beyond(shape, dim, bound):
    return lax.broadcasted_iota(jnp.int32, shape, dim) >= bound


def pushed(block, down, across):
    rows, cols = block.shape
    edge = jnp.zeros((rows, LANES), block.dtype)
    tiles = [block[:, start : start + LANES] for start in range(0, cols, LANES)]
    tiles = [pltpu.roll(tile, across, 1) for tile in tiles]
    kept = beyond((rows, LANES), 1, across)
    pairs = zip(tiles + [edge], [edge] + tiles)
    block = jnp.concatenate([jnp.where(kept, tile, before) for tile, before in pairs], axis=1)
    cols += LANES
    tall = block.reshape(rows // SUBLANES, SUBLANES, cols)
    tall = pltpu.roll(tall, down, 1)
    edge = jnp.zeros((1, SUBLANES, cols), block.dtype)
    below = jnp.concatenate([tall, edge], axis=0)
    above = jnp.concatenate([edge, tall], axis=0)
    tall = jnp.where(beyond(below.shape, 1, down), below, above)
    return tall.reshape(rows + SUBLANES, cols)


def pulled(block, up, back):
    rows, cols = block.shape
    tall = block.reshape(rows // SUBLANES, SUBLANES, cols)
    tall = pltpu.roll(tall, (SUBLANES - up) & (SUBLANES - 1), 1)
    kept = beyond(tall[1:].shape, 1, SUBLANES - up)
    block = jnp.where(kept, tall[1:], tall[:-1]).reshape(rows - SUBLANES, cols)
    tiles = [block[:, start : start + LANES] for start in range(0, cols, LANES)]
    tiles = [pltpu.roll(tile, (LANES - back) & (LANES - 1), 1) for tile in tiles]
    kept = beyond((rows - SUBLANES, LANES), 1, LANES - back)
    pairs = zip(tiles[1:], tiles[:-1])
    return jnp.concatenate([jnp.where(kept, after, tile) for after, tile in pairs], axis=1)


def window_kernel(
    row, me, corners, tile, side_even, side_odd, end_even, end_odd, out, ext
):
    size = out.shape[-1]
    half = side_even.shape[-1]
    rows, cols = tile.shape[1:]
    left, right = from_sides(me[0], side_even[...], side_odd[...])
    top, bottom = from_sides(row[0], end_even[...], end_odd[...])
    for part in range(2):
        ext[part, :half, : cols + 2 * half] = top[part].astype(jnp.float32)
        ext[part, half : half + rows, :half] = left[part].astype(jnp.float32)
        ext[part, half : half + rows, half : half + cols] = tile[part].astype(jnp.float32)
        ext[part, half : half + rows, half + cols : cols + 2 * half] = right[part].astype(jnp.float32)
        ext[part, half + rows : 2 * half + rows, : cols + 2 * half] = bottom[part].astype(jnp.float32)
    tall = size + SUBLANES
    wide = size + LANES

    def slot_step(slot, carry):
        base_row, rest_row, base_col, rest_col = corner_of(
            corners, slot, half, rows + 2 * half - size
        )
        for part in range(2):
            block = ext[part, pl.ds(base_row, tall), pl.ds(base_col, wide)]
            out[slot, part] = pulled(block, rest_row, rest_col).astype(jnp.bfloat16)
        return carry

    lax.fori_loop(0, out.shape[0], slot_step, 0)


def levels_kernel(intensity, measured, zeros, held, sem):
    copy = pltpu.make_async_copy(intensity, held, sem)
    copy.start()
    zeros[...] = jnp.zeros_like(zeros)
    copy.wait()
    for slot in range(measured.shape[0]):
        measured[slot] = jnp.sqrt(held[0, 0, slot].astype(jnp.float32))


def windows_of(row, me, corners, tile, sides, ends, slot_count, size):
    half = sides[0].shape[-1]
    extent = (2, tile.shape[1] + 2 * half + SUBLANES, tile.shape[2] + 2 * half + LANES)
    return call(
        window_kernel,
        [((slot_count, 2, size, size), jnp.bfloat16)],
        (row, SMEM),
        (me, SMEM),
        (corners, SMEM),
        tile,
        *sides,
        *ends,
        scratch=[pltpu.VMEM(extent, jnp.float32)],
    )[0]


def dft_kernel(goes_to, comes_from, steps, counts, me, *refs):
    blocks = refs[: len(steps)]
    windows, measured, forward, inverse = refs[len(steps) : len(steps) + 4]
    outs = refs[len(steps) + 4 : 2 * len(steps) + 4]
    placed, probes, terms = refs[2 * len(steps) + 4 :]
    size = windows.shape[-1]
    rows = blocks[0].shape[2]
    starts = [pl.multiple_of(comes_from(me[0], step) * rows, rows) for step in steps]
    targets = [pl.multiple_of(goes_to(me[0], step) * rows, rows) for step in steps]

    def dot(left, right):
        return jnp.dot(left, right, preferred_element_type=jnp.float32)

    for block, start in zip(blocks, starts):
        probes[:, :, pl.ds(start, rows)] = block[...]
    slots = range(windows.shape[0])

    def held(ref, slot):
        return ref[slot, 0].astype(jnp.float32), ref[slot, 1].astype(jnp.float32)

    def stacked(re, im):
        return jnp.concatenate([re.astype(jnp.bfloat16), im.astype(jnp.bfloat16)], axis=0)

    def beside(products):
        columns = [products[:, slot * size : (slot + 1) * size] for slot in slots]
        turned = [jnp.concatenate([c[:size], c[size:]], axis=1) for c in columns]
        return jnp.concatenate(turned, axis=0)

    def parts(products, slot):
        block = products[slot * size : (slot + 1) * size]
        return block[:, :size], block[:, size:]

    leaving = []
    for slot in slots:
        probe_re, probe_im = held(probes, slot)
        window_re, window_im = held(windows, slot)
        leaving.append(
            stacked(
                probe_re * window_re - probe_im * window_im,
                probe_re * window_im + probe_im * window_re,
            )
        )
    half = dot(forward[...], jnp.concatenate(leaving, axis=1)).astype(jnp.bfloat16)
    far = dot(beside(half), inverse[...])
    changes = []
    for slot in slots:
        far_re, far_im = parts(far, slot)
        power = jnp.maximum(far_re * far_re + far_im * far_im, FLOOR * FLOOR)
        live = jnp.where(slot < counts[0, 0], 1.0, 0.0).astype(jnp.float32)
        factor = (measured[slot] * lax.rsqrt(power) - 1.0) * live
        changes.append(stacked(far_re * factor, far_im * factor))
    back = dot(inverse[...], jnp.concatenate(changes, axis=1)).astype(jnp.bfloat16)
    update = dot(beside(back), forward[...])
    for slot in slots:
        update_re, update_im = parts(update, slot)
        probe_re, probe_im = held(probes, slot)
        window_re, window_im = held(windows, slot)
        terms[slot, 0] = (window_re * update_re + window_im * update_im).astype(jnp.bfloat16)
        terms[slot, 1] = (window_re * update_im - window_im * update_re).astype(jnp.bfloat16)
        placed[slot, 0] = probe_re * update_re + probe_im * update_im
        placed[slot, 1] = probe_re * update_im - probe_im * update_re
    for out, start in zip(outs, targets):
        out[...] = terms[:, :, pl.ds(start, rows)]


def place_kernel(half, row, corners, pieces, zeros, first, accum, second):
    size = pieces.shape[-1]
    rows = accum.shape[1] - SUBLANES - 2 * half
    width = first.shape[2]
    for slot in range(pieces.shape[0]):
        base_row, rest_row, base_col, rest_col = corner_of(
            corners, slot, half, rows + 2 * half - size
        )
        for part in range(2):
            block = pushed(pieces[slot, part], rest_row, rest_col)
            where = (part, pl.ds(base_row, size + SUBLANES), pl.ds(base_col, size + LANES))
            accum[where] += block
    top = accum[:, :half, :width].astype(jnp.bfloat16)
    bottom = accum[:, half + rows : 2 * half + rows, :width].astype(jnp.bfloat16)
    first[...], second[...] = by_side(row[0], top, bottom)


def rows_kernel(row, me, accum, even, odd, first, center, second, total):
    half = even.shape[1]
    rows, cols = center.shape[1:]
    got_top, got_bottom = from_sides(row[0], even[...], odd[...])
    total[...] = accum[:, half : half + rows, : cols + 2 * half]
    total[:, :half] += got_top.astype(jnp.float32)
    total[:, rows - half :] += got_bottom.astype(jnp.float32)
    center[...] = total[:, :, half : half + cols]
    left = total[:, :, :half].astype(jnp.bfloat16)
    right = total[:, :, half + cols :].astype(jnp.bfloat16)
    first[...], second[...] = by_side(me[0], left, right)


def cols_kernel(me, center, even, odd, out):
    half = even.shape[2]
    cols = out.shape[2]
    got_left, got_right = from_sides(me[0], even[...], odd[...])
    out[...] = center[...]
    out[:, :, :half] += got_left.astype(jnp.float32)
    out[:, :, cols - half :] += got_right.astype(jnp.float32)


def sums_kernel(held_in, places, goals, row, *refs):
    count = len(places)
    received = refs[held_in : held_in + count]
    added = refs[held_in + count : held_in + count + sum(goal[2] for goal in goals)]
    outs = refs[held_in + count + len(added) : -3]
    terms, held, sem = refs[-3:]
    copies = fetch(refs[:held_in], places, held, sem)
    num_modes = outs[0].shape[-4]
    slot_count = received[0].shape[0]
    slots = slot_count
    first = min(goal[1] for goal in goals)
    for at in range(count):
        terms[at, first:] = received[at][first:].astype(jnp.float32)
    for copy in copies:
        copy.wait()

    def mode_step(k, carry):
        rest = list(added)
        for (step, first, adds), out in zip(goals, outs):
            region = (row[0] + step).astype(jnp.float32)
            addend = rest.pop(0) if adds else None
            scales = [
                jnp.where(held[at, slots, slot] == region, held[at, slot, k], 0.0)
                for at in range(count)
                for slot in range(first, slot_count)
            ]
            for part in range(2):
                pieces = [
                    terms[at, slot, part] for at in range(count) for slot in range(first, slot_count)
                ]
                total = scales[0] * pieces[0]
                for scale, piece in zip(scales[1:], pieces[1:]):
                    total += scale * piece
                if adds:
                    total += addend[k, part].astype(jnp.float32)
                out[k, part] = total.astype(out.dtype)
        return carry

    lax.fori_loop(0, num_modes, mode_step, 0)


def sums(row, goals, weights, places, received, added, num_modes, dtypes):
    shape = (num_modes,) + received[0].shape[1:]
    return call(
        functools.partial(sums_kernel, len(weights), places, goals),
        [(shape, dtype) for dtype in dtypes],
        (row, SMEM),
        *weights,
        *received,
        *added,
        scratch=[pltpu.VMEM((len(received),) + received[0].shape, jnp.float32)]
        + held_weights(len(places), weights[0]),
    )


def gradients(object_field, modes, coeffs, offsets, region, counts, intensity):
    size = modes.shape[-1]
    half = size // 2
    num_modes = modes.shape[1]
    slot_count = coeffs.shape[2]
    rows, cols = object_field.shape[1:]
    block = (slot_count,) + modes.shape[2:]
    row = lax.axis_index("row").reshape(1)
    me = lax.axis_index("col").reshape(1)
    steps, goes_to, comes_from = partners("col")
    every = [0] + steps
    count = lax.axis_size("col")
    middle_step = count // 2
    near = list(range(1, middle_step))
    crossing = list(range(max(middle_step, 1), count))

    def move(value, step):
        return lax.ppermute(value, "col", [(i, goes_to(i, step)) for i in range(count)])

    side = (2, rows, half)
    (payload,) = call(
        payload_kernel,
        [((slot_count + 1, LANES), jnp.float32)],
        (coeffs, HBM),
        (region, HBM),
        scratch=[pltpu.VMEM(x.shape, x.dtype) for x in (coeffs, region)]
        + [pltpu.SemaphoreType.DMA((2,))],
    )
    low, *edges = call(
        edges_kernel,
        [(object_field.shape, jnp.bfloat16)] + [(side, jnp.bfloat16)] * 2,
        (me, SMEM),
        (object_field, HBM),
        scratch=[pltpu.VMEM(object_field.shape, object_field.dtype), pltpu.SemaphoreType.DMA],
    )
    paired = count > 1 and count & (count - 1) == 0
    if paired:
        across = move(payload, middle_step)
        blocks_shape = (2,) + payload.shape
        (pair,) = call(pair_kernel, [(blocks_shape, jnp.float32)], payload, across)
        weights = [pair] + [move(pair, step) for step in near]

        def made_at(step):
            return step % middle_step, step // middle_step

        came_at = made_at
    else:
        weights = [payload[None]]
        weights += [move(payload[None], step) for step in range(1, count)]

        def made_at(step):
            return -step % count, 0

        def came_at(step):
            return step, 0

    follower = shift(modes, "row", -1)

    sides = swap(edges, "col")
    wide = (2, half, cols + 2 * half)
    ends = call(widen_kernel, [(wide, jnp.bfloat16)] * 2, (row, SMEM), (me, SMEM), low, *sides)
    ends = swap(ends, "row")

    blocks = {}
    turns = slab_order(count, paired)
    made = slabs(row, weights, [made_at(step) for step in turns], modes, follower)
    for step, slab in zip(turns, made):
        blocks[step] = move(slab, step) if step else slab

    corners = pltpu.with_memory_space_constraint(offsets[0, 0].T, pltpu.HBM)
    extent = (2, rows + 2 * half + SUBLANES, cols + 2 * half + LANES)
    measured, zeros = call(
        levels_kernel,
        [((slot_count, size, size), jnp.float32), (extent, jnp.float32)],
        (intensity, HBM),
        scratch=[pltpu.VMEM(intensity.shape, intensity.dtype), pltpu.SemaphoreType.DMA],
    )
    windows = windows_of(row, me, corners, low, sides, ends, slot_count, size)
    whole = (slot_count, 2, size, size)
    *terms, placed = call(
        functools.partial(dft_kernel, goes_to, comes_from, every),
        [(block, jnp.bfloat16)] * count + [(whole, jnp.float32)],
        (counts, SMEM),
        (me, SMEM),
        *[blocks[step] for step in every],
        windows,
        measured,
        *dft_tables(size),
        scratch=[pltpu.VMEM(whole, jnp.bfloat16)] * 2,
        limit=32,
    )
    terms = dict(zip(every, terms))
    received = {step: move(terms[step], step) if step else terms[step] for step in every}

    even, accum, odd = call(
        functools.partial(place_kernel, half),
        [(wide, jnp.bfloat16), (extent, jnp.float32), (wide, jnp.bfloat16)],
        (row, SMEM),
        (corners, SMEM),
        placed,
        zeros,
        aliases={3: 1},
    )
    over_ends = swap([even, odd], "row")
    even, center, odd = call(
        rows_kernel,
        [(side, jnp.bfloat16), ((2, rows, cols), jnp.float32), (side, jnp.bfloat16)],
        (row, SMEM),
        (me, SMEM),
        accum,
        *over_ends,
        scratch=[pltpu.VMEM((2, rows, cols + 2 * half), jnp.float32)],
    )
    over_sides = swap([even, odd], "col")
    (object_grad,) = call(
        cols_kernel, [(object_field.shape, jnp.float32)], (me, SMEM), center, *over_sides
    )

    def add_up(group, goals, added, dtypes):
        return sums(
            row,
            goals,
            weights,
            [came_at(step) for step in group],
            [received[step] for step in group],
            added,
            num_modes,
            dtypes,
        )

    (following,) = add_up([0] + near, ((1, 1, False),), [], [jnp.float32])
    if len(crossing) > 1:
        (following,) = add_up(crossing[:-1], ((1, 1, True),), [following], [jnp.float32])
    (following,) = add_up(crossing[-1:], ((1, 1, True),), [following], [jnp.bfloat16])
    passed = shift(following, "row", 1)
    (own,) = add_up(every, ((0, 0, False),), [], [jnp.float32])
    mode_grad = (own + passed.astype(jnp.float32))[None]
    return (object_grad, mode_grad)


def solution(mesh):
    in_specs = (
        P(None, "row", "col"),
        P("row", None, None, "col", None),
        P("row", "col", None, None),
        P("row", "col", None, None),
        P("row", "col", None),
        P("row", "col"),
        P("row", "col", None, None, None),
    )
    out_specs = (P(None, "row", "col"), P("row", None, None, "col", None))
    return jax.shard_map(gradients, mesh=mesh, in_specs=in_specs, out_specs=out_specs, check_vma=False)
```
